32 devices in a mesh: leaf: 2 (over y), seq: 4 (over x, core), tensor: 4 (over z).
Axes of the slice: x: 2, y: 2, z: 4, core: 2. Of those that a mesh axis runs over, the one named last changes fastest.
Arguments:
- hidden_in: bfloat16 [4, 1024, 1536], P('leaf', 'seq'), may hold values from -6 to 6
- parents: int32 [4, 8], P('leaf'), may hold values from -1 to 6, as said below
- cotangent: bfloat16 [4, 1024, 1536], P('leaf', 'seq'), may hold values from -6 to 6
- attn_gain: bfloat16 [2, 1536], P(None, ('leaf', 'seq')), may hold values from 0.5 to 1.5
- w_query: bfloat16 [2, 1536, 1536], P(None, ('leaf', 'seq'), 'tensor'), may hold values from -0.15625 to 0.15625
- b_query: bfloat16 [2, 12, 128], P(None, 'tensor', ('leaf', 'seq')), may hold values from -3 to 3
- w_key: bfloat16 [2, 1536, 256], P(None, ('leaf', 'seq')), may hold values from -0.15625 to 0.15625
- b_key: bfloat16 [2, 2, 128], P(None, None, ('leaf', 'seq')), may hold values from -3 to 3
- w_value: bfloat16 [2, 1536, 256], P(None, ('leaf', 'seq')), may hold values from -0.15625 to 0.15625
- b_value: bfloat16 [2, 2, 128], P(None, None, ('leaf', 'seq')), may hold values from -3 to 3
- w_out: bfloat16 [2, 1536, 1536], P(None, 'tensor', ('leaf', 'seq')), may hold values from -1.75 to 1.75
- mlp_gain: bfloat16 [2, 1536], P(None, ('leaf', 'seq')), may hold values from 0.5 to 1.5
- w_gate: bfloat16 [2, 1536, 8960], P(None, ('leaf', 'seq'), 'tensor'), may hold values from -0.15625 to 0.15625
- w_up: bfloat16 [2, 1536, 8960], P(None, ('leaf', 'seq'), 'tensor'), may hold values from -0.15625 to 0.15625
- w_down: bfloat16 [2, 8960, 1536], P(None, 'tensor', ('leaf', 'seq')), may hold values from -0.0625 to 0.0625
Outputs:
- hidden_out: bfloat16 [4, 1024, 1536], P('leaf', 'seq')
- input_grad: float32 [4, 1024, 1536], P('leaf', 'seq')
- attn_gain_grad: float32 [2, 1536], P(None, ('leaf', 'seq'))
- w_query_grad: float32 [2, 1536, 1536], P(None, ('leaf', 'seq'), 'tensor')
- b_query_grad: float32 [2, 12, 128], P(None, 'tensor', ('leaf', 'seq'))
- w_key_grad: float32 [2, 1536, 256], P(None, ('leaf', 'seq'))
- b_key_grad: float32 [2, 2, 128], P(None, None, ('leaf', 'seq'))
- w_value_grad: float32 [2, 1536, 256], P(None, ('leaf', 'seq'))
- b_value_grad: float32 [2, 2, 128], P(None, None, ('leaf', 'seq'))
- w_out_grad: float32 [2, 1536, 1536], P(None, 'tensor', ('leaf', 'seq'))
- mlp_gain_grad: float32 [2, 1536], P(None, ('leaf', 'seq'))
- w_gate_grad: float32 [2, 1536, 8960], P(None, ('leaf', 'seq'), 'tensor')
- w_up_grad: float32 [2, 1536, 8960], P(None, ('leaf', 'seq'), 'tensor')
- w_down_grad: float32 [2, 8960, 1536], P(None, 'tensor', ('leaf', 'seq'))
The draws below stay inside these ranges and needn't reach their ends.
Inputs may be any that keep to these rules, and one draw needn't show every extreme that they name: `parents`: in every row, block 0 gives -1; blocks 1 to 3 and the last block 7 give b - 1; every other block b gives a block from 3 to b - 1.
All inputs are finite; a program needn't handle non-finite values.
Results may differ from the reference program's by a relative error of at most 0.035.
Values may be sent and summed in bfloat16 or wider, within the bound.
No kernel may reach another device: no remote copies, remote signals or barrier semaphores. Data moves between devices by JAX's collectives and lax.ppermute only.
A program may use at most 384 MiB of HBM per device.

```python
import math
import jax
import jax.numpy as jnp
from jax import lax

D = 1536
H = 12
KVH = 2
HD = 128
FF = 8960
LAYERS = 2
BLK = 128
NBLK = 8
TRUNK = 4
TREE_LEN = 1024
TREES = 4


def draw_parents(key, part):
    block_ids = jnp.arange(NBLK, dtype=jnp.int32)
    lowest = jnp.where(block_ids < TRUNK, block_ids - 1, TRUNK - 1)
    spread = jnp.maximum(block_ids - lowest, 1)
    raw_bits = jax.random.randint(key, (TREES, NBLK), 0, 1 << 20, dtype=jnp.int32)
    chosen = lowest[None, :] + raw_bits % spread[None, :]
    chosen = jnp.where(block_ids[None, :] < TRUNK, block_ids[None, :] - 1, chosen)
    chosen = jnp.where(block_ids[None, :] == NBLK - 1, NBLK - 2, chosen)
    return chosen.astype(jnp.int32)


def steps_of(key, shape, pieces, low, top_value):
    loudness = 1.0
    for dim, shards_of in pieces:
        steps = jax.random.uniform(jax.random.fold_in(jax.random.fold_in(key, 6), dim), (shards_of,), jnp.float32, low / len(pieces), top_value / len(pieces))
        loudness = loudness * jnp.repeat(jnp.exp(steps), shape[dim] // shards_of).reshape((-1,) + (1,) * (len(shape) - 1 - dim))
    return loudness


def scatter_about(stream_key, extent, width, most, cuts=(), held_as=jnp.bfloat16):
    result = width * jax.random.normal(stream_key, extent, jnp.float32)
    if cuts:
        result = result * steps_of(stream_key, extent, cuts, -0.22, 0.18)
    return jnp.clip(result, -most, most).astype(held_as)


def setup_inputs(seed: int = 0) -> dict:
    arg_keys = jax.random.split(jax.random.key(seed), 16)
    hidden_in = scatter_about(arg_keys[0], (TREES, TREE_LEN, D), 1.0, 6.0, ((0, 2), (1, 4)))
    parents = draw_parents(jax.random.fold_in(arg_keys[15], 71), 0)
    cotangent = scatter_about(arg_keys[2], (TREES, TREE_LEN, D), 1.0, 6.0, ((0, 2), (1, 4)))
    attn_gain = jnp.clip(1.0 + 0.1 * jax.random.normal(arg_keys[3], (LAYERS, D), jnp.float32), 0.5, 1.5).astype(jnp.bfloat16)
    w_query = scatter_about(arg_keys[4], (LAYERS, D, H * HD), D ** -0.5, 0.15625, ((1, 8), (2, 4)))
    b_query = scatter_about(arg_keys[5], (LAYERS, H, HD), 0.5, 3.0, ((1, 4), (2, 8)))
    w_key = scatter_about(arg_keys[6], (LAYERS, D, KVH * HD), D ** -0.5, 0.15625, ((1, 8),))
    b_key = scatter_about(arg_keys[7], (LAYERS, KVH, HD), 0.5, 3.0, ((2, 8),))
    w_value = scatter_about(arg_keys[8], (LAYERS, D, KVH * HD), D ** -0.5, 0.15625, ((1, 8),))
    b_value = scatter_about(arg_keys[9], (LAYERS, KVH, HD), 0.5, 3.0, ((2, 8),))
    w_out = scatter_about(arg_keys[10], (LAYERS, H * HD, D), (H * HD // 128) ** -0.5, 1.75, ((1, 4), (2, 8)))
    mlp_gain = jnp.clip(1.0 + 0.1 * jax.random.normal(arg_keys[11], (LAYERS, D), jnp.float32), 0.5, 1.5).astype(jnp.bfloat16)
    w_gate = scatter_about(arg_keys[12], (LAYERS, D, FF), D ** -0.5, 0.15625, ((1, 8), (2, 4)))
    w_up = scatter_about(arg_keys[13], (LAYERS, D, FF), D ** -0.5, 0.15625, ((1, 8), (2, 4)))
    w_down = scatter_about(arg_keys[14], (LAYERS, FF, D), FF ** -0.5, 0.0625, ((1, 4), (2, 8)))
    return {"hidden_in": hidden_in, "parents": parents, "cotangent": cotangent, "attn_gain": attn_gain, "w_query": w_query, "b_query": b_query, "w_key": w_key, "b_key": b_key, "w_value": w_value, "b_value": b_value, "w_out": w_out, "mlp_gain": mlp_gain, "w_gate": w_gate, "w_up": w_up, "w_down": w_down}


eps_norm = 1e-06
rope_base = 1000000.0
neg_fill = -1e+30

@jax.custom_vjp
def low(v):
    return lax.optimization_barrier(v.astype(jnp.bfloat16)).astype(jnp.float32)

@jax.custom_vjp
def low_back(v):
    return v

def low_keep(v):
    return (low(v), None)

def low_pass(kept, grad):
    return (grad,)

def back_keep(v):
    return (v, None)

def back_low(kept, grad):
    return (low(grad),)
low.defvjp(low_keep, low_pass)
low_back.defvjp(back_keep, back_low)

def matmul(left_op, right_op):
    return jnp.dot(left_op, right_op, precision=lax.Precision.HIGHEST)

def tree_tables(parent_row):
    block_ids = jnp.arange(NBLK, dtype=jnp.int32)
    reach_flag = block_ids[:, None] == block_ids[None, :]
    current = block_ids
    for walk_idx in range(NBLK):
        safe_idx = jnp.maximum(current, 0).astype(jnp.int32)
        current = jnp.where(current >= 0, parent_row[safe_idx], -1).astype(jnp.int32)
        reach_flag = reach_flag | (block_ids[None, :] == current[:, None])
    reach_tab = reach_flag.astype(jnp.int32)
    depth_tab = (lax.optimization_barrier(jnp.sum(reach_tab, axis=1)) - 1).astype(jnp.int32)
    return (reach_tab, depth_tab)

def token_tables(parent_row):
    reach_tab, depth_tab = tree_tables(parent_row)
    token_idx = jnp.arange(NBLK * BLK, dtype=jnp.int32)
    block_idx = token_idx // BLK
    position = (BLK * depth_tab[block_idx] + token_idx % BLK).astype(jnp.int32)
    visible = (reach_tab[block_idx][:, block_idx] > 0) & (token_idx[None, :] <= token_idx[:, None])
    return (position, visible)

def angles(position, head_dim):
    freq_idx = jnp.arange(head_dim // 2, dtype=jnp.float32)
    inv_freq = rope_base ** (-2.0 * freq_idx / head_dim)
    turn_val = position.astype(jnp.float32)[:, None] * inv_freq[None, :]
    return (jnp.cos(turn_val), jnp.sin(turn_val))

def rotate(values_in, cosine, sine_val):
    half_dim = values_in.shape[-1] // 2
    first_half = values_in[..., :half_dim]
    second_half = values_in[..., half_dim:]
    cos_wide = cosine[:, None, :]
    sin_wide = sine_val[:, None, :]
    return jnp.concatenate([first_half * cos_wide - second_half * sin_wide, second_half * cos_wide + first_half * sin_wide], axis=-1)

def rms_norm(values_in, gain_vec):
    inv_norm = lax.rsqrt(lax.optimization_barrier(jnp.mean(values_in * values_in, axis=-1, keepdims=True)) + eps_norm)
    return values_in * inv_norm * gain_vec

def layer_tree(hidden, position, visible, params):
    attn_gain, w_query, b_query, w_key, b_key, w_value, b_value, w_out, mlp_gain, w_gate, w_up, w_down = params
    count_tok = hidden.shape[0]
    heads_n = b_query.shape[0]
    kv_heads = b_key.shape[0]
    head_dim = b_query.shape[1]
    group_n = heads_n // kv_heads
    cosine, sine_val = angles(position, head_dim)
    normed = low(rms_norm(hidden, attn_gain))
    query_lin = low_back(matmul(normed, w_query) + b_query.reshape(-1))
    key_lin = low_back(matmul(normed, w_key) + b_key.reshape(-1))
    value_lin = low_back(matmul(normed, w_value) + b_value.reshape(-1))
    query_rot = low(rotate(query_lin.reshape(count_tok, heads_n, head_dim), cosine, sine_val))
    key_rot = low(rotate(key_lin.reshape(count_tok, kv_heads, head_dim), cosine, sine_val))
    value_low = low(value_lin.reshape(count_tok, kv_heads, head_dim))
    key_rep = jnp.repeat(key_rot, group_n, axis=1)
    value_rep = jnp.repeat(value_low, group_n, axis=1)
    scores = jnp.einsum('qhd,khd->hqk', query_rot, key_rep, precision=lax.Precision.HIGHEST) / math.sqrt(head_dim)
    scores = low_back(jnp.where(visible[None, :, :], scores, neg_fill))
    row_top = lax.optimization_barrier(jnp.max(scores, axis=-1, keepdims=True))
    expo_val = jnp.exp(scores - row_top)
    prob_tab = low(expo_val / lax.optimization_barrier(jnp.sum(expo_val, axis=-1, keepdims=True)))
    attended = jnp.einsum('hqk,khd->qhd', prob_tab, value_rep, precision=lax.Precision.HIGHEST)
    attended = low(low_back(attended.reshape(count_tok, heads_n * head_dim)))
    branch = low_back(matmul(attended, w_out))
    middle = hidden + branch
    normed_mlp = low(rms_norm(middle, mlp_gain))
    gate_val = low_back(matmul(normed_mlp, w_gate))
    up_val = low_back(matmul(normed_mlp, w_up))
    mixed_val = low(jax.nn.silu(gate_val) * up_val)
    return middle + low_back(matmul(mixed_val, w_down))

def forward(start_val, position, visible, params_all):
    hidden = start_val
    for layer_idx in range(LAYERS):
        params = tuple((member[layer_idx] for member in params_all))

        def tree_step(packed, params=params):
            return layer_tree(packed[0], packed[1], packed[2], params)
        hidden = lax.map(jax.checkpoint(tree_step), (hidden, position, visible))
    return hidden

def reference(hidden_in, parents, cotangent, attn_gain, w_query, b_query, w_key, b_key, w_value, b_value, w_out, mlp_gain, w_gate, w_up, w_down):
    position, visible = jax.vmap(token_tables)(parents)
    params_all = tuple((member.astype(jnp.float32) for member in (attn_gain, w_query, b_query, w_key, b_key, w_value, b_value, w_out, mlp_gain, w_gate, w_up, w_down)))

    def run_layers(start_val, weights):
        return forward(start_val, position, visible, weights)
    final_out, pullback = jax.vjp(run_layers, hidden_in.astype(jnp.float32), params_all)
    input_grad, weight_grads = pullback(cotangent.astype(jnp.float32))
    return (final_out.astype(jnp.bfloat16), input_grad, weight_grads[0], weight_grads[1], weight_grads[2], weight_grads[3], weight_grads[4], weight_grads[5], weight_grads[6], weight_grads[7], weight_grads[8], weight_grads[9], weight_grads[10], weight_grads[11])
```

```python
import functools
import math

import jax
import jax.numpy as jnp
from jax import lax
from jax.experimental import pallas as pl
from jax.experimental.pallas import tpu as pltpu
from jax.sharding import PartitionSpec as P

BLK = 128
NBLK = 8
PAD_ROWS = 16

eps_norm = 1e-06
rope_base = 1000000.0
neg_fill = -1e30

f32 = jnp.float32
bf16 = jnp.bfloat16


def matmul(left_op, right_op):
    return jnp.dot(left_op, right_op, preferred_element_type=f32)


def dot_left(left_op, right_op):
    return lax.dot_general(
        left_op, right_op, (((0,), (0,)), ((), ())), preferred_element_type=f32
    )


def dot_right(left_op, right_op):
    return lax.dot_general(
        left_op, right_op, (((1,), (1,)), ((), ())), preferred_element_type=f32
    )


def swap(array, axis, bit):
    size = lax.axis_size(axis)
    return lax.ppermute(array, axis, [(i, i ^ bit) for i in range(size)])


def axis_bits(axis):
    size = lax.axis_size(axis)
    return [1 << k for k in range(size.bit_length() - 1)]


def doubling_order(bits):
    order = [0]
    for bit in bits:
        order = order + [i ^ bit for i in order]
    return order


def gather_rows(own, axis, bits):
    current = own
    for bit in bits:
        current = jnp.concatenate([current, swap(current, axis, bit)], axis=0)
    return current


def scatter_rows(partial, axis, bits):
    current = partial
    for bit in bits:
        half = current.shape[0] // 2
        got = swap(current[half:].astype(bf16), axis, bit)
        current = current[:half].astype(f32) + got.astype(f32)
    return current


def fabric():
    seq_bits = axis_bits("seq")
    return (
        [("seq", bit) for bit in seq_bits[1:]]
        + [("leaf", bit) for bit in axis_bits("leaf")]
        + [("seq", bit) for bit in seq_bits[:1]]
    )


def fabric_order(flip):
    links = fabric()
    order = list(range(len(links)))
    outer = order[:-1]
    if flip:
        outer = outer[::-1]
    return outer + order[-1:]


def gather_blocks(own, flip):
    links = fabric()
    rows = own.shape[0]
    current = own
    index = [0]
    for k in fabric_order(flip):
        axis, bit = links[k]
        current = jnp.concatenate([current, swap(current, axis, bit)], axis=0)
        index = index + [i | (1 << k) for i in index]
    if index == list(range(len(index))):
        return current
    place = {i: p for p, i in enumerate(index)}
    return jnp.concatenate(
        [current[place[i] * rows : (place[i] + 1) * rows] for i in range(len(index))], axis=0
    )


def reduce_blocks(low_part, high_part, flip):
    links = fabric()
    axis, bit = links[-1]
    got = swap(high_part().astype(bf16), axis, bit)
    current = (low_part() + got.astype(f32)).astype(bf16)
    index = list(range(1 << (len(links) - 1)))
    rows = current.shape[0] // len(index)
    blocks = {i: current[i * rows : (i + 1) * rows] for i in index}
    for k in fabric_order(not flip)[:-1]:
        axis, bit = links[k]
        away = [i for i in index if i & (1 << k)]
        index = [i for i in index if not i & (1 << k)]
        got = swap(jnp.concatenate([blocks[i] for i in away], axis=0), axis, bit)
        total = {}
        for p, i in enumerate(index):
            part = got[p * rows : (p + 1) * rows].astype(f32)
            total[i] = blocks[i].astype(f32) + part
        blocks = {i: part if len(index) == 1 else part.astype(bf16) for i, part in total.items()}
    return blocks[0]


def tree_tables(parent_row):
    block_ids = jnp.arange(NBLK, dtype=jnp.int32)
    step_up = (block_ids[None, :] == parent_row[:, None]).astype(jnp.int32)
    reach_tab = jnp.eye(NBLK, dtype=jnp.int32) + step_up
    for repeat_idx in range(max(1, (NBLK - 1).bit_length())):
        reach_tab = (jnp.dot(reach_tab, reach_tab) > 0).astype(jnp.int32)
    depth_tab = jnp.sum(reach_tab, axis=1) - 1
    return (reach_tab, depth_tab)


def geometry(parent_row, token_idx, key_idx):
    reach_tab, depth_tab = tree_tables(parent_row)
    block_ids = jnp.arange(NBLK, dtype=jnp.int32)
    query_hot = (token_idx[:, None] // BLK == block_ids[None, :]).astype(f32)
    key_hot = (key_idx[:, None] // BLK == block_ids[None, :]).astype(f32)
    link_rows = jnp.dot(query_hot, reach_tab.astype(f32), precision=lax.Precision.HIGHEST)
    link_tab = jnp.dot(link_rows, key_hot.T, precision=lax.Precision.HIGHEST)
    visible = (link_tab > 0.5) & (key_idx[None, :] <= token_idx[:, None])
    depth_rows = jnp.dot(query_hot, depth_tab.astype(f32), precision=lax.Precision.HIGHEST)
    position = BLK * depth_rows + (token_idx % BLK).astype(f32)
    return (position, visible.astype(f32))


def wide_angles(position, head_dim):
    freq_idx = jnp.arange(head_dim // 2, dtype=f32)
    inv_freq = rope_base ** (-2.0 * freq_idx / head_dim)
    turn_val = position[:, None] * inv_freq[None, :]
    cosine, sine_val = (jnp.cos(turn_val), jnp.sin(turn_val))
    return (
        jnp.concatenate([cosine, cosine], axis=1),
        jnp.concatenate([-sine_val, sine_val], axis=1),
    )


def project_kernel(heads, head_dim, x_ref, w_ref, b_ref, cos_ref, sin_ref, q_ref, kv_ref):
    lin = jnp.dot(x_ref[...], w_ref[...], preferred_element_type=f32) + b_ref[...]
    cos_wide = cos_ref[...]
    sin_wide = sin_ref[...]
    for h in range(heads + 1):
        part = lin[:, h * head_dim : (h + 1) * head_dim]
        turned = part * cos_wide + pltpu.roll(part, head_dim // 2, 1) * sin_wide
        if h < heads:
            q_ref[:, h * head_dim : (h + 1) * head_dim] = turned.astype(bf16)
        else:
            kv_ref[:, :head_dim] = turned.astype(bf16)
    kv_ref[:, head_dim:] = lin[:, (heads + 1) * head_dim :].astype(bf16)


def project(normed, w_qkv, bias, cos_wide, sin_wide, heads, head_dim):
    rows, width = normed.shape
    cols = w_qkv.shape[1]
    return pl.pallas_call(
        functools.partial(project_kernel, heads, head_dim),
        out_shape=(
            jax.ShapeDtypeStruct((rows, heads * head_dim), bf16),
            jax.ShapeDtypeStruct((rows, 2 * head_dim), bf16),
        ),
        compiler_params=pltpu.CompilerParams(vmem_limit_bytes=32 << 20),
        cost_estimate=pl.CostEstimate(
            flops=2 * rows * width * cols,
            bytes_accessed=2 * (rows * width + width * cols + rows * cols),
            transcendentals=0,
        ),
        name="project",
    )(normed, w_qkv, bias, cos_wide, sin_wide)


def attend_kernel(heads, head_dim, scale, q_ref, kv_ref, vis_ref, o_ref, lse_ref):
    keys = kv_ref[:, :head_dim]
    values = kv_ref[:, head_dim:]
    seen = vis_ref[...] > 0.5
    lane = lax.broadcasted_iota(jnp.int32, lse_ref.shape, 1)
    lse_all = jnp.zeros(lse_ref.shape, f32)
    for h in range(heads):
        cols = slice(h * head_dim, (h + 1) * head_dim)
        scores = lax.dot_general(
            q_ref[:, cols], keys, (((1,), (1,)), ((), ())), preferred_element_type=f32
        )
        scores = jnp.where(seen, scores * scale, neg_fill)
        top = jnp.max(scores, axis=1, keepdims=True)
        expo = jnp.exp(scores - top)
        total = jnp.sum(expo, axis=1, keepdims=True)
        prob = (expo * (1.0 / total)).astype(bf16)
        o_ref[:, cols] = jnp.dot(prob, values, preferred_element_type=f32).astype(bf16)
        lse_all = jnp.where(lane == h, top + jnp.log(total), lse_all)
    lse_ref[...] = lse_all


def attend(query, kv_all, visible, heads, head_dim):
    rows = query.shape[0]
    keys = kv_all.shape[0]
    return pl.pallas_call(
        functools.partial(attend_kernel, heads, head_dim, 1.0 / math.sqrt(head_dim)),
        out_shape=(
            jax.ShapeDtypeStruct((rows, heads * head_dim), bf16),
            jax.ShapeDtypeStruct((rows, 128), f32),
        ),
        compiler_params=pltpu.CompilerParams(vmem_limit_bytes=40 << 20),
        cost_estimate=pl.CostEstimate(
            flops=4 * rows * keys * heads * head_dim,
            bytes_accessed=4 * rows * keys + 4 * rows * heads * head_dim + 4 * keys * head_dim,
            transcendentals=rows * keys * heads,
        ),
        name="attend",
    )(query, kv_all, visible)


def attend_back_kernel(
    heads, head_dim, scale, q_ref, kv_ref, vis_ref, lse_ref, do_ref, cos_ref, sin_ref,
    dq_ref, keep_ref, send_ref,
):
    keys = kv_ref[:, :head_dim]
    values = kv_ref[:, head_dim:]
    seen = vis_ref[...] > 0.5
    cos_wide = cos_ref[...]
    sin_wide = sin_ref[...]
    dkey = None
    for h in range(heads):
        cols = slice(h * head_dim, (h + 1) * head_dim)
        query = q_ref[:, cols]
        dout = do_ref[:, cols]
        scores = lax.dot_general(
            query, keys, (((1,), (1,)), ((), ())), preferred_element_type=f32
        )
        scores = jnp.where(seen, scores * scale, neg_fill)
        prob = jnp.exp(scores - lse_ref[:, h : h + 1])
        dprob = lax.dot_general(
            dout, values, (((1,), (1,)), ((), ())), preferred_element_type=f32
        )
        delta = jnp.sum(prob * dprob, axis=1, keepdims=True)
        dscore = (prob * (dprob - delta)).astype(bf16)
        dquery = jnp.dot(dscore, keys, preferred_element_type=f32) * scale
        dquery = dquery * cos_wide - pltpu.roll(dquery, head_dim // 2, 1) * sin_wide
        dq_ref[:, cols] = dquery.astype(bf16)
        dk_part = lax.dot_general(
            dscore, query, (((0,), (0,)), ((), ())), preferred_element_type=f32
        )
        dv_part = lax.dot_general(
            prob.astype(bf16), dout, (((0,), (0,)), ((), ())), preferred_element_type=f32
        )
        if dkey is None:
            dkey, dvalue = (dk_part, dv_part)
        else:
            dkey, dvalue = (dkey + dk_part, dvalue + dv_part)
    dkey = dkey * scale
    half = keep_ref.shape[0]
    keep_ref[:, :head_dim] = dkey[:half]
    keep_ref[:, head_dim:] = dvalue[:half]
    send_ref[:, :head_dim] = dkey[half:].astype(bf16)
    send_ref[:, head_dim:] = dvalue[half:].astype(bf16)


def attend_back(query, kv_all, visible, lse, dout, cos_wide, sin_wide, heads, head_dim):
    rows = query.shape[0]
    keys = kv_all.shape[0]
    return pl.pallas_call(
        functools.partial(attend_back_kernel, heads, head_dim, 1.0 / math.sqrt(head_dim)),
        out_shape=(
            jax.ShapeDtypeStruct((rows, heads * head_dim), bf16),
            jax.ShapeDtypeStruct((keys // 2, 2 * head_dim), f32),
            jax.ShapeDtypeStruct((keys // 2, 2 * head_dim), bf16),
        ),
        compiler_params=pltpu.CompilerParams(vmem_limit_bytes=48 << 20),
        cost_estimate=pl.CostEstimate(
            flops=10 * rows * keys * heads * head_dim,
            bytes_accessed=4 * rows * keys + 8 * rows * heads * head_dim + 10 * keys * head_dim,
            transcendentals=rows * keys * heads,
        ),
        name="attend_back",
    )(query, kv_all, visible, lse, dout, cos_wide, sin_wide)


def inv_rms(values):
    return lax.rsqrt(jnp.mean(values * values, axis=1, keepdims=True) + eps_norm)


def norm_back(carry_grad, dnorm_in, source, inv_norm, gain_row):
    gain_term = jnp.sum(dnorm_in * source * inv_norm, axis=0)
    scaled = dnorm_in * gain_row
    cube_val = inv_norm * inv_norm * inv_norm
    new_grad = (
        carry_grad
        + inv_norm * scaled
        - source * cube_val * jnp.mean(scaled * source, axis=1, keepdims=True)
    )
    return (new_grad, gain_term)


def body(
    hidden_in,
    parents,
    cotangent,
    attn_gain,
    w_query,
    b_query,
    w_key,
    b_key,
    w_value,
    b_value,
    w_out,
    mlp_gain,
    w_gate,
    w_up,
    w_down,
):
    micro_n, rows_dev, width = hidden_in.shape
    layer_n, shard = w_query.shape[:2]
    heads = b_query.shape[1]
    bias_cols = b_query.shape[2]
    kv_heads = b_key.shape[1]
    head_dim = w_key.shape[2] // kv_heads
    tensor_n = lax.axis_size("tensor")
    seq_n = lax.axis_size("seq")
    leaf_n = lax.axis_size("leaf")
    tensor_i = lax.axis_index("tensor")
    seq_i = lax.axis_index("seq")
    leaf_i = lax.axis_index("leaf")
    group_heads = heads * tensor_n // kv_heads
    kv_group = tensor_i * heads // group_heads
    q_cols = heads * head_dim
    qkv_cols = q_cols + 2 * head_dim
    links = fabric()
    block_n = 1 << len(links)

    z_bits = axis_bits("tensor")
    z_order = doubling_order(z_bits[::-1])
    share = rows_dev // tensor_n
    s_bits = axis_bits("seq")[::-1]
    s_order = doubling_order(s_bits)

    def z_scatter(partial):
        return scatter_rows(partial, "tensor", z_bits)

    def z_gather(own):
        return gather_rows(own, "tensor", z_bits[::-1])

    def block_home(block):
        seq_rel = sum(
            ((block >> k) & 1) * bit for k, (axis, bit) in enumerate(links) if axis == "seq"
        )
        leaf_rel = sum(
            ((block >> k) & 1) * bit for k, (axis, bit) in enumerate(links) if axis == "leaf"
        )
        return (leaf_i ^ leaf_rel) * seq_n + (seq_i ^ seq_rel)

    feature = jnp.arange(width, dtype=jnp.int32)
    feature_home = block_home(feature // shard) * shard + feature % shard
    feature_perm = (feature[:, None] == feature_home[None, :]).astype(bf16)
    block_ids = jnp.arange(block_n, dtype=jnp.int32)
    block_perm = (block_ids[:, None] == block_home(block_ids)[None, :]).astype(f32)

    def rows_in(array):
        return jnp.concatenate(
            [
                lax.dynamic_slice_in_dim(array, (tensor_i ^ rel) * share, share, 0)
                for rel in z_order
            ],
            axis=0,
        )

    place_of = [z_order.index(rel) for rel in range(tensor_n)]

    def rows_out(array):
        place_tab = jnp.array(place_of, dtype=jnp.int32)
        return jnp.concatenate(
            [
                lax.dynamic_slice_in_dim(array, place_tab[tensor_i ^ spot] * share, share, 0)
                for spot in range(tensor_n)
            ],
            axis=0,
        )

    def pack_small(gain1, gain2, bias_q, bias_k, bias_v):
        flat = jnp.concatenate([gain1, gain2, bias_q, bias_k, bias_v], axis=-1)
        return jnp.pad(flat, [(0, 0)] * (flat.ndim - 1) + [(0, qkv_cols - flat.shape[-1])])

    weights = []
    for layer in range(layer_n):
        flip = layer % 2 == 1
        small = pack_small(
            attn_gain[layer],
            mlp_gain[layer],
            b_query[layer].reshape(-1),
            lax.dynamic_slice_in_dim(b_key[layer], kv_group, 1, 0).reshape(-1),
            lax.dynamic_slice_in_dim(b_value[layer], kv_group, 1, 0).reshape(-1),
        )
        own = jnp.concatenate(
            [
                w_query[layer],
                lax.dynamic_slice_in_dim(w_key[layer], kv_group * head_dim, head_dim, 1),
                lax.dynamic_slice_in_dim(w_value[layer], kv_group * head_dim, head_dim, 1),
            ],
            axis=1,
        )
        own = jnp.concatenate([own, jnp.pad(small[None], ((0, PAD_ROWS - 1), (0, 0)))], axis=0)
        packed = gather_blocks(own, flip).reshape(block_n, shard + PAD_ROWS, qkv_cols)
        w_qkv = packed[:, :shard].reshape(width, qkv_cols)
        small_all = packed[:, shard].astype(f32)
        gain1 = small_all[:, :shard].reshape(1, width)
        gain2 = small_all[:, shard : 2 * shard].reshape(1, width)
        bias_part = jnp.dot(
            block_perm,
            small_all[:, 2 * shard : 2 * shard + (heads + 2) * bias_cols],
            precision=lax.Precision.HIGHEST,
        )
        bias = (
            bias_part.reshape(block_n, heads + 2, bias_cols)
            .transpose(1, 0, 2)
            .reshape(1, qkv_cols)
        )
        w_out_t = gather_blocks(w_out[layer].T, not flip)
        w_gate_all = gather_blocks(w_gate[layer], flip)
        w_up_all = gather_blocks(w_up[layer], not flip)
        w_down_t = gather_blocks(w_down[layer].T, flip)
        weights.append((w_qkv, bias, gain1, gain2, w_out_t, w_gate_all, w_up_all, w_down_t))

    row_ids = jnp.arange(rows_dev, dtype=jnp.int32)
    z_tab = jnp.array(z_order, dtype=jnp.int32)
    local_row = (tensor_i ^ z_tab[row_ids // share]) * share + row_ids % share
    token_idx = seq_i * rows_dev + local_row
    s_tab = jnp.array(s_order, dtype=jnp.int32)
    key_idx = ((seq_i ^ s_tab)[:, None] * rows_dev + local_row[None, :]).reshape(-1)
    tables = []
    for micro in range(micro_n):
        position, visible = geometry(parents[micro], token_idx, key_idx)
        cos_wide, sin_wide = wide_angles(position, head_dim)
        tables.append((cos_wide, sin_wide, visible))

    states = []
    normed_first = []
    for micro in range(micro_n):
        start = matmul(rows_in(hidden_in[micro]), feature_perm)
        states.append(start[:share])
        normed_first.append((start * inv_rms(start) * weights[0][2]).astype(bf16))
    kept = {}
    for layer in range(layer_n):
        w_qkv, bias, gain1, gain2, w_out_t, w_gate_all, w_up_all, w_down_t = weights[layer]
        for micro in range(micro_n):
            cos_wide, sin_wide, visible = tables[micro]
            start = states[micro]
            inv_attn = inv_rms(start)
            if layer == 0:
                normed = normed_first[micro]
            else:
                normed = z_gather((start * inv_attn * gain1).astype(bf16))
            query, kv_own = project(normed, w_qkv, bias, cos_wide, sin_wide, heads, head_dim)
            kv_all = gather_rows(kv_own, "seq", s_bits)
            attended, lse = attend(query, kv_all, visible, heads, head_dim)
            middle = start + z_scatter(dot_right(attended, w_out_t))
            inv_mlp = inv_rms(middle)
            normed_mlp = z_gather((middle * inv_mlp * gain2).astype(bf16))
            gate = matmul(normed_mlp, w_gate_all)
            up = matmul(normed_mlp, w_up_all)
            mixed = (jax.nn.silu(gate) * up).astype(bf16)
            states[micro] = middle + z_scatter(dot_right(mixed, w_down_t))
            kept[layer, micro] = (
                start, inv_attn, normed, query, kv_all, lse, attended,
                middle, inv_mlp, normed_mlp, gate, up, mixed,
            )
    hidden_out = jnp.stack(
        [
            dot_right(rows_out(z_gather(states[micro].astype(bf16))), feature_perm).astype(bf16)
            for micro in range(micro_n)
        ]
    )

    grads = []
    downs = []
    for micro in range(micro_n):
        full = matmul(rows_in(cotangent[micro]), feature_perm)
        grads.append(full[:share])
        downs.append(full.astype(bf16))
    results = [None] * layer_n

    def cat(parts):
        return jnp.concatenate(parts, axis=0)

    half = width // 2

    def weight_grad(left, right, flip):
        return reduce_blocks(
            lambda: dot_left(left[:, :half], right), lambda: dot_left(left[:, half:], right), flip
        )

    for layer in reversed(range(layer_n)):
        flip = layer % 2 == 1
        w_qkv, bias, gain1, gain2, w_out_t, w_gate_all, w_up_all, w_down_t = weights[layer]
        sides = {name: [] for name in ("down", "gate", "up", "out", "lin")}
        gain1_terms = []
        gain2_terms = []
        middles = []
        for micro in range(micro_n):
            (
                start, inv_attn, normed, query, kv_all, lse, attended,
                middle, inv_mlp, normed_mlp, gate, up, mixed,
            ) = kept[layer, micro]
            grad_out = grads[micro]
            if downs[micro] is None:
                downs[micro] = z_gather(grad_out.astype(bf16))
            down_in = downs[micro]
            dmixed = matmul(down_in, w_down_t)
            sig = jax.nn.sigmoid(gate)
            dgate = (dmixed * up * sig * (1.0 + gate * (1.0 - sig))).astype(bf16)
            dup = (dmixed * (gate * sig)).astype(bf16)
            sides["down"].append(down_in)
            sides["gate"].append(dgate)
            sides["up"].append(dup)
            dnorm = z_scatter(dot_right(dgate, w_gate_all) + dot_right(dup, w_up_all))
            grad_mid, gain_term = norm_back(grad_out, dnorm, middle, inv_mlp, gain2)
            gain2_terms.append(gain_term)
            out_in = z_gather(grad_mid.astype(bf16))
            sides["out"].append(out_in)
            middles.append(grad_mid)
        for micro in range(micro_n):
            (
                start, inv_attn, normed, query, kv_all, lse, attended,
                middle, inv_mlp, normed_mlp, gate, up, mixed,
            ) = kept[layer, micro]
            cos_wide, sin_wide, visible = tables[micro]
            dattended = matmul(sides["out"][micro], w_out_t).astype(bf16)
            dquery, keep_kv, send_kv = attend_back(
                query, kv_all, visible, lse, dattended, cos_wide, sin_wide, heads, head_dim
            )
            got = swap(send_kv, "seq", s_bits[-1])
            dkv = scatter_rows(keep_kv + got.astype(f32), "seq", s_bits[:-1][::-1])
            dkey = dkv[:, :head_dim]
            dkey = dkey * cos_wide - jnp.roll(dkey, head_dim // 2, axis=1) * sin_wide
            dlin = jnp.concatenate(
                [dquery, dkey.astype(bf16), dkv[:, head_dim:].astype(bf16)], axis=1
            )
            sides["lin"].append(dlin)
            dnorm = z_scatter(dot_right(dlin, w_qkv))
            grad_in, gain_term = norm_back(middles[micro], dnorm, start, inv_attn, gain1)
            gain1_terms.append(gain_term)
            grads[micro] = grad_in
            downs[micro] = None
        saved = {
            name: cat([kept[layer, micro][spot] for micro in range(micro_n)])
            for name, spot in (("normed", 2), ("attended", 6), ("mlp", 9), ("mixed", 12))
        }
        stacked = {name: cat(parts) for name, parts in sides.items()}
        down_t = weight_grad(stacked["down"], saved["mixed"], flip)
        gate_g = weight_grad(saved["mlp"], stacked["gate"], flip)
        up_g = weight_grad(saved["mlp"], stacked["up"], not flip)
        out_t = weight_grad(stacked["out"], saved["attended"], not flip)

        bias_sum = jnp.sum(stacked["lin"].astype(f32), axis=0)
        bias_blocks = bias_sum.reshape(heads + 2, block_n, bias_cols).transpose(1, 0, 2)
        bias_blocks = jnp.dot(
            block_perm.T,
            bias_blocks.reshape(block_n, (heads + 2) * bias_cols),
            precision=lax.Precision.HIGHEST,
        )
        small = jnp.concatenate(
            [
                sum(gain1_terms).reshape(block_n, shard),
                sum(gain2_terms).reshape(block_n, shard),
                bias_blocks,
            ],
            axis=1,
        )
        small = jnp.pad(small, ((0, 0), (0, qkv_cols - small.shape[1])))
        small = jnp.pad(small[:, None], ((0, 0), (0, PAD_ROWS - 1), (0, 0)))

        def with_small(part, rows_of_small):
            blocks = part.reshape(-1, shard, qkv_cols)
            return jnp.concatenate([blocks, rows_of_small], axis=1).reshape(-1, qkv_cols)

        normed_all, lin_all = (saved["normed"], stacked["lin"])
        packed = reduce_blocks(
            lambda: with_small(dot_left(normed_all[:, :half], lin_all), small[: block_n // 2]),
            lambda: with_small(dot_left(normed_all[:, half:], lin_all), small[block_n // 2 :]),
            flip,
        )
        query_g = packed[:shard, :q_cols]
        small_g = packed[shard]
        cross = jnp.concatenate(
            [packed[:shard, q_cols:], packed[shard : shard + PAD_ROWS, : 2 * head_dim],
             packed[shard : shard + PAD_ROWS, 2 * head_dim : 4 * head_dim]],
            axis=0,
        ).astype(bf16)
        cross = gather_rows(cross, "tensor", z_bits[::-1]).astype(f32)
        cross = cross.reshape(tensor_n, shard + 2 * PAD_ROWS, 2 * head_dim)
        groups = (tensor_i ^ z_tab) * heads // group_heads
        tail = jnp.concatenate([cross[:, shard], cross[:, shard + PAD_ROWS]], axis=1)
        gains_g = jnp.sum(tail[:, : 2 * shard], axis=0)
        key_parts = cross[:, :shard, :head_dim]
        value_parts = cross[:, :shard, head_dim:]
        bias_at = 2 * shard + heads * bias_cols
        bk_parts = tail[:, bias_at : bias_at + bias_cols]
        bv_parts = tail[:, bias_at + bias_cols : bias_at + 2 * bias_cols]

        def by_group(parts):
            pick = [
                (groups == g).astype(f32).reshape((-1,) + (1,) * (parts.ndim - 1))
                for g in range(kv_heads)
            ]
            return [jnp.sum(parts * p, axis=0) for p in pick]

        results[layer] = (
            gains_g[:shard],
            query_g,
            small_g[2 * shard : bias_at].reshape(heads, bias_cols),
            jnp.concatenate(by_group(key_parts), axis=1),
            jnp.stack(by_group(bk_parts)),
            jnp.concatenate(by_group(value_parts), axis=1),
            jnp.stack(by_group(bv_parts)),
            out_t.T,
            gains_g[shard : 2 * shard],
            gate_g,
            up_g,
            down_t.T,
        )
    input_grad = jnp.stack(
        [
            dot_right(rows_out(z_gather(grads[micro].astype(bf16))), feature_perm)
            for micro in range(micro_n)
        ]
    )
    return (hidden_out, input_grad) + tuple(
        jnp.stack([results[layer][spot] for layer in range(layer_n)]) for spot in range(12)
    )


def solution(mesh):
    both = ("leaf", "seq")
    return jax.shard_map(
        body,
        mesh=mesh,
        in_specs=(
            P("leaf", "seq", None),
            P("leaf", None),
            P("leaf", "seq", None),
            P(None, both),
            P(None, both, "tensor"),
            P(None, "tensor", both),
            P(None, both, None),
            P(None, None, both),
            P(None, both, None),
            P(None, None, both),
            P(None, "tensor", both),
            P(None, both),
            P(None, both, "tensor"),
            P(None, both, "tensor"),
            P(None, "tensor", both),
        ),
        out_specs=(
            P("leaf", "seq", None),
            P("leaf", "seq", None),
            P(None, both),
            P(None, both, "tensor"),
            P(None, "tensor", both),
            P(None, both, None),
            P(None, None, both),
            P(None, both, None),
            P(None, None, both),
            P(None, "tensor", both),
            P(None, both),
            P(None, both, "tensor"),
            P(None, both, "tensor"),
            P(None, "tensor", both),
        ),
        check_vma=False,
    )
```

```python
import functools
import math

import jax
import jax.numpy as jnp
from jax import lax
from jax.experimental import pallas as pl
from jax.experimental.pallas import tpu as pltpu
from jax.sharding import PartitionSpec as P

BLK = 128
NBLK = 8
PAD = 16
COST = 16
TIMES = {
    "entry": 2.5,
    "mlp": 14,
    "mlp_back": 15,
    "attend": 5,
    "attend_back": 7.5,
    "lin_back": 4.5,
    "project": 4.2,
    "weight_grad": 9,
    "fold_rows": 3,
    "weight_grad_small": 4,
    "fold": 1.3,
    "join": 1.2,
    "add": 1.0,
    "finish_grads": 3,
}
START = 1.5
LINKS = {"z1": 11.0, "z2": 12.0, "kv": 6.5, "core": 3.0, "core_w": 9.0, "row2": 42.0, "row1": 22.0,
         "row2_small": 12.0, "row1_small": 7.0}


def cost(name):
    return pl.CostEstimate(
        flops=int(TIMES.get(name, 2) * ORDER[0].scale * 1.15e9), bytes_accessed=1000, transcendentals=0
    )


class Order:
    def __init__(self):
        self.last = None
        self.now = 0.0
        self.free = {}
        self.scale = COST

    def link(self, kind, wire, at):
        begin = max(at, self.free.get(wire, 0.0))
        end = begin + LINKS[kind]
        self.free[wire] = end - 2.0
        self.now += START
        return end

    def took(self, outs):
        self.last = min(outs, key=lambda a: math.prod(a.shape))

    def run(self, tasks, more):
        waiting = [[task, next(task)] for task in tasks]
        while waiting or more:
            while more:
                task = more.pop()
                waiting.append([task, next(task)])
            ready = []
            for entry_ in waiting:
                name, when, rank = entry_[1]
                when = when() if callable(when) else when
                if when is not None:
                    ready.append((entry_, name, when, rank))
            soonest = min(when for _, _, when, _ in ready)
            self.now = max(self.now, soonest)
            chosen = min(
                (item for item in ready if item[2] <= self.now), key=lambda item: (item[3], item[2])
            )
            self.now += TIMES.get(chosen[1], 2.0)
            try:
                chosen[0][1] = chosen[0][0].send(self.now)
            except StopIteration:
                waiting.remove(chosen[0])


ORDER = [Order()]


eps_norm = 1e-06
rope_base = 1000000.0
neg_fill = -1e30

f32 = jnp.float32
bf16 = jnp.bfloat16

ANY = pl.BlockSpec(memory_space=pl.ANY)
HBM = pl.BlockSpec(memory_space=pltpu.HBM)
LOAD = pl.BlockSpec(memory_space=pltpu.HBM)
STORE = pl.BlockSpec(memory_space=pltpu.HBM)
VMEM = pl.BlockSpec(memory_space=pltpu.VMEM)
SMEM = pl.BlockSpec(memory_space=pltpu.SMEM)


def dot(left_op, right_op):
    return jnp.dot(left_op, right_op, preferred_element_type=f32)


def dot_left(left_op, right_op):
    return lax.dot_general(
        left_op, right_op, (((0,), (0,)), ((), ())), preferred_element_type=f32
    )


def dot_right(left_op, right_op):
    return lax.dot_general(
        left_op, right_op, (((1,), (1,)), ((), ())), preferred_element_type=f32
    )


def spans(total, step):
    return [(at, min(step, total - at)) for at in range(0, total, step)]


def shape(dims, dtype):
    return jax.ShapeDtypeStruct(tuple(dims), dtype)


EARLY = []


def flush(ref):
    for item in EARLY[-1]:
        if item[0] is ref and not item[2]:
            item[1].start()
            item[2] = True


def call(kernel, name, out_shape, in_specs, operands, scratch=(), out_specs=None, deps=(), **more):
    several = isinstance(out_shape, tuple)
    outs = out_shape if several else (out_shape,)
    if out_specs is None:
        out_specs = tuple(VMEM for _ in outs)
    order = ORDER[0]
    if order.last is not None:
        deps = tuple(deps) + (order.last,)
    count = len(operands)
    size = lambda a: math.prod(a.shape) * jnp.dtype(a.dtype).itemsize
    token = not any(spec is VMEM for spec in out_specs)
    if token:
        out_shape = outs = tuple(outs) + (shape((8, 128), f32),)
        spec = pl.BlockSpec((8, 128), lambda i: (0, 0)) if "grid" in more else VMEM
        out_specs = tuple(out_specs) + (spec,)
        plain = kernel

        def kernel(*refs):
            mark = refs[count + len(outs) - 1]
            mark[...] = jnp.zeros(mark.shape, f32)
            plain(*refs[: count + len(outs) - 1], *refs[count + len(outs) :])

    if "grid" in more:
        room = 24 << 20
        loads, stores = [], []
    else:
        loads = [n for n, spec in enumerate(in_specs) if spec is LOAD]
        stores = [n for n, spec in enumerate(out_specs) if spec is STORE]
        fast = (VMEM, LOAD, STORE)
        room = sum(size(a) for a, spec in zip(operands, in_specs) if spec in fast)
        room += sum(size(a) for a, spec in zip(outs, out_specs) if spec in fast)
        room += sum(size(a) for a in scratch if a.memory_space == pltpu.VMEM)
        room = min(58 << 20, room + room // 2 + (6 << 20))
    moved = [operands[n] for n in loads] + [outs[n] for n in stores]
    extra = [pltpu.VMEM(a.shape, a.dtype) for a in moved]
    if moved:
        extra.append(pltpu.SemaphoreType.DMA((len(moved),)))

    def wrapped(*refs):
        ins, rest = list(refs[:count]), refs[count + len(deps) :]
        results, rest = list(rest[: len(outs)]), rest[len(outs) :]
        inner, rest = rest[: len(scratch)], rest[len(scratch) :]
        copies, items = [], []
        for k, n in enumerate(loads):
            copies.append(pltpu.make_async_copy(ins[n], rest[k], rest[-1].at[k]))
            ins[n] = rest[k]
        for copy in copies:
            copy.start()
        for k, n in enumerate(stores, len(loads)):
            items.append([rest[k], pltpu.make_async_copy(rest[k], results[n], rest[-1].at[k]), False])
            results[n] = rest[k]
        for copy in copies:
            copy.wait()
        EARLY.append(items)
        kernel(*ins, *results, *inner)
        EARLY.pop()
        for item in items:
            if not item[2]:
                item[1].start()
        for item in items:
            item[1].wait()

    made = pl.pallas_call(
        wrapped,
        out_shape=outs,
        in_specs=list(in_specs) + [ANY] * len(deps),
        out_specs=tuple(out_specs),
        scratch_shapes=list(scratch) + extra,
        compiler_params=pltpu.CompilerParams(vmem_limit_bytes=room),
        cost_estimate=cost(name),
        name=name,
        **more,
    )(*operands, *deps)
    order.took(made)
    if token:
        made = made[:-1]
    return made if several else made[0]


def swap(array, axis, bit):
    size = lax.axis_size(axis)
    return lax.ppermute(array, axis, [(i, i ^ bit) for i in range(size)])


def axis_bits(axis):
    size = lax.axis_size(axis)
    return [1 << k for k in range(size.bit_length() - 1)]


def fabric(flip):
    seq_bits = axis_bits("seq")
    outer = [("seq", bit) for bit in seq_bits[1:]] + [("leaf", bit) for bit in axis_bits("leaf")]
    return (outer[::-1] if flip else outer) + [("seq", seq_bits[0])]


def gather_pieces(own, flip):
    pieces = [own]
    for axis, bit in fabric(flip):
        pieces = pieces + [swap(piece, axis, bit) for piece in pieces]
    return pieces


class Place:
    def __init__(self):
        self.tensor_i = lax.axis_index("tensor")
        self.seq_i = lax.axis_index("seq")
        self.leaf_i = lax.axis_index("leaf")
        self.seq_n = lax.axis_size("seq")
        self.leaf_n = lax.axis_size("leaf")
        self.blocks = self.seq_n * self.leaf_n
        values = [self.tensor_i & 1, self.tensor_i >> 1]
        self.at = {"half": 0, "quarter": 1}
        for flip in (False, True):
            self.at["blocks", flip] = len(values)
            values += self.homes(fabric(flip))
            self.at["grads", flip] = len(values)
            values += self.homes(fabric(not flip)[:-1] + fabric(flip)[-1:])
        self.at["seq"] = len(values)
        values += self.seq_homes()
        self.at["chip"] = len(values)
        values += [self.seq_i & 1, self.seq_i >> 1]
        self.table = jnp.stack([jnp.asarray(v, jnp.int32) for v in values])

    def homes(self, links):
        out = []
        for p in range(1 << len(links)):
            seq_rel = sum(b for k, (a, b) in enumerate(links) if a == "seq" and p >> k & 1)
            leaf_rel = sum(b for k, (a, b) in enumerate(links) if a == "leaf" and p >> k & 1)
            out.append((self.leaf_i ^ leaf_rel) * self.seq_n + (self.seq_i ^ seq_rel))
        return out

    def seq_homes(self):
        out = [self.seq_i]
        for bit in axis_bits("seq")[::-1]:
            out = out + [h ^ bit for h in out]
        return out


class Weight:
    def __init__(self, arrays, rows, flip):
        self.arrays = list(arrays)
        self.rows = rows
        self.flip = flip

    def source(self, place, scal, refs, block, skip, rows, cols):
        if len(self.arrays) == 1:
            return refs[0].at[pl.ds(block * self.rows + skip, rows), cols], block
        home = scal[place.at["blocks", self.flip] + block]
        return refs[block].at[pl.ds(skip, rows), cols], home

    def halves(self, place, scal, refs, buf, sems, skip=0):
        mid = buf.shape[1] // 256 * 128
        parts = (slice(0, mid), slice(mid, buf.shape[1]))
        return [
            self.copies(
                place, scal, refs, buf.at[:, part], sems.at[n], skip=skip, cols=part
            )
            for n, part in enumerate(parts)
        ]

    def copies(self, place, scal, refs, buf, sems, skip=0, cols=slice(None)):
        rows = buf.shape[0] // place.blocks
        out = []
        for block in range(place.blocks):
            src, home = self.source(place, scal, refs, block, skip, rows, cols)
            if not isinstance(home, int):
                home = pl.multiple_of(home * rows, PAD)
            else:
                home = home * rows
            out.append(pltpu.make_async_copy(src, buf.at[pl.ds(home, rows)], sems.at[block]))
        return out


def row_spot(index, rows):
    return pl.ds(pl.multiple_of(index * rows, PAD), rows)


def put_halves(place, scal, buf, own_ref, got_ref):
    half = own_ref.shape[0]
    which = scal[place.at["half"]]
    buf[row_spot(which, half), :] = own_ref[...]
    buf[row_spot(1 - which, half), :] = got_ref[...]


def fold_kernel(spot, scal, keep_ref, got_ref, next_keep, next_send):
    rows = next_keep.shape[0]
    which = scal[spot]
    mine = row_spot(which, rows)
    away = row_spot(1 - which, rows)
    next_keep[...] = keep_ref[mine, :] + got_ref[mine, :].astype(f32)
    next_send[...] = (keep_ref[away, :] + got_ref[away, :].astype(f32)).astype(bf16)


def fold(place, spot, keep, got):
    rows, cols = keep.shape
    return call(
        functools.partial(fold_kernel, place.at[spot] if isinstance(spot, str) else spot),
        "fold",
        (shape((rows // 2, cols), f32), shape((rows // 2, cols), bf16)),
        [SMEM, VMEM, VMEM],
        (place.table, keep, got),
    )


def join_kernel(spot, scal, own_ref, got_ref, out_ref):
    rows = own_ref.shape[0]
    which = scal[spot]
    out_ref[row_spot(which, rows), :] = own_ref[...]
    out_ref[row_spot(1 - which, rows), :] = got_ref[...]


def join(place, spot, own, got, deps=()):
    rows, cols = own.shape
    return call(
        functools.partial(join_kernel, place.at[spot]),
        "join",
        shape((2 * rows, cols), own.dtype),
        [SMEM, VMEM, VMEM],
        (place.table, own, got),
        deps=deps,
    )


def normed_rows(values, gain):
    inv = lax.rsqrt(jnp.mean(values * values, axis=1, keepdims=True) + eps_norm)
    return (values * inv * gain).astype(bf16)


def entry_kernel(place, scal, x_ref, gain_ref, share_ref, normed_ref):
    rows = share_ref.shape[0]
    values = x_ref[...].astype(f32)
    normed_ref[...] = normed_rows(values, gain_ref[...])
    spot = scal[place.at["half"]] * 2 + scal[place.at["quarter"]]
    share_ref[...] = x_ref[row_spot(spot, rows), :].astype(f32)


def entry(place, hidden, gain, share):
    rows, width = hidden.shape
    return call(
        functools.partial(entry_kernel, place),
        "entry",
        (shape((share, width), f32), shape((rows, width), bf16)),
        [SMEM, LOAD, VMEM],
        (place.table, hidden, gain),
        out_specs=(VMEM, STORE),
    )


def finish_norm_kernel(base_ref, keep_ref, got_ref, gain_ref, sum_ref, normed_ref):
    total = base_ref[...] + (keep_ref[...] + got_ref[...].astype(f32))
    sum_ref[...] = total
    normed_ref[...] = normed_rows(total, gain_ref[...])


def finish_norm(base, keep, got, gain):
    return call(
        finish_norm_kernel,
        "finish_norm",
        (shape(base.shape, f32), shape(base.shape, bf16)),
        [LOAD, VMEM, VMEM, VMEM],
        (base, keep, got, gain),
        out_specs=(STORE, VMEM),
    )


def finish_plain_kernel(base_ref, keep_ref, got_ref, out_ref):
    out_ref[...] = (base_ref[...] + (keep_ref[...] + got_ref[...].astype(f32))).astype(bf16)


def finish_plain(base, keep, got):
    return call(
        finish_plain_kernel, "finish_plain", shape(base.shape, bf16), [LOAD, VMEM, VMEM], (base, keep, got)
    )


def finish_back_kernel(carry_ref, keep_ref, got_ref, src_ref, gain_ref, grad_ref, low_ref, term_ref):
    dnorm = keep_ref[...] + got_ref[...].astype(f32)
    source = src_ref[...]
    inv = lax.rsqrt(jnp.mean(source * source, axis=1, keepdims=True) + eps_norm)
    term_ref[...] = jnp.sum(dnorm * source * inv, axis=0, keepdims=True)
    scaled = dnorm * gain_ref[...]
    back = jnp.mean(scaled * source, axis=1, keepdims=True)
    grad = carry_ref[...] + inv * scaled - source * (inv * inv * inv) * back
    grad_ref[...] = grad
    low_ref[...] = grad.astype(bf16)


def finish_back(carry, keep, got, source, gain):
    width = carry.shape[1]
    return call(
        finish_back_kernel,
        "finish_back",
        (shape(carry.shape, f32), shape(carry.shape, bf16), shape((1, width), f32)),
        [LOAD, VMEM, VMEM, LOAD, VMEM],
        (carry, keep, got, source, gain),
        out_specs=(STORE, VMEM, STORE),
    )


def split_rows(place, scal, total_ref, keep_ref, send_ref):
    half = keep_ref.shape[0]
    which = scal[place.at["half"]]
    keep_ref[...] = total_ref[row_spot(which, half), :]
    send_ref[...] = total_ref[row_spot(1 - which, half), :].astype(bf16)


def project_kernel(place, weight, heads, hd, parts, *refs):
    scal, refs = refs[0], refs[1:]
    x_refs, refs = refs[:parts], refs[parts:]
    bias_ref, cos_ref, sin_ref = refs[:3]
    refs = refs[3:]
    w_refs, refs = refs[: len(weight.arrays)], refs[len(weight.arrays) :]
    q_ref, kv_ref, refs = refs[0], refs[1], refs[2:]
    if parts == 2:
        x_out, refs = refs[0], refs[1:]
    buf, sems = refs
    cols = (heads + 2) * hd
    copies = weight.copies(place, scal, w_refs, buf, sems, cols=slice(0, cols))
    for copy in copies:
        copy.start()
    if parts == 2:
        put_halves(place, scal, x_out, *x_refs)
        values = x_out[...]
    else:
        values = x_refs[0][...]
    for copy in copies:
        copy.wait()
    cos_wide = cos_ref[...]
    sin_wide = sin_ref[...]
    lin = dot(values, buf[...]) + bias_ref[...]
    for h in range(heads + 1):
        part = lin[:, h * hd : (h + 1) * hd]
        turned = part * cos_wide + pltpu.roll(part, hd // 2, 1) * sin_wide
        if h < heads:
            q_ref[:, h * hd : (h + 1) * hd] = turned.astype(bf16)
        else:
            kv_ref[:, :hd] = turned.astype(bf16)
    kv_ref[:, hd:] = lin[:, (heads + 1) * hd :].astype(bf16)


def project(place, x_parts, weight, bias, cos_wide, sin_wide, heads, hd):
    rows = sum(part.shape[0] for part in x_parts)
    width = x_parts[0].shape[1]
    cols = (heads + 2) * hd
    outs = [shape((rows, heads * hd), bf16), shape((rows, 2 * hd), bf16)]
    if len(x_parts) == 2:
        outs.append(shape((rows, width), bf16))
    return call(
        functools.partial(project_kernel, place, weight, heads, hd, len(x_parts)),
        "project",
        tuple(outs),
        [SMEM] + [LOAD if len(x_parts) == 1 else VMEM] * len(x_parts) + [VMEM, LOAD, LOAD]
        + [ANY] * len(weight.arrays),
        (place.table, *x_parts, bias, cos_wide, sin_wide, *weight.arrays),
        [pltpu.VMEM((width, cols), bf16), pltpu.SemaphoreType.DMA((place.blocks,))],
        out_specs=(STORE, VMEM) + (STORE,) * (len(outs) - 2),
    )


def put_keys(place, scal, buf, kv_refs):
    rows = kv_refs[0].shape[0]
    for n, ref in enumerate(kv_refs):
        buf[row_spot(scal[place.at["seq"] + n], rows), :] = ref[...]


def attend_kernel(place, weight, heads, hd, *refs):
    scal, q_ref, vis_ref, refs = refs[0], refs[1], refs[2], refs[3:]
    kv_refs, refs = refs[: place.seq_n], refs[place.seq_n :]
    w_refs, refs = refs[: len(weight.arrays)], refs[len(weight.arrays) :]
    o_ref, lse_ref, keep_ref, send_ref, kv_buf, w_buf, total_buf, sems = refs
    cols = slice((heads + 2) * hd, (2 * heads + 2) * hd)
    copies = weight.copies(place, scal, w_refs, w_buf, sems, cols=cols)
    for copy in copies:
        copy.start()
    put_keys(place, scal, kv_buf, kv_refs)
    keys = kv_buf[:, :hd]
    values = kv_buf[:, hd:]
    seen = vis_ref[...] > 0.5
    scale = 1.0 / math.sqrt(hd)
    lane = lax.broadcasted_iota(jnp.int32, lse_ref.shape, 1)
    lse_all = jnp.zeros(lse_ref.shape, f32)
    for h in range(heads):
        spot = slice(h * hd, (h + 1) * hd)
        scores = dot_right(q_ref[:, spot], keys) * scale
        scores = jnp.where(seen, scores, neg_fill)
        top = jnp.max(scores, axis=1, keepdims=True)
        expo = jnp.exp(scores - top)
        total = jnp.sum(expo, axis=1, keepdims=True)
        prob = (expo * (1.0 / total)).astype(bf16)
        o_ref[:, spot] = dot(prob, values).astype(bf16)
        lse_all = jnp.where(lane == h, top + jnp.log(total), lse_all)
    lse_ref[...] = lse_all
    flush(o_ref)
    flush(lse_ref)
    for copy in copies:
        copy.wait()
    for at, size in spans(w_buf.shape[0], 512):
        total_buf[:, at : at + size] = dot_right(o_ref[...], w_buf[at : at + size, :])
    split_rows(place, scal, total_buf, keep_ref, send_ref)


def attend(place, query, kv_parts, visible, weight, heads, hd, width):
    rows = query.shape[0]
    keys = visible.shape[1]
    half = rows // 2
    return call(
        functools.partial(attend_kernel, place, weight, heads, hd),
        "attend",
        (
            shape((rows, heads * hd), bf16),
            shape((rows, 128), f32),
            shape((half, width), f32),
            shape((half, width), bf16),
        ),
        [SMEM, LOAD, LOAD] + [VMEM] * len(kv_parts) + [ANY] * len(weight.arrays),
        (place.table, query, visible, *kv_parts, *weight.arrays),
        [
            pltpu.VMEM((keys, 2 * hd), bf16),
            pltpu.VMEM((width, heads * hd), bf16),
            pltpu.VMEM((rows, width), f32),
            pltpu.SemaphoreType.DMA((place.blocks,)),
        ],
        out_specs=(STORE, STORE, VMEM, VMEM),
    )


def attend_back_kernel(place, weight, heads, hd, *refs):
    (scal, own_ref, got_ref, q_ref, vis_ref, lse_ref, cos_ref, sin_ref), refs = refs[:8], refs[8:]
    kv_refs, refs = refs[: place.seq_n], refs[place.seq_n :]
    w_refs, refs = refs[: len(weight.arrays)], refs[len(weight.arrays) :]
    full_ref, dq_ref, keep_ref, send_ref, kv_buf, w_buf, do_buf, dkv_buf, sems = refs
    cols = slice((heads + 2) * hd, (2 * heads + 2) * hd)
    copies = weight.copies(place, scal, w_refs, w_buf, sems, cols=cols)
    for copy in copies:
        copy.start()
    put_halves(place, scal, full_ref, own_ref, got_ref)
    flush(full_ref)
    put_keys(place, scal, kv_buf, kv_refs)
    keys = kv_buf[:, :hd]
    values = kv_buf[:, hd:]
    seen = vis_ref[...] > 0.5
    cos_wide = cos_ref[...]
    sin_wide = sin_ref[...]
    scale = 1.0 / math.sqrt(hd)
    for copy in copies:
        copy.wait()
    do_buf[...] = dot(full_ref[...], w_buf[...]).astype(bf16)
    for h in range(heads):
        spot = slice(h * hd, (h + 1) * hd)
        query = q_ref[:, spot]
        dout = do_buf[:, spot]
        scores = dot_right(query, keys) * scale
        scores = jnp.where(seen, scores, neg_fill)
        prob = jnp.exp(scores - lse_ref[:, h : h + 1])
        dprob = dot_right(dout, values)
        delta = jnp.sum(prob * dprob, axis=1, keepdims=True)
        dscore = (prob * (dprob - delta)).astype(bf16)
        dquery = dot(dscore, keys) * scale
        dquery = dquery * cos_wide - pltpu.roll(dquery, hd // 2, 1) * sin_wide
        dq_ref[:, spot] = dquery.astype(bf16)
        dk_part = dot_left(dscore, query) * scale
        dv_part = dot_left(prob.astype(bf16), dout)
        if h == 0:
            dkv_buf[:, :hd] = dk_part
            dkv_buf[:, hd:] = dv_part
        else:
            dkv_buf[:, :hd] += dk_part
            dkv_buf[:, hd:] += dv_part
    rows = kv_refs[0].shape[0]
    core = scal[place.at["chip"]]
    for n in range(place.seq_n // 2):
        spot = slice(n * rows, (n + 1) * rows)
        keep_ref[spot, :] = dkv_buf[row_spot(2 * n + core, rows), :]
        send_ref[spot, :] = dkv_buf[row_spot(2 * n + 1 - core, rows), :].astype(bf16)


def attend_back(place, own, got, query, kv_parts, visible, lse, cos_wide, sin_wide, weight, heads, hd, deps=()):
    rows = query.shape[0]
    keys = visible.shape[1]
    width = own.shape[1]
    return call(
        functools.partial(attend_back_kernel, place, weight, heads, hd),
        "attend_back",
        (
            shape((rows, width), bf16),
            shape((rows, heads * hd), bf16),
            shape((keys // 2, 2 * hd), f32),
            shape((keys // 2, 2 * hd), bf16),
        ),
        [SMEM, VMEM, VMEM] + [LOAD] * (5 + len(kv_parts)) + [ANY] * len(weight.arrays),
        (place.table, own, got, query, visible, lse, cos_wide, sin_wide, *kv_parts, *weight.arrays),
        [
            pltpu.VMEM((keys, 2 * hd), bf16),
            pltpu.VMEM((width, heads * hd), bf16),
            pltpu.VMEM((rows, heads * hd), bf16),
            pltpu.VMEM((keys, 2 * hd), f32),
            pltpu.SemaphoreType.DMA((place.blocks,)),
        ],
        out_specs=(STORE, STORE, VMEM, VMEM),
        deps=deps,
    )


def lin_back_kernel(place, weight, heads, hd, *refs):
    (scal, dq_ref, dkv_ref, got_ref, cos_ref, sin_ref), refs = refs[:6], refs[6:]
    w_refs, refs = refs[: len(weight.arrays)], refs[len(weight.arrays) :]
    dlin_ref, sums_ref, keep_ref, send_ref, w_buf, total_buf, sems = refs
    cols = (heads + 2) * hd
    copies = weight.copies(place, scal, w_refs, w_buf, sems, cols=slice(0, cols))
    for copy in copies:
        copy.start()
    dkv = dkv_ref[...] + got_ref[...].astype(f32)
    dkey = dkv[:, :hd]
    dkey = dkey * cos_ref[...] - pltpu.roll(dkey, hd // 2, 1) * sin_ref[...]
    dlin_ref[:, : heads * hd] = dq_ref[...]
    dlin_ref[:, heads * hd : (heads + 1) * hd] = dkey.astype(bf16)
    dlin_ref[:, (heads + 1) * hd :] = dkv[:, hd:].astype(bf16)
    dlin = dlin_ref[...]
    sums_ref[...] = jnp.sum(dlin.astype(f32), axis=0, keepdims=True)
    flush(dlin_ref)
    for copy in copies:
        copy.wait()
    for at, size in spans(w_buf.shape[0], 512):
        total_buf[:, at : at + size] = dot_right(dlin, w_buf[at : at + size, :])
    split_rows(place, scal, total_buf, keep_ref, send_ref)


def lin_back(place, dquery, dkv, got, cos_wide, sin_wide, weight, heads, hd, width, deps=()):
    rows = dquery.shape[0]
    cols = (heads + 2) * hd
    return call(
        functools.partial(lin_back_kernel, place, weight, heads, hd),
        "lin_back",
        (
            shape((rows, cols), bf16),
            shape((1, cols), f32),
            shape((rows // 2, width), f32),
            shape((rows // 2, width), bf16),
        ),
        [SMEM, LOAD, VMEM, VMEM, LOAD, LOAD] + [ANY] * len(weight.arrays),
        (place.table, dquery, dkv, got, cos_wide, sin_wide, *weight.arrays),
        [
            pltpu.VMEM((width, cols), bf16),
            pltpu.VMEM((rows, width), f32),
            pltpu.SemaphoreType.DMA((place.blocks,)),
        ],
        out_specs=(STORE, STORE, VMEM, VMEM),
        deps=deps,
    )


class Paired:
    def __init__(self, gate, up, rows):
        self.parts = (Weight(gate, rows, False), Weight(up, rows, False))
        self.arrays = list(gate) + list(up)
        self.rows = rows

    def halves(self, place, scal, refs, buf, sems, skip=0):
        count = len(self.arrays) // 2
        if skip:
            return self.parts[1].halves(place, scal, refs[count:], buf, sems)
        return self.parts[0].halves(place, scal, refs[:count], buf, sems)


def start_all(copies):
    for copy in copies:
        copy.start()


def wait_all(copies):
    for copy in copies:
        copy.wait()


def mlp_kernel(place, w_in, w_down, *refs):
    (scal, own_ref, got_ref), refs = refs[:3], refs[3:]
    in_refs, refs = refs[: len(w_in.arrays)], refs[len(w_in.arrays) :]
    down_refs, refs = refs[: len(w_down.arrays)], refs[len(w_down.arrays) :]
    (
        full_ref, gate_ref, up_ref, mix_ref, keep_ref, send_ref,
        gate_buf, up_buf, down_buf, total_buf, gate_sems, up_sems, down_sems,
    ) = refs
    shard = gate_buf.shape[0] // place.blocks
    gate_copies = w_in.halves(place, scal, in_refs, gate_buf, gate_sems)
    up_copies = w_in.halves(place, scal, in_refs, up_buf, up_sems, skip=shard)
    down_copies = w_down.halves(place, scal, down_refs, down_buf, down_sems)
    start_all(gate_copies[0])
    put_halves(place, scal, full_ref, own_ref, got_ref)
    flush(full_ref)
    values = full_ref[...]
    units = gate_buf.shape[1]
    mid = units // 256 * 128
    parts = (spans(mid, 384), [(mid + at, size) for at, size in spans(units - mid, 384)])
    start_all(gate_copies[1])
    wait_all(gate_copies[0])
    for n in range(2):
        start_all(up_copies[n])
        for at, size in parts[n]:
            gate_ref[:, at : at + size] = dot(values, gate_buf[:, at : at + size]).astype(bf16)
        wait_all(gate_copies[1] if n == 0 else up_copies[0])
    flush(gate_ref)
    for n in range(2):
        start_all(down_copies[n])
        for at, size in parts[n]:
            spot = slice(at, at + size)
            up = dot(values, up_buf[:, spot])
            gate = gate_ref[:, spot].astype(f32)
            up_ref[:, spot] = up.astype(bf16)
            mix_ref[:, spot] = (gate * jax.nn.sigmoid(gate) * up).astype(bf16)
        wait_all(up_copies[1] if n == 0 else down_copies[0] + down_copies[1])
    flush(up_ref)
    flush(mix_ref)
    mixed = mix_ref[...]
    for at, size in spans(down_buf.shape[0], 512):
        total_buf[:, at : at + size] = dot_right(mixed, down_buf[at : at + size, :])
    split_rows(place, scal, total_buf, keep_ref, send_ref)


def mlp(place, own, got, w_in, w_down):
    half, width = own.shape
    rows = 2 * half
    units = w_in.arrays[0].shape[1]
    dma = pltpu.SemaphoreType.DMA((2, place.blocks))
    return call(
        functools.partial(mlp_kernel, place, w_in, w_down),
        "mlp",
        (
            shape((rows, width), bf16),
            shape((rows, units), bf16),
            shape((rows, units), bf16),
            shape((rows, units), bf16),
            shape((half, width), f32),
            shape((half, width), bf16),
        ),
        [SMEM, VMEM, VMEM] + [ANY] * (len(w_in.arrays) + len(w_down.arrays)),
        (place.table, own, got, *w_in.arrays, *w_down.arrays),
        [
            pltpu.VMEM((width, units), bf16),
            pltpu.VMEM((width, units), bf16),
            pltpu.VMEM((width, units), bf16),
            pltpu.VMEM((rows, width), f32),
            dma,
            dma,
            dma,
        ],
        out_specs=(STORE, STORE, STORE, STORE, VMEM, VMEM),
    )


def mlp_back_kernel(place, w_in, w_down, parts, *refs):
    scal, refs = refs[0], refs[1:]
    d_refs, refs = refs[:parts], refs[parts:]
    gate_ref, up_ref, refs = refs[0], refs[1], refs[2:]
    in_refs, refs = refs[: len(w_in.arrays)], refs[len(w_in.arrays) :]
    down_refs, refs = refs[: len(w_down.arrays)], refs[len(w_down.arrays) :]
    dgate_ref, dup_ref, keep_ref, send_ref, refs = refs[0], refs[1], refs[2], refs[3], refs[4:]
    if parts == 2:
        full_ref, refs = refs[0], refs[1:]
    gate_buf, up_buf, down_buf, total_buf, gate_sems, up_sems, down_sems = refs
    shard = gate_buf.shape[0] // place.blocks
    gate_copies = w_in.halves(place, scal, in_refs, gate_buf, gate_sems)
    up_copies = w_in.halves(place, scal, in_refs, up_buf, up_sems, skip=shard)
    down_copies = w_down.halves(place, scal, down_refs, down_buf, down_sems)
    start_all(down_copies[0])
    if parts == 2:
        put_halves(place, scal, full_ref, *d_refs)
        flush(full_ref)
        values = full_ref[...]
    else:
        values = d_refs[0][...]
    units = gate_buf.shape[1]
    mid = units // 256 * 128
    cuts = (spans(mid, 384), [(mid + at, size) for at, size in spans(units - mid, 384)])
    start_all(down_copies[1])
    wait_all(down_copies[0])
    for n in range(2):
        start_all(gate_copies[n])
        for at, size in cuts[n]:
            spot = slice(at, at + size)
            dmixed = dot(values, down_buf[:, spot])
            gate = gate_ref[:, spot].astype(f32)
            up = up_ref[:, spot].astype(f32)
            sig = jax.nn.sigmoid(gate)
            dgate_ref[:, spot] = (dmixed * up * sig * (1.0 + gate * (1.0 - sig))).astype(bf16)
            dup_ref[:, spot] = (dmixed * (gate * sig)).astype(bf16)
        if n == 0:
            wait_all(down_copies[1])
    start_all(up_copies[0] + up_copies[1])
    flush(dgate_ref)
    flush(dup_ref)
    wait_all(gate_copies[0] + gate_copies[1])
    dgate = dgate_ref[...]
    dup = dup_ref[...]
    for at, size in spans(gate_buf.shape[0], 512):
        spot = slice(at, at + size)
        total_buf[:, spot] = dot_right(dgate, gate_buf[spot, :])
    wait_all(up_copies[0] + up_copies[1])
    for at, size in spans(gate_buf.shape[0], 512):
        spot = slice(at, at + size)
        total_buf[:, spot] += dot_right(dup, up_buf[spot, :])
    split_rows(place, scal, total_buf, keep_ref, send_ref)


def mlp_back(place, d_parts, gate, up, w_in, w_down, deps=()):
    rows = sum(part.shape[0] for part in d_parts)
    width = d_parts[0].shape[1]
    half = rows // 2
    units = gate.shape[1]
    outs = [
        shape((rows, units), bf16),
        shape((rows, units), bf16),
        shape((half, width), f32),
        shape((half, width), bf16),
    ]
    if len(d_parts) == 2:
        outs.append(shape((rows, width), bf16))
    dma = pltpu.SemaphoreType.DMA((2, place.blocks))
    return call(
        functools.partial(mlp_back_kernel, place, w_in, w_down, len(d_parts)),
        "mlp_back",
        tuple(outs),
        [SMEM] + [LOAD if len(d_parts) == 1 else VMEM] * len(d_parts) + [LOAD, LOAD]
        + [ANY] * (len(w_in.arrays) + len(w_down.arrays)),
        (place.table, *d_parts, gate, up, *w_in.arrays, *w_down.arrays),
        [
            pltpu.VMEM((width, units), bf16),
            pltpu.VMEM((width, units), bf16),
            pltpu.VMEM((width, units), bf16),
            pltpu.VMEM((rows, width), f32),
            dma,
            dma,
            dma,
        ],
        out_specs=(STORE, STORE, VMEM, VMEM) + (STORE,) * (len(outs) - 4),
        deps=deps,
    )


def weight_grad_kernel(place, micro_n, pairs, homes, *refs):
    scal, refs = refs[0], refs[1:]
    left_refs = [refs[p * micro_n : (p + 1) * micro_n] for p in range(pairs)]
    refs = refs[pairs * micro_n :]
    right_refs = [refs[p * micro_n : (p + 1) * micro_n] for p in range(pairs)]
    refs = refs[pairs * micro_n :]
    outs = 1 if homes is None else 2
    out_refs, refs = refs[:outs], refs[outs:]
    bufs, sems = refs[:pairs], refs[pairs]
    shard = bufs[0].shape[0] // place.blocks
    half = place.blocks // 2
    copies = []
    at_col = 0
    for p in range(pairs):
        buf = bufs[p]
        cols = buf.shape[1]
        ready = 0
        for at, size in spans(buf.shape[0], 256):
            spot = slice(at, at + size)
            total = None
            for left, right in zip(left_refs[p], right_refs[p]):
                part = dot_left(left[:, spot], right[...])
                total = part if total is None else total + part
            buf[spot, :] = total.astype(bf16)
            while homes is None and (ready + 1) * shard <= at + size:
                src = buf.at[pl.ds(ready * shard, shard)]
                dst = out_refs[0].at[pl.ds(ready * shard, shard), pl.ds(at_col, cols)]
                copies.append(pltpu.make_async_copy(src, dst, sems.at[len(copies)]))
                copies[-1].start()
                ready += 1
        if homes is not None:
            for block in list(range(half, place.blocks)) + list(range(half)):
                home = scal[homes + block]
                src = buf.at[pl.ds(pl.multiple_of(home * shard, PAD), shard)]
                out = out_refs[block // half]
                dst = out.at[pl.ds(block % half * shard, shard), pl.ds(at_col, cols)]
                copies.append(pltpu.make_async_copy(src, dst, sems.at[len(copies)]))
                copies[-1].start()
        at_col += cols
    for copy in copies:
        copy.wait()


def weight_grad(place, pairs, homes, deps=()):
    micro_n = len(pairs[0][0])
    rows, width = pairs[0][0][0].shape
    cols = [rights[0].shape[1] for _, rights in pairs]
    if homes is None:
        outs = (shape((width, sum(cols)), bf16),)
    else:
        outs = (shape((width // 2, sum(cols)), bf16),) * 2
    lefts = [a for left, _ in pairs for a in left]
    rights = [a for _, right in pairs for a in right]
    copies = place.blocks * len(pairs)
    return call(
        functools.partial(weight_grad_kernel, place, micro_n, len(pairs), homes),
        "weight_grad" if sum(cols) > width else "weight_grad_small",
        outs,
        [SMEM] + [LOAD] * (len(lefts) + len(rights)),
        (place.table, *lefts, *rights),
        [pltpu.VMEM((width, c), bf16) for c in cols] + [pltpu.SemaphoreType.DMA((copies,))],
        out_specs=tuple(HBM for _ in outs),
        deps=deps,
    )


def fold_rows_kernel(keep_lo, keep_hi, got_lo, got_hi, keep_ref, send_ref):
    keep_ref[...] = (keep_lo[...].astype(f32) + got_lo[...].astype(f32)).astype(bf16)
    send_ref[...] = (keep_hi[...].astype(f32) + got_hi[...].astype(f32)).astype(bf16)


def fold_rows(keep, got):
    rows, cols = keep.shape
    half = rows // 2
    tile = half
    for count in (8, 4, 3, 2):
        if half % (count * PAD) == 0:
            tile = half // count
            break
    steps = half // tile
    low = pl.BlockSpec((tile, cols), lambda i: (i, 0))
    high = pl.BlockSpec((tile, cols), lambda i: (i + steps, 0))
    return call(
        fold_rows_kernel,
        "fold_rows",
        (shape((half, cols), bf16), shape((half, cols), bf16)),
        [low, high, low, high],
        (keep, keep, got, got),
        out_specs=(low, low),
        grid=(steps,),
    )


def combine_kernel(keep_ref, got_ref, out_ref):
    out_ref[...] = (keep_ref[...].astype(f32) + got_ref[...].astype(f32)).astype(bf16)


def combine(keep, got):
    return call(
        combine_kernel,
        "combine",
        shape(keep.shape, bf16),
        [LOAD, LOAD],
        (keep, got),
        out_specs=(STORE,),
    )


def finish_grads_kernel(counts, *refs):
    out_ref = refs[-1]
    cols = out_ref.shape[1]
    layer = pl.program_id(0)
    at = 0
    for n, count in enumerate(counts):

        @pl.when(layer == n)
        def write(parts=refs[at : at + count]):
            out_ref[...] = sum(part[...].astype(f32) for part in parts)[:, :cols]

        at += count


def finish_grads(layers, cols, window):
    rows = layers[0][0][0].shape[0]
    specs, operands = [], []
    for arrays, spot in layers:
        for array in arrays:
            specs.append(pl.BlockSpec((rows, window), lambda i, spot=spot: (0, spot)))
            operands.append(array)
    return call(
        functools.partial(finish_grads_kernel, [len(arrays) for arrays, _ in layers]),
        "finish_grads",
        shape((len(layers), rows, cols), f32),
        specs,
        tuple(operands),
        out_specs=(pl.BlockSpec((pl.Squeezed(), rows, cols), lambda i: (i, 0, 0)),),
        grid=(len(layers),),
    )


def pack_attn_kernel(place, group_at, smalls, *refs):
    scal, q_ref, k_ref, v_ref, o_ref = refs[:5]
    small_refs, out_ref = refs[5:-1], refs[-1]
    rows, cols = q_ref.shape
    hd = k_ref.shape[1] // 2
    high = scal[group_at] == 1
    pick = lambda ref: jnp.where(high, ref[:, hd:], ref[:, :hd])
    out_ref[:rows, :cols] = q_ref[...]
    out_ref[:rows, cols : cols + hd] = pick(k_ref)
    out_ref[:rows, cols + hd : cols + 2 * hd] = pick(v_ref)
    out_ref[:rows, cols + 2 * hd :] = o_ref[...]
    if smalls:
        gain1, gain2, bias_q, bias_k, bias_v = small_refs
        layers, n = gain1.shape
        heads, bias_n = bias_q.shape[1:]
        out_ref[rows:, :] = jnp.zeros((2 * PAD, out_ref.shape[1]), bf16)
        at = rows
        for block in (gain1[...], gain2[...]):
            out_ref[at : at + layers, :n] = block
            at += layers
        for layer in range(layers):
            out_ref[at : at + heads, :bias_n] = bias_q[layer]
            at += heads
            for ref in (bias_k, bias_v):
                both = ref[layer].astype(f32)
                out_ref[at : at + 1, :bias_n] = jnp.where(high, both[1:], both[:1]).astype(bf16)
                at += 1


def pack_attn(place, layer, w_query, w_key, w_value, w_out_t, smalls):
    _, rows, cols = w_query.shape
    kv_cols = w_key.shape[2]
    block = lambda c: pl.BlockSpec((pl.Squeezed(), rows, c), lambda i: (layer, 0, 0))
    whole = lambda a: pl.BlockSpec(a.shape, lambda i: (0,) * a.ndim)
    out = (rows + (2 * PAD if smalls else 0), 2 * cols + kv_cols)
    return call(
        functools.partial(pack_attn_kernel, place, place.at["quarter"], bool(smalls)),
        "pack",
        shape(out, bf16),
        [SMEM, block(cols), block(kv_cols), block(kv_cols), block(cols)]
        + [whole(a) for a in smalls],
        (place.table, w_query, w_key, w_value, w_out_t, *smalls),
        out_specs=(pl.BlockSpec(out, lambda i: (0, 0)),),
        grid=(1,),
    )


def pack_wide_kernel(*refs):
    out_ref = refs[-1]
    at = 0
    for ref in refs[:-1]:
        rows, cols = ref.shape
        spot = slice(at, at + rows)
        if out_ref.shape[1] > cols:
            tail = cols // 128 * 128
            out_ref[spot, tail:] = jnp.zeros((rows, out_ref.shape[1] - tail), bf16)
        out_ref[spot, :cols] = ref[...]
        at += rows


def pack_wide(layer, arrays, units):
    _, rows, cols = arrays[0].shape
    block = pl.BlockSpec((pl.Squeezed(), rows, cols), lambda i: (layer, 0, 0))
    out = (rows * len(arrays), units)
    return call(
        pack_wide_kernel,
        "pack",
        shape(out, bf16),
        [block] * len(arrays),
        tuple(arrays),
        out_specs=(pl.BlockSpec(out, lambda i: (0, 0)),),
        grid=(1,),
    )


def unpack_kernel(place, weight, shard, heads, bias_n, layers, *refs):
    scal, refs = refs[0], refs[1:]
    w_refs, refs = refs[: len(weight.arrays)], refs[len(weight.arrays) :]
    outs, buf, sems = refs[:-2], refs[-2], refs[-1]
    copies = weight.copies(place, scal, w_refs, buf, sems, skip=shard, cols=slice(0, buf.shape[1]))
    for copy in copies:
        copy.start()
    for copy in copies:
        copy.wait()
    for block in range(place.blocks):
        part = buf[block * 2 * PAD : (block + 1) * 2 * PAD, :].astype(f32)
        at = 0
        for n in range(2 * layers):
            outs[n][:, block * shard : (block + 1) * shard] = part[at : at + 1, :shard]
            at += 1
        for layer in range(layers):
            for h in range(heads + 2):
                spot = h * bias_n * place.blocks + block * bias_n
                outs[2 * layers + layer][:, spot : spot + bias_n] = part[at : at + 1, :bias_n]
                at += 1


def unpack(place, weight, shard, heads, bias_n, layers, width):
    cols = (heads + 2) * bias_n * place.blocks
    return call(
        functools.partial(unpack_kernel, place, weight, shard, heads, bias_n, layers),
        "unpack",
        (shape((1, width), f32),) * (2 * layers) + (shape((1, cols), f32),) * layers,
        [SMEM] + [ANY] * len(weight.arrays),
        (place.table, *weight.arrays),
        [
            pltpu.VMEM((place.blocks * 2 * PAD, 256), bf16),
            pltpu.SemaphoreType.DMA((place.blocks,)),
        ],
    )


def hold_kernel(src_ref, out_ref):
    out_ref[...] = src_ref[...]


def hold(array):
    return call(hold_kernel, "hold", shape(array.shape, array.dtype), [VMEM], (array,))


def touch_kernel(*refs):
    refs[-1][...] = jnp.zeros(refs[-1].shape, f32)


def touch(arrays):
    call(touch_kernel, "touch", shape((8, 128), f32), [HBM] * len(arrays), tuple(arrays))


def small_kernel(place, layers, trees, hd, *refs):
    scal, out_ref = refs[0], refs[-1]
    refs = refs[1:-1]
    count = layers * trees
    gains1, gains2, sums = refs[:count], refs[count : 2 * count], refs[2 * count :]
    half, quarter = scal[place.at["half"]], scal[place.at["quarter"]]
    out_ref[...] = jnp.zeros(out_ref.shape, f32)
    width = out_ref.shape[1]
    for layer in range(layers):
        part = slice(layer * trees, (layer + 1) * trees)
        total = lambda group: sum(ref[...] for ref in group[part])
        out_ref[layer : layer + 1, :] = total(gains1)
        out_ref[layers + layer : layers + layer + 1, :] = total(gains2)
        row = total(sums)
        q_cols = row.shape[1] - 2 * hd
        at = 2 * layers + layer
        for n in range(width // q_cols):
            mine = quarter * 2 + half == n
            out_ref[at : at + 1, n * q_cols : (n + 1) * q_cols] = jnp.where(
                mine, row[:, :q_cols], 0.0
            )
        at += layers
        for n in range(2):
            for kind in range(2):
                spot = (2 * kind + n) * hd
                start = q_cols + kind * hd
                out_ref[at : at + 1, spot : spot + hd] = jnp.where(
                    quarter == n, row[:, start : start + hd], 0.0
                )


def add_kernel(left_ref, right_ref, out_ref):
    out_ref[...] = left_ref[...] + right_ref[...]


def tree_tables(parent_row):
    block_ids = jnp.arange(NBLK, dtype=jnp.int32)
    step_up = (block_ids[None, :] == parent_row[:, None]).astype(jnp.int32)
    reach_tab = jnp.eye(NBLK, dtype=jnp.int32) + step_up
    for repeat_idx in range(max(1, (NBLK - 1).bit_length())):
        reach_tab = (jnp.dot(reach_tab, reach_tab) > 0).astype(jnp.int32)
    depth_tab = jnp.sum(reach_tab, axis=1) - 1
    return (reach_tab, depth_tab)


def geometry(parent_row, seq_index, rows_dev):
    reach_tab, depth_tab = tree_tables(parent_row)
    token_idx = seq_index * rows_dev + jnp.arange(rows_dev, dtype=jnp.int32)
    key_idx = jnp.arange(NBLK * BLK, dtype=jnp.int32)
    block_ids = jnp.arange(NBLK, dtype=jnp.int32)
    query_hot = (token_idx[:, None] // BLK == block_ids[None, :]).astype(f32)
    key_hot = (key_idx[:, None] // BLK == block_ids[None, :]).astype(f32)
    link_rows = jnp.dot(query_hot, reach_tab.astype(f32), precision=lax.Precision.HIGHEST)
    link_tab = jnp.dot(link_rows, key_hot.T, precision=lax.Precision.HIGHEST)
    visible = (link_tab > 0.5) & (key_idx[None, :] <= token_idx[:, None])
    depth_rows = jnp.dot(query_hot, depth_tab.astype(f32), precision=lax.Precision.HIGHEST)
    position = BLK * depth_rows + (token_idx % BLK).astype(f32)
    return (position, visible.astype(f32))


def wide_angles(position, head_dim):
    freq_idx = jnp.arange(head_dim // 2, dtype=f32)
    inv_freq = rope_base ** (-2.0 * freq_idx / head_dim)
    turn_val = position[:, None] * inv_freq[None, :]
    cosine, sine_val = (jnp.cos(turn_val), jnp.sin(turn_val))
    return (
        jnp.concatenate([cosine, cosine], axis=1),
        jnp.concatenate([-sine_val, sine_val], axis=1),
    )


def body(
    hidden_in,
    parents,
    cotangent,
    attn_gain,
    w_query,
    b_query,
    w_key,
    b_key,
    w_value,
    b_value,
    w_out,
    mlp_gain,
    w_gate,
    w_up,
    w_down,
):
    place = Place()
    both = ("leaf", "seq")
    micro_n, rows_dev, width = hidden_in.shape
    layer_n, shard = w_query.shape[:2]
    heads, bias_cols = b_query.shape[1:]
    kv_heads = b_key.shape[1]
    hd = w_key.shape[2] // kv_heads
    tensor_n = lax.axis_size("tensor")
    units = -(-w_gate.shape[2] // 256) * 256
    blocks = place.blocks
    assert tensor_n == 4 and kv_heads == 2 and layer_n == 2 and place.seq_n == 4
    kv_group = place.tensor_i >> 1
    q_cols = heads * hd
    qkv_cols = q_cols + 2 * hd
    pack_cols = qkv_cols + q_cols
    share = rows_dev // tensor_n

    order = ORDER[0] = Order()
    w_down_t = jnp.swapaxes(w_down, 1, 2)
    w_out_t = jnp.swapaxes(w_out, 1, 2)
    smalls = (attn_gain, mlp_gain, b_query, b_key, b_value)
    whole = lambda own: [lax.all_gather(own, both, axis=0, tiled=True)]
    links = fabric(True)
    own = pack_attn(place, 0, w_query, w_key, w_value, w_out_t, smalls)
    pieces = [own]
    for n, (axis, bit) in enumerate(links):
        pieces = pieces + [swap(piece, axis, bit) for piece in pieces]
        if n == len(links) - 2:
            touch([pieces[1]] + pieces[2:3])
    attn0 = Weight(pieces, shard, True)
    wide = lambda array, layer=0: pack_wide(layer, (array,), units)
    (a_axis, a_bit), (b_axis, b_bit), *others = fabric(False)
    own_gate, own_up = wide(w_gate), wide(w_up)
    side_up = swap(own_up, b_axis, b_bit)
    side_gate = swap(own_gate, b_axis, b_bit)
    *gain_rows, bias0, bias1 = unpack(place, attn0, shard, heads, bias_cols, layer_n, width)

    def rest_of_in():
        far_up = [side_up, swap(side_up, a_axis, a_bit)]
        gate = [own_gate, swap(wide(w_gate), a_axis, a_bit)]
        up = [own_up, swap(wide(w_up), a_axis, a_bit)]
        gate = gate + [side_gate, swap(gate[1], b_axis, b_bit)]
        up = up + far_up
        for axis, bit in others:
            gate = gate + [swap(piece, axis, bit) for piece in gate]
            up = up + [swap(piece, axis, bit) for piece in up]
        return gate, up

    def second_layer():
        attn = whole(pack_attn(place, 1, w_query, w_key, w_value, w_out_t, ()))
        down = whole(wide(w_down_t, 1))
        both_in = whole(pack_wide(1, (w_gate, w_up), units))
        return attn, both_in, down

    weights = [
        (attn0, None, None, bias0, gain_rows[0], gain_rows[2]),
        (None, None, None, bias1, gain_rows[1], gain_rows[3]),
    ]

    tables = []
    for micro in range(micro_n):
        position, visible = geometry(parents[micro], place.seq_i, rows_dev)
        tables.append(wide_angles(position, hd) + (visible,))

    spot = (place.at["half"], place.at["quarter"])
    quarter = place.table[spot[0]] * 2 + place.table[spot[1]]
    arrive = {(0, "attn"): 40.0, (1, "attn"): 170.0, (1, "mlp"): 260.0}
    finished = {}
    kept, slots, grads, settled, marks = {}, {}, {}, {}, set()
    finals, tails = [None] * micro_n, [None] * micro_n

    def scatter(keep, send, at):
        got = swap(send, "tensor", 1)
        at = yield "fold", order.link("z1", "z", at), 0
        keep, send = fold(place, "quarter", keep, got)
        got = swap(send, "tensor", 2)
        return keep, got, order.link("z2", "z", at)

    def gather(own, at):
        got = swap(own, "tensor", 2)
        at = yield "join", order.link("z2", "z", at), 0
        own = join(place, "quarter", own, got)
        got = swap(own, "tensor", 1)
        return own, got, order.link("z1", "z", at)

    def last_rows(micro, middle, keep, send):
        passed = lambda key: (lambda: 0.0 if key in marks else None)
        yield "hold", passed(("attend_back", 1, micro)), 0
        got = swap(hold(send), "tensor", 1)
        at = order.link("z1", "z", order.now)
        at = yield "fold", at, 1
        keep, send = fold(place, "quarter", keep, got)
        got = swap(send, "tensor", 2)
        at = order.link("z2", "z", at)
        at = yield "finish_plain", at, 1
        low = finish_plain(middle, keep, got)
        yield "hold", passed(("attend_back", 0, micro)), 0
        low = hold(low)
        at = order.now
        own, got, at = yield from gather(low, at)
        yield "join", at, 3
        finals[micro] = join(place, "half", own, got)

    def tree(micro):
        cos_wide, sin_wide, visible = tables[micro]
        at = yield "entry", 20.0, 1
        state, normed = entry(place, hidden_in[micro], weights[0][4], share)
        parts = (normed,)
        for layer in range(layer_n):
            bias, gain1, gain2 = weights[layer][3:]
            ready = lambda at=at, layer=layer: (
                max(at, arrive[layer, "attn"]) if layer == 0 or layer in settled else None
            )
            at = yield "project", ready, 2
            w_attn = settled[layer][0] if layer in settled else attn0
            outs = project(place, parts, w_attn, bias, cos_wide, sin_wide, heads, hd)
            marks.add(("project", layer, micro))
            query, kv_own = outs[:2]
            normed = outs[2] if len(outs) == 3 else parts[0]
            kv_parts = [kv_own]
            for bit in axis_bits("seq")[::-1]:
                kv_parts = kv_parts + [swap(part, "seq", bit) for part in kv_parts]
            at = yield "attend", order.link("kv", "kv", at) + 2.0, 2
            attended, lse, keep, send = attend(
                place, query, kv_parts, visible, w_attn, heads, hd, width
            )
            keep, got, at = yield from scatter(keep, send, at)
            at = yield "finish_norm", at, 0
            middle, low = finish_norm(state, keep, got, gain2)
            own, got, at = yield from gather(low, at)
            ready = lambda at=at, layer=layer: (
                max(at, arrive[layer, "mlp"]) if layer or 0 in settled else None
            )
            at = yield "mlp", ready, 2 + 0.1 * micro
            w_in, w_dn = settled[layer][1:]
            normed_mlp, gate, up, mixed, keep, send = mlp(place, own, got, w_in, w_dn)
            kept[layer, micro] = (
                state, normed, query, kv_parts, lse, attended,
                middle, normed_mlp, gate, up, mixed,
            )
            if layer < layer_n - 1:
                keep, got, at = yield from scatter(keep, send, at)
                at = yield "finish_norm", at, 0
                state, low = finish_norm(middle, keep, got, weights[layer + 1][4])
                own, got, at = yield from gather(low, at)
                parts = (own, got)
            else:
                more.append(last_rows(micro, middle, keep, send))
        carry = lax.dynamic_slice_in_dim(cotangent[micro], quarter * share, share, 0).astype(f32)
        downs = (cotangent[micro],)
        for layer in reversed(range(layer_n)):
            if layer == 0:
                order.scale = 1
            bias, gain1, gain2 = weights[layer][3:]
            w_attn, w_in, w_dn = settled[layer]
            (
                state, normed, query, kv_parts, lse, attended,
                middle, normed_mlp, gate, up, mixed,
            ) = kept[layer, micro]
            at = yield "mlp_back", at, 1.5 + 0.1 * micro
            outs = mlp_back(place, downs, gate, up, w_in, w_dn)
            dgate, dup, keep, send = outs[:4]
            full_down = outs[4] if len(outs) == 5 else downs[0]
            slots[layer, micro, "mlp"] = (full_down, dgate, dup)
            marks.add(("mlp_back", layer, micro))
            keep, got, at = yield from scatter(keep, send, at)
            at = yield "finish_back", at, 0
            mid, low, term2 = finish_back(carry, keep, got, middle, gain2)
            own, got, at = yield from gather(low, at)
            at = yield "attend_back", at, 2
            full_out, dquery, keep, send = attend_back(
                place, own, got, query, kv_parts, visible, lse, cos_wide, sin_wide,
                w_attn, heads, hd,
            )
            marks.add(("attend_back", layer, micro))
            slots[layer, micro, "out"] = (full_out,)
            got = swap(send, "seq", 1)
            at = yield "fold", order.link("core", "core", at), 0
            keep, send = fold(place, place.at["chip"] + 1, keep, got)
            got = swap(send, "seq", 2)
            marks.add(("kv", layer, micro))
            at = yield "lin_back", order.link("kv", "kv", at), 1
            dlin, sums, keep, send = lin_back(
                place, dquery, keep, got, cos_wide, sin_wide, w_attn, heads, hd, width
            )
            slots[layer, micro, "lin"] = (dlin,)
            keep, got, at = yield from scatter(keep, send, at)
            at = yield "finish_back", at, 0
            carry, low, term1 = finish_back(mid, keep, got, state, gain1)
            slots[layer, micro, "small"] = (term1, term2, sums)
            own, got, at = yield from gather(low, at)
            downs = (own, got)
        if micro == micro_n - 1:
            marks.add("end")
        yield "join", at, 1
        late = grads[0, "gate"] if micro == micro_n - 1 else ()
        tails[micro] = join(place, "half", *downs, deps=late)

    def reduce_links(layer, name, keep, send, flip, at):
        links = fabric(not flip)[:-1] + fabric(flip)[-1:]
        axis, bit = links[-1]
        got = swap(send, axis, bit)
        at = order.link("core_w", "core", at)
        for n, (axis, bit) in enumerate(links[:-1][::-1]):
            after = ("kv", layer, micro_n - 1)
            ready = lambda at=at, axis=axis: (
                max(at, order.free.get(axis, 0.0) - 4.0)
                if axis != "seq" or after in marks
                else None
            )
            at = yield "fold_rows", ready, 1
            keep, send = fold_rows(keep, got)
            got = swap(send, axis, bit)
            kind = ("row2" if n == 0 else "row1") + ("" if keep.shape[1] > width else "_small")
            at = order.link(kind, axis, at)
        if layer > 0:
            yield "combine", at, 1
            keep, got = combine(keep, got), None
        grads[layer, name] = (keep,) if got is None else (keep, got)

    def finishes():
        jobs = [
            ("gate", ("gate", 0), ("gate", 0), w_gate.shape[2], units),
            ("down", ("down", 0), ("down", 0), w_gate.shape[2], units),
            ("up", ("up", 0), ("up", 0), w_gate.shape[2], units),
            ("out", ("attn", 0), ("out", 0), q_cols, q_cols),
            ("lin", ("attn", 1), ("lin", 0), q_cols, q_cols),
        ]
        for name, (first, first_at), (second, second_at), cols, window in jobs:
            keys = ((0, first), (1, second))
            yield "finish_grads", (
                lambda keys=keys: 0.0 if all(key in grads for key in keys) and "end" in marks else None
            ), 7
            layers = [(grads[keys[0]], first_at), (grads[keys[1]], second_at)]
            finished[name] = finish_grads(layers, cols, window)

    def fillers(layer):
        trees = range(micro_n)
        saved = lambda n: [kept[layer, micro][n] for micro in trees]
        side = lambda kind, n: [slots[layer, micro, kind][n] for micro in trees]
        done = lambda kind: (
            lambda: 0.0 if all((layer, micro, kind) in slots for micro in trees) else None
        )
        near = lambda key: (lambda: 0.0 if (key, layer, micro_n - 1) in marks else None)

        def reduce_grad(name, pairs, flip, at):
            if layer == 0 and name != "up":
                deps = grads[0, "down"] if name == "attn" else ()
                (total,) = weight_grad(place, pairs, None, deps)
                grads[layer, name] = (
                    lax.psum_scatter(total, both, scatter_dimension=0, tiled=True),
                )
                return
            keep, send = weight_grad(place, pairs, place.at["grads", flip])
            more.append(reduce_links(layer, name, keep, send, flip, at))

        down = lambda: [(side("mlp", 0), saved(10))]
        gate = lambda: [(saved(7), side("mlp", 1))]
        up = lambda: [(saved(7), side("mlp", 2))]
        out = lambda: [(side("out", 0), saved(5))]
        lin = lambda: [(saved(1), side("lin", 0))]
        at = yield "weight_grad", done("mlp"), 5
        reduce_grad("down", down(), True, at)
        if layer > 0:
            at = yield "weight_grad", 0.0, 5
            reduce_grad("up", up(), True, at)
            at = yield "weight_grad_small", done("out"), 5
            reduce_grad("out", out(), True, at)
            at = yield "weight_grad", near("kv"), 3
            reduce_grad("gate", gate(), False, at)
            at = yield "weight_grad_small", done("lin"), 4
            reduce_grad("lin", lin(), True, at)
        else:
            at = yield "weight_grad", 0.0, 5
            reduce_grad("gate", gate(), False, at)
            at = yield "weight_grad", 0.0, 5
            reduce_grad("up", up(), True, at)
            at = yield "weight_grad_small", done("lin"), 0
            reduce_grad("attn", out() + lin(), False, at)

    def small_sums():
        keys = [(layer, micro, "small") for layer in range(layer_n) for micro in range(micro_n)]
        at = yield "small", (lambda: 0.0 if all(key in slots for key in keys) else None), 0.5
        parts = [slots[key][n] for n in range(3) for key in keys]
        total = call(
            functools.partial(small_kernel, place, layer_n, micro_n, hd),
            "small",
            shape((4 * layer_n, width), f32),
            [SMEM] + [LOAD] * len(parts),
            (place.table, *parts),
        )
        for axis, bit in fabric(False)[::-1] + [("tensor", 1), ("tensor", 2)]:
            got = swap(total, axis, bit)
            at = yield "add", order.link("core", "small", at), 0.5
            total = call(add_kernel, "add", shape(total.shape, f32), [VMEM, VMEM], (total, got))
        grads["small"] = total

    def arrivals():
        names = [("project", 0, micro) for micro in range(micro_n)]
        yield "pack", (lambda: 0.0 if all(name in marks for name in names) else None), 0
        gate, up = rest_of_in()
        down = whole(wide(w_down_t))
        settled[0] = (attn0, Paired(gate, up, shard), Weight(down, shard, False))
        at = order.now
        half = len(gate) // 2
        arrive[0, "mlp"] = at + 75.0
        yield "touch", at + 30.0, 1
        touch(gate[half : half + 2] + up[half : half + 1])
        yield "touch", at + 70.0, 1
        touch(gate[half + 2 :] + up[half + 1 :])
        yield "pack", at + 71.0, 1
        attn, both_in, down = second_layer()
        settled[1] = (
            Weight(attn, shard, False), Weight(both_in, 2 * shard, False), Weight(down, shard, False)
        )

    more = []
    order.run([tree(micro) for micro in range(micro_n)] + [fillers(1), fillers(0), small_sums(), arrivals(), finishes()], more)
    hidden_out = jnp.stack(finals)
    input_grad = jnp.stack(tails).astype(f32)

    names = ("gate", "up", "down", "lin", "out")
    gate_g, up_g, down_g, query_g, out_g = (finished[name] for name in names)
    key_gs, value_gs = [], []
    high = kv_group == 1
    for layer in range(layer_n):
        lin_at = q_cols if layer == 0 else 0
        parts = grads[layer, "attn" if layer == 0 else "lin"]
        cross = sum(part[:, lin_at + q_cols :].astype(f32) for part in parts)
        cross = cross + swap(cross.astype(bf16), "tensor", 1).astype(f32)
        other = swap(cross.astype(bf16), "tensor", 2).astype(f32)
        first = jnp.where(high, other, cross)
        second = jnp.where(high, cross, other)
        key_gs.append(jnp.concatenate([first[:, :hd], second[:, :hd]], axis=1))
        value_gs.append(jnp.concatenate([first[:, hd:], second[:, hd:]], axis=1))
    total = grads["small"]
    block = place.leaf_i * place.seq_n + place.seq_i
    gains = lax.dynamic_slice(total, (0, block * shard), (2 * layer_n, shard))
    cut = lambda a: lax.dynamic_slice_in_dim(a, block * bias_cols, bias_cols, a.ndim - 1)
    bq = total[2 * layer_n : 3 * layer_n].reshape(layer_n, tensor_n, heads, hd)
    bq = cut(lax.dynamic_index_in_dim(bq, place.tensor_i, 1, keepdims=False))
    kv_row = total[3 * layer_n :]
    bk = cut(kv_row[:, : 2 * hd].reshape(layer_n, 2, hd))
    bv = cut(kv_row[:, 2 * hd : 4 * hd].reshape(layer_n, 2, hd))
    return (
        hidden_out,
        input_grad,
        gains[:layer_n],
        query_g,
        bq,
        jnp.stack(key_gs),
        bk,
        jnp.stack(value_gs),
        bv,
        jnp.swapaxes(out_g, 1, 2),
        gains[layer_n:],
        gate_g,
        up_g,
        jnp.swapaxes(down_g, 1, 2),
    )


def solution(mesh):
    both = ("leaf", "seq")
    return jax.shard_map(
        body,
        mesh=mesh,
        in_specs=(
            P("leaf", "seq", None),
            P("leaf", None),
            P("leaf", "seq", None),
            P(None, both),
            P(None, both, "tensor"),
            P(None, "tensor", both),
            P(None, both, None),
            P(None, None, both),
            P(None, both, None),
            P(None, None, both),
            P(None, "tensor", both),
            P(None, both),
            P(None, both, "tensor"),
            P(None, both, "tensor"),
            P(None, "tensor", both),
        ),
        out_specs=(
            P("leaf", "seq", None),
            P("leaf", "seq", None),
            P(None, both),
            P(None, both, "tensor"),
            P(None, "tensor", both),
            P(None, both, None),
            P(None, None, both),
            P(None, both, None),
            P(None, None, both),
            P(None, "tensor", both),
            P(None, both),
            P(None, both, "tensor"),
            P(None, both, "tensor"),
            P(None, "tensor", both),
        ),
        check_vma=False,
    )
```

```python
import functools
import math

import jax
import jax.numpy as jnp
from jax import lax
from jax.experimental import pallas as pl
from jax.experimental.pallas import tpu as pltpu
from jax.sharding import PartitionSpec as P

BLK = 128
NBLK = 8
PAD = 16
COST = 16
TIMES = {
    "entry": 2.5,
    "mlp": 14,
    "mlp_back": 15,
    "attend": 5,
    "attend_back": 7.5,
    "lin_back": 4.5,
    "project": 4.2,
    "weight_grad": 9,
    "fold_rows": 3,
    "weight_grad_small": 4,
    "fold": 1.3,
    "join": 1.2,
    "add": 1.0,
    "finish_grads": 3,
}
START = 1.5
LINKS = {"z1": 11.0, "z2": 12.0, "kv": 6.5, "core": 3.0, "core_w": 9.0, "row2": 46, "row1": 25, "hop": 3.0,
         "row2_small": 21.0, "row1_small": 12.0}


def cost(name):
    return pl.CostEstimate(
        flops=int(TIMES.get(name, 2) * ORDER[0].scale * 1.15e9), bytes_accessed=1000, transcendentals=0
    )


class Order:
    def __init__(self):
        self.last = None
        self.now = 0.0
        self.free = {}
        self.scale = COST

    def link(self, kind, wire, at):
        begin = max(at, self.free.get(wire, 0.0))
        end = begin + LINKS[kind]
        self.free[wire] = end - 2.0
        self.now += START
        return end

    def took(self, outs):
        self.last = min(outs, key=lambda a: math.prod(a.shape))

    def run(self, tasks, more):
        waiting = [[task, next(task)] for task in tasks]
        while waiting or more:
            while more:
                task = more.pop()
                waiting.append([task, next(task)])
            ready = []
            for entry_ in waiting:
                name, when, rank = entry_[1]
                when = when() if callable(when) else when
                if when is not None:
                    ready.append((entry_, name, when, rank))
            soonest = min(when for _, _, when, _ in ready)
            self.now = max(self.now, soonest)
            chosen = min(
                (item for item in ready if item[2] <= self.now), key=lambda item: (item[3], item[2])
            )
            self.now += TIMES.get(chosen[1], 2.0)
            try:
                chosen[0][1] = chosen[0][0].send(self.now)
            except StopIteration:
                waiting.remove(chosen[0])


ORDER = [Order()]


eps_norm = 1e-06
rope_base = 1000000.0
neg_fill = -1e30

f32 = jnp.float32
bf16 = jnp.bfloat16

ANY = pl.BlockSpec(memory_space=pl.ANY)
HBM = pl.BlockSpec(memory_space=pltpu.HBM)
LOAD = pl.BlockSpec(memory_space=pltpu.HBM)
STORE = pl.BlockSpec(memory_space=pltpu.HBM)
VMEM = pl.BlockSpec(memory_space=pltpu.VMEM)
SMEM = pl.BlockSpec(memory_space=pltpu.SMEM)


def dot(left_op, right_op):
    return jnp.dot(left_op, right_op, preferred_element_type=f32)


def dot_left(left_op, right_op):
    return lax.dot_general(
        left_op, right_op, (((0,), (0,)), ((), ())), preferred_element_type=f32
    )


def dot_right(left_op, right_op):
    return lax.dot_general(
        left_op, right_op, (((1,), (1,)), ((), ())), preferred_element_type=f32
    )


def spans(total, step):
    return [(at, min(step, total - at)) for at in range(0, total, step)]


def shape(dims, dtype):
    return jax.ShapeDtypeStruct(tuple(dims), dtype)


EARLY = []


def flush(ref):
    for item in EARLY[-1]:
        if item[0] is ref and not item[2]:
            item[1].start()
            item[2] = True


def call(kernel, name, out_shape, in_specs, operands, scratch=(), out_specs=None, deps=(), **more):
    several = isinstance(out_shape, tuple)
    outs = out_shape if several else (out_shape,)
    if out_specs is None:
        out_specs = tuple(VMEM for _ in outs)
    order = ORDER[0]
    if order.last is not None:
        deps = tuple(deps) + (order.last,)
    count = len(operands)
    size = lambda a: math.prod(a.shape) * jnp.dtype(a.dtype).itemsize
    token = not any(spec is VMEM for spec in out_specs)
    if token:
        out_shape = outs = tuple(outs) + (shape((8, 128), f32),)
        spec = pl.BlockSpec((8, 128), lambda i: (0, 0)) if "grid" in more else VMEM
        out_specs = tuple(out_specs) + (spec,)
        plain = kernel

        def kernel(*refs):
            mark = refs[count + len(outs) - 1]
            mark[...] = jnp.zeros(mark.shape, f32)
            plain(*refs[: count + len(outs) - 1], *refs[count + len(outs) :])

    if "grid" in more:
        room = 24 << 20
        loads, stores = [], []
    else:
        loads = [n for n, spec in enumerate(in_specs) if spec is LOAD]
        stores = [n for n, spec in enumerate(out_specs) if spec is STORE]
        fast = (VMEM, LOAD, STORE)
        room = sum(size(a) for a, spec in zip(operands, in_specs) if spec in fast)
        room += sum(size(a) for a, spec in zip(outs, out_specs) if spec in fast)
        room += sum(size(a) for a in scratch if a.memory_space == pltpu.VMEM)
        room = min(58 << 20, room + room // 2 + (6 << 20))
    moved = [operands[n] for n in loads] + [outs[n] for n in stores]
    extra = [pltpu.VMEM(a.shape, a.dtype) for a in moved]
    if moved:
        extra.append(pltpu.SemaphoreType.DMA((len(moved),)))

    def wrapped(*refs):
        ins, rest = list(refs[:count]), refs[count + len(deps) :]
        results, rest = list(rest[: len(outs)]), rest[len(outs) :]
        inner, rest = rest[: len(scratch)], rest[len(scratch) :]
        copies, items = [], []
        for k, n in enumerate(loads):
            copies.append(pltpu.make_async_copy(ins[n], rest[k], rest[-1].at[k]))
            ins[n] = rest[k]
        for copy in copies:
            copy.start()
        for k, n in enumerate(stores, len(loads)):
            items.append([rest[k], pltpu.make_async_copy(rest[k], results[n], rest[-1].at[k]), False])
            results[n] = rest[k]
        for copy in copies:
            copy.wait()
        EARLY.append(items)
        kernel(*ins, *results, *inner)
        EARLY.pop()
        for item in items:
            if not item[2]:
                item[1].start()
        for item in items:
            item[1].wait()

    made = pl.pallas_call(
        wrapped,
        out_shape=outs,
        in_specs=list(in_specs) + [ANY] * len(deps),
        out_specs=tuple(out_specs),
        scratch_shapes=list(scratch) + extra,
        compiler_params=pltpu.CompilerParams(vmem_limit_bytes=room),
        cost_estimate=cost(name),
        name=name,
        **more,
    )(*operands, *deps)
    order.took(made)
    if token:
        made = made[:-1]
    return made if several else made[0]


def swap(array, axis, bit):
    size = lax.axis_size(axis)
    return lax.ppermute(array, axis, [(i, i ^ bit) for i in range(size)])


def axis_bits(axis):
    size = lax.axis_size(axis)
    return [1 << k for k in range(size.bit_length() - 1)]


def fabric(flip):
    seq_bits = axis_bits("seq")
    outer = [("seq", bit) for bit in seq_bits[1:]] + [("leaf", bit) for bit in axis_bits("leaf")]
    return (outer[::-1] if flip else outer) + [("seq", seq_bits[0])]


def gather_pieces(own, flip):
    pieces = [own]
    for axis, bit in fabric(flip):
        pieces = pieces + [swap(piece, axis, bit) for piece in pieces]
    return pieces


class Place:
    def __init__(self):
        self.tensor_i = lax.axis_index("tensor")
        self.seq_i = lax.axis_index("seq")
        self.leaf_i = lax.axis_index("leaf")
        self.seq_n = lax.axis_size("seq")
        self.leaf_n = lax.axis_size("leaf")
        self.blocks = self.seq_n * self.leaf_n
        values = [self.tensor_i & 1, self.tensor_i >> 1]
        self.at = {"half": 0, "quarter": 1}
        for flip in (False, True):
            self.at["blocks", flip] = len(values)
            values += self.homes(fabric(flip))
            self.at["grads", flip] = len(values)
            values += self.homes(fabric(not flip)[:-1] + fabric(flip)[-1:])
        self.at["seq"] = len(values)
        values += self.seq_homes()
        self.at["chip"] = len(values)
        values += [self.seq_i & 1, self.seq_i >> 1]
        self.table = jnp.stack([jnp.asarray(v, jnp.int32) for v in values])

    def homes(self, links):
        out = []
        for p in range(1 << len(links)):
            seq_rel = sum(b for k, (a, b) in enumerate(links) if a == "seq" and p >> k & 1)
            leaf_rel = sum(b for k, (a, b) in enumerate(links) if a == "leaf" and p >> k & 1)
            out.append((self.leaf_i ^ leaf_rel) * self.seq_n + (self.seq_i ^ seq_rel))
        return out

    def seq_homes(self):
        out = [self.seq_i]
        for bit in axis_bits("seq")[::-1]:
            out = out + [h ^ bit for h in out]
        return out


class Weight:
    def __init__(self, arrays, rows, flip, first=0):
        self.arrays = list(arrays)
        self.rows = rows
        self.flip = flip
        self.first = first

    def source(self, place, scal, refs, block, skip, rows, cols):
        skip = skip + self.first
        if len(self.arrays) == 1:
            return refs[0].at[pl.ds(block * self.rows + skip, rows), cols], block
        home = scal[place.at["blocks", self.flip] + block]
        return refs[block].at[pl.ds(skip, rows), cols], home

    def halves(self, place, scal, refs, buf, sems, skip=0):
        mid = buf.shape[1] // 256 * 128
        parts = (slice(0, mid), slice(mid, buf.shape[1]))
        return [
            self.copies(
                place, scal, refs, buf.at[:, part], sems.at[n], skip=skip, cols=part
            )
            for n, part in enumerate(parts)
        ]

    def copies(self, place, scal, refs, buf, sems, skip=0, cols=slice(None)):
        rows = buf.shape[0] // place.blocks
        out = []
        for block in range(place.blocks):
            src, home = self.source(place, scal, refs, block, skip, rows, cols)
            if not isinstance(home, int):
                home = pl.multiple_of(home * rows, PAD)
            else:
                home = home * rows
            out.append(pltpu.make_async_copy(src, buf.at[pl.ds(home, rows)], sems.at[block]))
        return out


def row_spot(index, rows):
    return pl.ds(pl.multiple_of(index * rows, PAD), rows)


def put_halves(place, scal, buf, own_ref, got_ref):
    half = own_ref.shape[0]
    which = scal[place.at["half"]]
    buf[row_spot(which, half), :] = own_ref[...]
    buf[row_spot(1 - which, half), :] = got_ref[...]


def fold_kernel(spot, scal, keep_ref, got_ref, next_keep, next_send):
    rows = next_keep.shape[0]
    which = scal[spot]
    mine = row_spot(which, rows)
    away = row_spot(1 - which, rows)
    next_keep[...] = keep_ref[mine, :] + got_ref[mine, :].astype(f32)
    next_send[...] = (keep_ref[away, :] + got_ref[away, :].astype(f32)).astype(bf16)


def fold(place, spot, keep, got):
    rows, cols = keep.shape
    return call(
        functools.partial(fold_kernel, place.at[spot] if isinstance(spot, str) else spot),
        "fold",
        (shape((rows // 2, cols), f32), shape((rows // 2, cols), bf16)),
        [SMEM, VMEM, VMEM],
        (place.table, keep, got),
    )


def join_kernel(spot, scal, own_ref, got_ref, out_ref):
    rows = own_ref.shape[0]
    which = scal[spot]
    out_ref[row_spot(which, rows), :] = own_ref[...]
    out_ref[row_spot(1 - which, rows), :] = got_ref[...]


def join(place, spot, own, got, deps=()):
    rows, cols = own.shape
    return call(
        functools.partial(join_kernel, place.at[spot]),
        "join",
        shape((2 * rows, cols), own.dtype),
        [SMEM, VMEM, VMEM],
        (place.table, own, got),
        deps=deps,
    )


def normed_rows(values, gain):
    inv = lax.rsqrt(jnp.mean(values * values, axis=1, keepdims=True) + eps_norm)
    return (values * inv * gain).astype(bf16)


def entry_kernel(place, scal, x_ref, gain_ref, share_ref, normed_ref):
    rows = share_ref.shape[0]
    values = x_ref[...].astype(f32)
    normed_ref[...] = normed_rows(values, gain_ref[...])
    spot = scal[place.at["half"]] * 2 + scal[place.at["quarter"]]
    share_ref[...] = x_ref[row_spot(spot, rows), :].astype(f32)


def entry(place, hidden, gain, share):
    rows, width = hidden.shape
    return call(
        functools.partial(entry_kernel, place),
        "entry",
        (shape((share, width), f32), shape((rows, width), bf16)),
        [SMEM, LOAD, VMEM],
        (place.table, hidden, gain),
        out_specs=(VMEM, STORE),
    )


def finish_norm_kernel(base_ref, keep_ref, got_ref, gain_ref, sum_ref, normed_ref):
    total = base_ref[...] + (keep_ref[...] + got_ref[...].astype(f32))
    sum_ref[...] = total
    normed_ref[...] = normed_rows(total, gain_ref[...])


def finish_norm(base, keep, got, gain):
    return call(
        finish_norm_kernel,
        "finish_norm",
        (shape(base.shape, f32), shape(base.shape, bf16)),
        [LOAD, VMEM, VMEM, VMEM],
        (base, keep, got, gain),
        out_specs=(STORE, VMEM),
    )


def finish_plain_kernel(base_ref, keep_ref, got_ref, out_ref):
    out_ref[...] = (base_ref[...] + (keep_ref[...] + got_ref[...].astype(f32))).astype(bf16)


def finish_plain(base, keep, got):
    return call(
        finish_plain_kernel, "finish_plain", shape(base.shape, bf16), [LOAD, VMEM, VMEM], (base, keep, got)
    )


def finish_back_kernel(carry_ref, keep_ref, got_ref, src_ref, gain_ref, grad_ref, low_ref, term_ref):
    dnorm = keep_ref[...] + got_ref[...].astype(f32)
    source = src_ref[...]
    inv = lax.rsqrt(jnp.mean(source * source, axis=1, keepdims=True) + eps_norm)
    term_ref[...] = jnp.sum(dnorm * source * inv, axis=0, keepdims=True)
    scaled = dnorm * gain_ref[...]
    back = jnp.mean(scaled * source, axis=1, keepdims=True)
    grad = carry_ref[...] + inv * scaled - source * (inv * inv * inv) * back
    grad_ref[...] = grad
    low_ref[...] = grad.astype(bf16)


def finish_back(carry, keep, got, source, gain):
    width = carry.shape[1]
    return call(
        finish_back_kernel,
        "finish_back",
        (shape(carry.shape, f32), shape(carry.shape, bf16), shape((1, width), f32)),
        [LOAD, VMEM, VMEM, LOAD, VMEM],
        (carry, keep, got, source, gain),
        out_specs=(STORE, VMEM, STORE),
    )


def split_rows(place, scal, total_ref, keep_ref, send_ref):
    half = keep_ref.shape[0]
    which = scal[place.at["half"]]
    keep_ref[...] = total_ref[row_spot(which, half), :]
    send_ref[...] = total_ref[row_spot(1 - which, half), :].astype(bf16)


def project_kernel(place, weight, heads, hd, parts, *refs):
    scal, refs = refs[0], refs[1:]
    x_refs, refs = refs[:parts], refs[parts:]
    bias_ref, cos_ref, sin_ref = refs[:3]
    refs = refs[3:]
    w_refs, refs = refs[: len(weight.arrays)], refs[len(weight.arrays) :]
    q_ref, kv_ref, refs = refs[0], refs[1], refs[2:]
    if parts == 2:
        x_out, refs = refs[0], refs[1:]
    buf, sems = refs
    cols = (heads + 2) * hd
    copies = weight.copies(place, scal, w_refs, buf, sems, cols=slice(0, cols))
    for copy in copies:
        copy.start()
    if parts == 2:
        put_halves(place, scal, x_out, *x_refs)
        values = x_out[...]
    else:
        values = x_refs[0][...]
    for copy in copies:
        copy.wait()
    cos_wide = cos_ref[...]
    sin_wide = sin_ref[...]
    lin = dot(values, buf[...]) + bias_ref[...]
    for h in range(heads + 1):
        part = lin[:, h * hd : (h + 1) * hd]
        turned = part * cos_wide + pltpu.roll(part, hd // 2, 1) * sin_wide
        if h < heads:
            q_ref[:, h * hd : (h + 1) * hd] = turned.astype(bf16)
        else:
            kv_ref[:, :hd] = turned.astype(bf16)
    kv_ref[:, hd:] = lin[:, (heads + 1) * hd :].astype(bf16)


def project(place, x_parts, weight, bias, cos_wide, sin_wide, heads, hd):
    rows = sum(part.shape[0] for part in x_parts)
    width = x_parts[0].shape[1]
    cols = (heads + 2) * hd
    outs = [shape((rows, heads * hd), bf16), shape((rows, 2 * hd), bf16)]
    if len(x_parts) == 2:
        outs.append(shape((rows, width), bf16))
    return call(
        functools.partial(project_kernel, place, weight, heads, hd, len(x_parts)),
        "project",
        tuple(outs),
        [SMEM] + [LOAD if len(x_parts) == 1 else VMEM] * len(x_parts) + [VMEM, LOAD, LOAD]
        + [ANY] * len(weight.arrays),
        (place.table, *x_parts, bias, cos_wide, sin_wide, *weight.arrays),
        [pltpu.VMEM((width, cols), bf16), pltpu.SemaphoreType.DMA((place.blocks,))],
        out_specs=(STORE, VMEM) + (STORE,) * (len(outs) - 2),
    )


def put_keys(place, scal, buf, kv_refs):
    rows = kv_refs[0].shape[0]
    for n, ref in enumerate(kv_refs):
        buf[row_spot(scal[place.at["seq"] + n], rows), :] = ref[...]


def attend_kernel(place, weight, heads, hd, *refs):
    scal, q_ref, vis_ref, refs = refs[0], refs[1], refs[2], refs[3:]
    kv_refs, refs = refs[: place.seq_n], refs[place.seq_n :]
    w_refs, refs = refs[: len(weight.arrays)], refs[len(weight.arrays) :]
    o_ref, lse_ref, keep_ref, send_ref, kv_buf, w_buf, total_buf, sems = refs
    cols = slice((heads + 2) * hd, (2 * heads + 2) * hd)
    copies = weight.copies(place, scal, w_refs, w_buf, sems, cols=cols)
    for copy in copies:
        copy.start()
    put_keys(place, scal, kv_buf, kv_refs)
    keys = kv_buf[:, :hd]
    values = kv_buf[:, hd:]
    seen = vis_ref[...] > 0.5
    scale = 1.0 / math.sqrt(hd)
    lane = lax.broadcasted_iota(jnp.int32, lse_ref.shape, 1)
    lse_all = jnp.zeros(lse_ref.shape, f32)
    for h in range(heads):
        spot = slice(h * hd, (h + 1) * hd)
        scores = dot_right(q_ref[:, spot], keys) * scale
        scores = jnp.where(seen, scores, neg_fill)
        top = jnp.max(scores, axis=1, keepdims=True)
        expo = jnp.exp(scores - top)
        total = jnp.sum(expo, axis=1, keepdims=True)
        prob = (expo * (1.0 / total)).astype(bf16)
        o_ref[:, spot] = dot(prob, values).astype(bf16)
        lse_all = jnp.where(lane == h, top + jnp.log(total), lse_all)
    lse_ref[...] = lse_all
    flush(o_ref)
    flush(lse_ref)
    for copy in copies:
        copy.wait()
    for at, size in spans(w_buf.shape[0], 512):
        total_buf[:, at : at + size] = dot_right(o_ref[...], w_buf[at : at + size, :])
    split_rows(place, scal, total_buf, keep_ref, send_ref)


def attend(place, query, kv_parts, visible, weight, heads, hd, width):
    rows = query.shape[0]
    keys = visible.shape[1]
    half = rows // 2
    return call(
        functools.partial(attend_kernel, place, weight, heads, hd),
        "attend",
        (
            shape((rows, heads * hd), bf16),
            shape((rows, 128), f32),
            shape((half, width), f32),
            shape((half, width), bf16),
        ),
        [SMEM, LOAD, LOAD] + [VMEM] * len(kv_parts) + [ANY] * len(weight.arrays),
        (place.table, query, visible, *kv_parts, *weight.arrays),
        [
            pltpu.VMEM((keys, 2 * hd), bf16),
            pltpu.VMEM((width, heads * hd), bf16),
            pltpu.VMEM((rows, width), f32),
            pltpu.SemaphoreType.DMA((place.blocks,)),
        ],
        out_specs=(STORE, STORE, VMEM, VMEM),
    )


def attend_back_kernel(place, weight, heads, hd, *refs):
    (scal, own_ref, got_ref, q_ref, vis_ref, lse_ref, cos_ref, sin_ref), refs = refs[:8], refs[8:]
    kv_refs, refs = refs[: place.seq_n], refs[place.seq_n :]
    w_refs, refs = refs[: len(weight.arrays)], refs[len(weight.arrays) :]
    full_ref, dq_ref, keep_ref, send_ref, kv_buf, w_buf, do_buf, dkv_buf, sems = refs
    cols = slice((heads + 2) * hd, (2 * heads + 2) * hd)
    copies = weight.copies(place, scal, w_refs, w_buf, sems, cols=cols)
    for copy in copies:
        copy.start()
    put_halves(place, scal, full_ref, own_ref, got_ref)
    flush(full_ref)
    put_keys(place, scal, kv_buf, kv_refs)
    keys = kv_buf[:, :hd]
    values = kv_buf[:, hd:]
    seen = vis_ref[...] > 0.5
    cos_wide = cos_ref[...]
    sin_wide = sin_ref[...]
    scale = 1.0 / math.sqrt(hd)
    for copy in copies:
        copy.wait()
    do_buf[...] = dot(full_ref[...], w_buf[...]).astype(bf16)
    for h in range(heads):
        spot = slice(h * hd, (h + 1) * hd)
        query = q_ref[:, spot]
        dout = do_buf[:, spot]
        scores = dot_right(query, keys) * scale
        scores = jnp.where(seen, scores, neg_fill)
        prob = jnp.exp(scores - lse_ref[:, h : h + 1])
        dprob = dot_right(dout, values)
        delta = jnp.sum(prob * dprob, axis=1, keepdims=True)
        dscore = (prob * (dprob - delta)).astype(bf16)
        dquery = dot(dscore, keys) * scale
        dquery = dquery * cos_wide - pltpu.roll(dquery, hd // 2, 1) * sin_wide
        dq_ref[:, spot] = dquery.astype(bf16)
        dk_part = dot_left(dscore, query) * scale
        dv_part = dot_left(prob.astype(bf16), dout)
        if h == 0:
            dkv_buf[:, :hd] = dk_part
            dkv_buf[:, hd:] = dv_part
        else:
            dkv_buf[:, :hd] += dk_part
            dkv_buf[:, hd:] += dv_part
    rows = kv_refs[0].shape[0]
    core = scal[place.at["chip"]]
    for n in range(place.seq_n // 2):
        spot = slice(n * rows, (n + 1) * rows)
        keep_ref[spot, :] = dkv_buf[row_spot(2 * n + core, rows), :]
        send_ref[spot, :] = dkv_buf[row_spot(2 * n + 1 - core, rows), :].astype(bf16)


def attend_back(place, own, got, query, kv_parts, visible, lse, cos_wide, sin_wide, weight, heads, hd, deps=()):
    rows = query.shape[0]
    keys = visible.shape[1]
    width = own.shape[1]
    return call(
        functools.partial(attend_back_kernel, place, weight, heads, hd),
        "attend_back",
        (
            shape((rows, width), bf16),
            shape((rows, heads * hd), bf16),
            shape((keys // 2, 2 * hd), f32),
            shape((keys // 2, 2 * hd), bf16),
        ),
        [SMEM, VMEM, VMEM] + [LOAD] * (5 + len(kv_parts)) + [ANY] * len(weight.arrays),
        (place.table, own, got, query, visible, lse, cos_wide, sin_wide, *kv_parts, *weight.arrays),
        [
            pltpu.VMEM((keys, 2 * hd), bf16),
            pltpu.VMEM((width, heads * hd), bf16),
            pltpu.VMEM((rows, heads * hd), bf16),
            pltpu.VMEM((keys, 2 * hd), f32),
            pltpu.SemaphoreType.DMA((place.blocks,)),
        ],
        out_specs=(STORE, STORE, VMEM, VMEM),
        deps=deps,
    )


def lin_back_kernel(place, weight, heads, hd, *refs):
    (scal, dq_ref, dkv_ref, got_ref, cos_ref, sin_ref), refs = refs[:6], refs[6:]
    w_refs, refs = refs[: len(weight.arrays)], refs[len(weight.arrays) :]
    dlin_ref, sums_ref, keep_ref, send_ref, w_buf, total_buf, sems = refs
    cols = (heads + 2) * hd
    copies = weight.copies(place, scal, w_refs, w_buf, sems, cols=slice(0, cols))
    for copy in copies:
        copy.start()
    dkv = dkv_ref[...] + got_ref[...].astype(f32)
    dkey = dkv[:, :hd]
    dkey = dkey * cos_ref[...] - pltpu.roll(dkey, hd // 2, 1) * sin_ref[...]
    dlin_ref[:, : heads * hd] = dq_ref[...]
    dlin_ref[:, heads * hd : (heads + 1) * hd] = dkey.astype(bf16)
    dlin_ref[:, (heads + 1) * hd :] = dkv[:, hd:].astype(bf16)
    dlin = dlin_ref[...]
    sums_ref[...] = jnp.sum(dlin.astype(f32), axis=0, keepdims=True)
    flush(dlin_ref)
    for copy in copies:
        copy.wait()
    for at, size in spans(w_buf.shape[0], 512):
        total_buf[:, at : at + size] = dot_right(dlin, w_buf[at : at + size, :])
    split_rows(place, scal, total_buf, keep_ref, send_ref)


def lin_back(place, dquery, dkv, got, cos_wide, sin_wide, weight, heads, hd, width, deps=()):
    rows = dquery.shape[0]
    cols = (heads + 2) * hd
    return call(
        functools.partial(lin_back_kernel, place, weight, heads, hd),
        "lin_back",
        (
            shape((rows, cols), bf16),
            shape((1, cols), f32),
            shape((rows // 2, width), f32),
            shape((rows // 2, width), bf16),
        ),
        [SMEM, LOAD, VMEM, VMEM, LOAD, LOAD] + [ANY] * len(weight.arrays),
        (place.table, dquery, dkv, got, cos_wide, sin_wide, *weight.arrays),
        [
            pltpu.VMEM((width, cols), bf16),
            pltpu.VMEM((rows, width), f32),
            pltpu.SemaphoreType.DMA((place.blocks,)),
        ],
        out_specs=(STORE, STORE, VMEM, VMEM),
        deps=deps,
    )


class Mixed:
    def __init__(self, arrays, gate, up, rows):
        self.arrays = list(arrays)
        self.spots = (gate, up)
        self.rows = rows

    def halves(self, place, scal, refs, buf, sems, skip=0):
        spots = self.spots[1 if skip else 0]
        parts = [refs[n].at[pl.ds(at, self.rows)] for n, at in spots]
        return Weight(parts, self.rows, False).halves(place, scal, parts, buf, sems)


def start_all(copies):
    for copy in copies:
        copy.start()


def wait_all(copies):
    for copy in copies:
        copy.wait()


def mlp_kernel(place, w_in, w_down, *refs):
    (scal, own_ref, got_ref), refs = refs[:3], refs[3:]
    in_refs, refs = refs[: len(w_in.arrays)], refs[len(w_in.arrays) :]
    down_refs, refs = refs[: len(w_down.arrays)], refs[len(w_down.arrays) :]
    (
        full_ref, gate_ref, up_ref, mix_ref, keep_ref, send_ref,
        gate_buf, up_buf, down_buf, total_buf, gate_sems, up_sems, down_sems,
    ) = refs
    shard = gate_buf.shape[0] // place.blocks
    gate_copies = w_in.halves(place, scal, in_refs, gate_buf, gate_sems)
    up_copies = w_in.halves(place, scal, in_refs, up_buf, up_sems, skip=shard)
    down_copies = w_down.halves(place, scal, down_refs, down_buf, down_sems)
    start_all(gate_copies[0])
    put_halves(place, scal, full_ref, own_ref, got_ref)
    flush(full_ref)
    values = full_ref[...]
    units = gate_buf.shape[1]
    mid = units // 256 * 128
    parts = (spans(mid, 384), [(mid + at, size) for at, size in spans(units - mid, 384)])
    start_all(gate_copies[1])
    wait_all(gate_copies[0])
    for n in range(2):
        start_all(up_copies[n])
        for at, size in parts[n]:
            gate_ref[:, at : at + size] = dot(values, gate_buf[:, at : at + size]).astype(bf16)
        wait_all(gate_copies[1] if n == 0 else up_copies[0])
    flush(gate_ref)
    for n in range(2):
        start_all(down_copies[n])
        for at, size in parts[n]:
            spot = slice(at, at + size)
            up = dot(values, up_buf[:, spot])
            gate = gate_ref[:, spot].astype(f32)
            up_ref[:, spot] = up.astype(bf16)
            mix_ref[:, spot] = (gate * jax.nn.sigmoid(gate) * up).astype(bf16)
        wait_all(up_copies[1] if n == 0 else down_copies[0] + down_copies[1])
    flush(up_ref)
    flush(mix_ref)
    mixed = mix_ref[...]
    for at, size in spans(down_buf.shape[0], 512):
        total_buf[:, at : at + size] = dot_right(mixed, down_buf[at : at + size, :])
    split_rows(place, scal, total_buf, keep_ref, send_ref)


def mlp(place, own, got, w_in, w_down):
    half, width = own.shape
    rows = 2 * half
    units = w_in.arrays[0].shape[1]
    dma = pltpu.SemaphoreType.DMA((2, place.blocks))
    return call(
        functools.partial(mlp_kernel, place, w_in, w_down),
        "mlp",
        (
            shape((rows, width), bf16),
            shape((rows, units), bf16),
            shape((rows, units), bf16),
            shape((rows, units), bf16),
            shape((half, width), f32),
            shape((half, width), bf16),
        ),
        [SMEM, VMEM, VMEM] + [ANY] * (len(w_in.arrays) + len(w_down.arrays)),
        (place.table, own, got, *w_in.arrays, *w_down.arrays),
        [
            pltpu.VMEM((width, units), bf16),
            pltpu.VMEM((width, units), bf16),
            pltpu.VMEM((width, units), bf16),
            pltpu.VMEM((rows, width), f32),
            dma,
            dma,
            dma,
        ],
        out_specs=(STORE, STORE, STORE, STORE, VMEM, VMEM),
    )


def mlp_back_kernel(place, w_in, w_down, parts, *refs):
    scal, refs = refs[0], refs[1:]
    d_refs, refs = refs[:parts], refs[parts:]
    gate_ref, up_ref, refs = refs[0], refs[1], refs[2:]
    in_refs, refs = refs[: len(w_in.arrays)], refs[len(w_in.arrays) :]
    down_refs, refs = refs[: len(w_down.arrays)], refs[len(w_down.arrays) :]
    dgate_ref, dup_ref, keep_ref, send_ref, refs = refs[0], refs[1], refs[2], refs[3], refs[4:]
    if parts == 2:
        full_ref, refs = refs[0], refs[1:]
    gate_buf, up_buf, down_buf, total_buf, gate_sems, up_sems, down_sems = refs
    shard = gate_buf.shape[0] // place.blocks
    gate_copies = w_in.halves(place, scal, in_refs, gate_buf, gate_sems)
    up_copies = w_in.halves(place, scal, in_refs, up_buf, up_sems, skip=shard)
    down_copies = w_down.halves(place, scal, down_refs, down_buf, down_sems)
    start_all(down_copies[0])
    if parts == 2:
        put_halves(place, scal, full_ref, *d_refs)
        flush(full_ref)
        values = full_ref[...]
    else:
        values = d_refs[0][...]
    units = gate_buf.shape[1]
    mid = units // 256 * 128
    cuts = (spans(mid, 384), [(mid + at, size) for at, size in spans(units - mid, 384)])
    start_all(down_copies[1])
    wait_all(down_copies[0])
    for n in range(2):
        start_all(gate_copies[n])
        for at, size in cuts[n]:
            spot = slice(at, at + size)
            dmixed = dot(values, down_buf[:, spot])
            gate = gate_ref[:, spot].astype(f32)
            up = up_ref[:, spot].astype(f32)
            sig = jax.nn.sigmoid(gate)
            dgate_ref[:, spot] = (dmixed * up * sig * (1.0 + gate * (1.0 - sig))).astype(bf16)
            dup_ref[:, spot] = (dmixed * (gate * sig)).astype(bf16)
        if n == 0:
            wait_all(down_copies[1])
    start_all(up_copies[0] + up_copies[1])
    flush(dgate_ref)
    flush(dup_ref)
    wait_all(gate_copies[0] + gate_copies[1])
    dgate = dgate_ref[...]
    dup = dup_ref[...]
    for at, size in spans(gate_buf.shape[0], 512):
        spot = slice(at, at + size)
        total_buf[:, spot] = dot_right(dgate, gate_buf[spot, :])
    wait_all(up_copies[0] + up_copies[1])
    for at, size in spans(gate_buf.shape[0], 512):
        spot = slice(at, at + size)
        total_buf[:, spot] += dot_right(dup, up_buf[spot, :])
    split_rows(place, scal, total_buf, keep_ref, send_ref)


def mlp_back(place, d_parts, gate, up, w_in, w_down, deps=()):
    rows = sum(part.shape[0] for part in d_parts)
    width = d_parts[0].shape[1]
    half = rows // 2
    units = gate.shape[1]
    outs = [
        shape((rows, units), bf16),
        shape((rows, units), bf16),
        shape((half, width), f32),
        shape((half, width), bf16),
    ]
    if len(d_parts) == 2:
        outs.append(shape((rows, width), bf16))
    dma = pltpu.SemaphoreType.DMA((2, place.blocks))
    return call(
        functools.partial(mlp_back_kernel, place, w_in, w_down, len(d_parts)),
        "mlp_back",
        tuple(outs),
        [SMEM] + [LOAD if len(d_parts) == 1 else VMEM] * len(d_parts) + [LOAD, LOAD]
        + [ANY] * (len(w_in.arrays) + len(w_down.arrays)),
        (place.table, *d_parts, gate, up, *w_in.arrays, *w_down.arrays),
        [
            pltpu.VMEM((width, units), bf16),
            pltpu.VMEM((width, units), bf16),
            pltpu.VMEM((width, units), bf16),
            pltpu.VMEM((rows, width), f32),
            dma,
            dma,
            dma,
        ],
        out_specs=(STORE, STORE, VMEM, VMEM) + (STORE,) * (len(outs) - 4),
        deps=deps,
    )


def weight_grad_kernel(place, micro_n, pairs, homes, *refs):
    scal, refs = refs[0], refs[1:]
    left_refs = [refs[p * micro_n : (p + 1) * micro_n] for p in range(pairs)]
    refs = refs[pairs * micro_n :]
    right_refs = [refs[p * micro_n : (p + 1) * micro_n] for p in range(pairs)]
    refs = refs[pairs * micro_n :]
    outs = 1 if homes is None else 2
    out_refs, refs = refs[:outs], refs[outs:]
    bufs, sems = refs[:pairs], refs[pairs]
    shard = bufs[0].shape[0] // place.blocks
    half = place.blocks // 2
    copies = []
    at_col = 0
    for p in range(pairs):
        buf = bufs[p]
        cols = buf.shape[1]
        ready = 0
        for at, size in spans(buf.shape[0], 256):
            spot = slice(at, at + size)
            total = None
            for left, right in zip(left_refs[p], right_refs[p]):
                part = dot_left(left[:, spot], right[...])
                total = part if total is None else total + part
            buf[spot, :] = total.astype(bf16)
            while homes is None and (ready + 1) * shard <= at + size:
                src = buf.at[pl.ds(ready * shard, shard)]
                dst = out_refs[0].at[pl.ds(ready * shard, shard), pl.ds(at_col, cols)]
                copies.append(pltpu.make_async_copy(src, dst, sems.at[len(copies)]))
                copies[-1].start()
                ready += 1
        if homes is not None:
            for block in list(range(half, place.blocks)) + list(range(half)):
                home = scal[homes + block]
                src = buf.at[pl.ds(pl.multiple_of(home * shard, PAD), shard)]
                out = out_refs[block // half]
                dst = out.at[pl.ds(block % half * shard, shard), pl.ds(at_col, cols)]
                copies.append(pltpu.make_async_copy(src, dst, sems.at[len(copies)]))
                copies[-1].start()
        at_col += cols
    for copy in copies:
        copy.wait()


def weight_grad(place, pairs, homes, deps=()):
    micro_n = len(pairs[0][0])
    rows, width = pairs[0][0][0].shape
    cols = [rights[0].shape[1] for _, rights in pairs]
    if homes is None:
        outs = (shape((width, sum(cols)), bf16),)
    else:
        outs = (shape((width // 2, sum(cols)), bf16),) * 2
    lefts = [a for left, _ in pairs for a in left]
    rights = [a for _, right in pairs for a in right]
    copies = place.blocks * len(pairs)
    return call(
        functools.partial(weight_grad_kernel, place, micro_n, len(pairs), homes),
        "weight_grad" if sum(cols) > width else "weight_grad_small",
        outs,
        [SMEM] + [LOAD] * (len(lefts) + len(rights)),
        (place.table, *lefts, *rights),
        [pltpu.VMEM((width, c), bf16) for c in cols] + [pltpu.SemaphoreType.DMA((copies,))],
        out_specs=tuple(HBM for _ in outs),
        deps=deps,
    )


def fold_rows_kernel(keep_lo, keep_hi, got_lo, got_hi, keep_ref, send_ref):
    keep_ref[...] = (keep_lo[...].astype(f32) + got_lo[...].astype(f32)).astype(bf16)
    send_ref[...] = (keep_hi[...].astype(f32) + got_hi[...].astype(f32)).astype(bf16)


def fold_rows(keep, got):
    rows, cols = keep.shape
    half = rows // 2
    tile = half
    for count in (8, 4, 3, 2):
        if half % (count * PAD) == 0:
            tile = half // count
            break
    steps = half // tile
    low = pl.BlockSpec((tile, cols), lambda i: (i, 0))
    high = pl.BlockSpec((tile, cols), lambda i: (i + steps, 0))
    return call(
        fold_rows_kernel,
        "fold_rows",
        (shape((half, cols), bf16), shape((half, cols), bf16)),
        [low, high, low, high],
        (keep, keep, got, got),
        out_specs=(low, low),
        grid=(steps,),
    )


def combine_kernel(keep_ref, got_ref, out_ref):
    out_ref[...] = (keep_ref[...].astype(f32) + got_ref[...].astype(f32)).astype(bf16)


def combine(keep, got):
    return call(
        combine_kernel,
        "combine",
        shape(keep.shape, bf16),
        [LOAD, LOAD],
        (keep, got),
        out_specs=(STORE,),
    )


def finish_grads_kernel(counts, *refs):
    out_ref = refs[-1]
    cols = out_ref.shape[1]
    layer = pl.program_id(0)
    at = 0
    for n, count in enumerate(counts):

        @pl.when(layer == n)
        def write(parts=refs[at : at + count]):
            out_ref[...] = sum(part[...].astype(f32) for part in parts)[:, :cols]

        at += count


def finish_grads(layers, cols, window):
    rows = layers[0][0][0].shape[0]
    specs, operands = [], []
    for arrays, spot in layers:
        for array in arrays:
            specs.append(pl.BlockSpec((rows, window), lambda i, spot=spot: (0, spot)))
            operands.append(array)
    return call(
        functools.partial(finish_grads_kernel, [len(arrays) for arrays, _ in layers]),
        "finish_grads",
        shape((len(layers), rows, cols), f32),
        specs,
        tuple(operands),
        out_specs=(pl.BlockSpec((pl.Squeezed(), rows, cols), lambda i: (i, 0, 0)),),
        grid=(len(layers),),
    )


def pack_attn_kernel(place, group_at, smalls, *refs):
    scal, q_ref, k_ref, v_ref, o_ref = refs[:5]
    small_refs, out_ref = refs[5:-1], refs[-1]
    rows, cols = q_ref.shape
    hd = k_ref.shape[1] // 2
    high = scal[group_at] == 1
    pick = lambda ref: jnp.where(high, ref[:, hd:], ref[:, :hd])
    out_ref[:rows, :cols] = q_ref[...]
    out_ref[:rows, cols : cols + hd] = pick(k_ref)
    out_ref[:rows, cols + hd : cols + 2 * hd] = pick(v_ref)
    out_ref[:rows, cols + 2 * hd :] = o_ref[...]
    if smalls:
        gain1, gain2, bias_q, bias_k, bias_v = small_refs
        layers, n = gain1.shape
        heads, bias_n = bias_q.shape[1:]
        out_ref[rows:, :] = jnp.zeros((2 * PAD, out_ref.shape[1]), bf16)
        at = rows
        for block in (gain1[...], gain2[...]):
            out_ref[at : at + layers, :n] = block
            at += layers
        for layer in range(layers):
            out_ref[at : at + heads, :bias_n] = bias_q[layer]
            at += heads
            for ref in (bias_k, bias_v):
                both = ref[layer].astype(f32)
                out_ref[at : at + 1, :bias_n] = jnp.where(high, both[1:], both[:1]).astype(bf16)
                at += 1


def pack_attn(place, layer, w_query, w_key, w_value, w_out_t, smalls):
    _, rows, cols = w_query.shape
    kv_cols = w_key.shape[2]
    block = lambda c: pl.BlockSpec((pl.Squeezed(), rows, c), lambda i: (layer, 0, 0))
    whole = lambda a: pl.BlockSpec(a.shape, lambda i: (0,) * a.ndim)
    out = (rows + (2 * PAD if smalls else 0), 2 * cols + kv_cols)
    return call(
        functools.partial(pack_attn_kernel, place, place.at["quarter"], bool(smalls)),
        "pack",
        shape(out, bf16),
        [SMEM, block(cols), block(kv_cols), block(kv_cols), block(cols)]
        + [whole(a) for a in smalls],
        (place.table, w_query, w_key, w_value, w_out_t, *smalls),
        out_specs=(pl.BlockSpec(out, lambda i: (0, 0)),),
        grid=(1,),
    )


def pack_wide_kernel(*refs):
    out_ref = refs[-1]
    at = 0
    for ref in refs[:-1]:
        rows, cols = ref.shape
        spot = slice(at, at + rows)
        if out_ref.shape[1] > cols:
            tail = cols // 128 * 128
            out_ref[spot, tail:] = jnp.zeros((rows, out_ref.shape[1] - tail), bf16)
        out_ref[spot, :cols] = ref[...]
        at += rows


def pack_wide(layer, arrays, units):
    _, rows, cols = arrays[0].shape
    block = pl.BlockSpec((pl.Squeezed(), rows, cols), lambda i: (layer, 0, 0))
    out = (rows * len(arrays), units)
    return call(
        pack_wide_kernel,
        "pack",
        shape(out, bf16),
        [block] * len(arrays),
        tuple(arrays),
        out_specs=(pl.BlockSpec(out, lambda i: (0, 0)),),
        grid=(1,),
    )


def unpack_kernel(place, weight, shard, heads, bias_n, layers, *refs):
    scal, refs = refs[0], refs[1:]
    w_refs, refs = refs[: len(weight.arrays)], refs[len(weight.arrays) :]
    outs, buf, sems = refs[:-2], refs[-2], refs[-1]
    copies = weight.copies(place, scal, w_refs, buf, sems, skip=shard, cols=slice(0, buf.shape[1]))
    for copy in copies:
        copy.start()
    for copy in copies:
        copy.wait()
    for block in range(place.blocks):
        part = buf[block * 2 * PAD : (block + 1) * 2 * PAD, :].astype(f32)
        at = 0
        for n in range(2 * layers):
            outs[n][:, block * shard : (block + 1) * shard] = part[at : at + 1, :shard]
            at += 1
        for layer in range(layers):
            for h in range(heads + 2):
                spot = h * bias_n * place.blocks + block * bias_n
                outs[2 * layers + layer][:, spot : spot + bias_n] = part[at : at + 1, :bias_n]
                at += 1


def unpack(place, weight, shard, heads, bias_n, layers, width):
    cols = (heads + 2) * bias_n * place.blocks
    return call(
        functools.partial(unpack_kernel, place, weight, shard, heads, bias_n, layers),
        "unpack",
        (shape((1, width), f32),) * (2 * layers) + (shape((1, cols), f32),) * layers,
        [SMEM] + [ANY] * len(weight.arrays),
        (place.table, *weight.arrays),
        [
            pltpu.VMEM((place.blocks * 2 * PAD, 256), bf16),
            pltpu.SemaphoreType.DMA((place.blocks,)),
        ],
    )


def hold_kernel(src_ref, out_ref):
    out_ref[...] = src_ref[...]


def hold(array):
    return call(hold_kernel, "hold", shape(array.shape, array.dtype), [VMEM], (array,))


def corners_kernel(far_ref, side_ref, gate_ref, up_ref, sems):
    rows = gate_ref.shape[0]
    copies = [
        pltpu.make_async_copy(far_ref.at[pl.ds(0, rows)], gate_ref, sems.at[0]),
        pltpu.make_async_copy(side_ref.at[pl.ds(rows, rows)], up_ref, sems.at[1]),
    ]
    start_all(copies)
    wait_all(copies)


def corners(far, side):
    out = shape((far.shape[0] // 2, far.shape[1]), bf16)
    return call(
        corners_kernel, "pack", (out, out), [HBM, HBM], (far, side),
        [pltpu.SemaphoreType.DMA((2,))], (HBM, HBM),
    )


def touch_kernel(*refs):
    refs[-1][...] = jnp.zeros(refs[-1].shape, f32)


def touch(arrays):
    call(touch_kernel, "touch", shape((8, 128), f32), [HBM] * len(arrays), tuple(arrays))


def small_kernel(place, layers, trees, hd, *refs):
    scal, out_ref = refs[0], refs[-1]
    refs = refs[1:-1]
    count = layers * trees
    gains1, gains2, sums = refs[:count], refs[count : 2 * count], refs[2 * count :]
    half, quarter = scal[place.at["half"]], scal[place.at["quarter"]]
    out_ref[...] = jnp.zeros(out_ref.shape, f32)
    width = out_ref.shape[1]
    for layer in range(layers):
        part = slice(layer * trees, (layer + 1) * trees)
        total = lambda group: sum(ref[...] for ref in group[part])
        out_ref[layer : layer + 1, :] = total(gains1)
        out_ref[layers + layer : layers + layer + 1, :] = total(gains2)
        row = total(sums)
        q_cols = row.shape[1] - 2 * hd
        at = 2 * layers + layer
        for n in range(width // q_cols):
            mine = quarter * 2 + half == n
            out_ref[at : at + 1, n * q_cols : (n + 1) * q_cols] = jnp.where(
                mine, row[:, :q_cols], 0.0
            )
        at += layers
        for n in range(2):
            for kind in range(2):
                spot = (2 * kind + n) * hd
                start = q_cols + kind * hd
                out_ref[at : at + 1, spot : spot + hd] = jnp.where(
                    quarter == n, row[:, start : start + hd], 0.0
                )


def kv_pick_kernel(skip, *refs):
    low_ref, total_ref = refs[-1], refs[-2]
    at = 0
    for ref in refs[:-2]:
        rows = ref.shape[0]
        low_ref[at : at + rows, :] = ref[:, skip:]
        total_ref[at : at + rows, :] = ref[:, skip:].astype(f32)
        at += rows


def kv_add_kernel(left_ref, right_ref, total_ref, low_ref):
    total = left_ref[...] + right_ref[...].astype(f32)
    total_ref[...] = total
    low_ref[...] = total.astype(bf16)


def kv_place_kernel(group_at, scal, own_ref, got_ref, key_ref, value_ref):
    layers, rows, cols = key_ref.shape
    hd = cols // 2
    high = scal[group_at] == 1
    for layer in range(layers):
        spot = slice(layer * rows, (layer + 1) * rows)
        own = own_ref[spot, :]
        got = got_ref[spot, :].astype(f32)
        first = jnp.where(high, got, own)
        second = jnp.where(high, own, got)
        key_ref[layer, :, :hd] = first[:, :hd]
        key_ref[layer, :, hd:] = second[:, :hd]
        value_ref[layer, :, :hd] = first[:, hd:]
        value_ref[layer, :, hd:] = second[:, hd:]


def add_kernel(left_ref, right_ref, out_ref):
    out_ref[...] = left_ref[...] + right_ref[...]


def tree_tables(parent_row):
    block_ids = jnp.arange(NBLK, dtype=jnp.int32)
    step_up = (block_ids[None, :] == parent_row[:, None]).astype(jnp.int32)
    reach_tab = jnp.eye(NBLK, dtype=jnp.int32) + step_up
    for repeat_idx in range(max(1, (NBLK - 1).bit_length())):
        reach_tab = (jnp.dot(reach_tab, reach_tab) > 0).astype(jnp.int32)
    depth_tab = jnp.sum(reach_tab, axis=1) - 1
    return (reach_tab, depth_tab)


def geometry(parent_row, seq_index, rows_dev):
    reach_tab, depth_tab = tree_tables(parent_row)
    token_idx = seq_index * rows_dev + jnp.arange(rows_dev, dtype=jnp.int32)
    key_idx = jnp.arange(NBLK * BLK, dtype=jnp.int32)
    block_ids = jnp.arange(NBLK, dtype=jnp.int32)
    query_hot = (token_idx[:, None] // BLK == block_ids[None, :]).astype(f32)
    key_hot = (key_idx[:, None] // BLK == block_ids[None, :]).astype(f32)
    link_rows = jnp.dot(query_hot, reach_tab.astype(f32), precision=lax.Precision.HIGHEST)
    link_tab = jnp.dot(link_rows, key_hot.T, precision=lax.Precision.HIGHEST)
    visible = (link_tab > 0.5) & (key_idx[None, :] <= token_idx[:, None])
    depth_rows = jnp.dot(query_hot, depth_tab.astype(f32), precision=lax.Precision.HIGHEST)
    position = BLK * depth_rows + (token_idx % BLK).astype(f32)
    return (position, visible.astype(f32))


def wide_angles(position, head_dim):
    freq_idx = jnp.arange(head_dim // 2, dtype=f32)
    inv_freq = rope_base ** (-2.0 * freq_idx / head_dim)
    turn_val = position[:, None] * inv_freq[None, :]
    cosine, sine_val = (jnp.cos(turn_val), jnp.sin(turn_val))
    return (
        jnp.concatenate([cosine, cosine], axis=1),
        jnp.concatenate([-sine_val, sine_val], axis=1),
    )


def body(
    hidden_in,
    parents,
    cotangent,
    attn_gain,
    w_query,
    b_query,
    w_key,
    b_key,
    w_value,
    b_value,
    w_out,
    mlp_gain,
    w_gate,
    w_up,
    w_down,
):
    place = Place()
    both = ("leaf", "seq")
    micro_n, rows_dev, width = hidden_in.shape
    layer_n, shard = w_query.shape[:2]
    heads, bias_cols = b_query.shape[1:]
    kv_heads = b_key.shape[1]
    hd = w_key.shape[2] // kv_heads
    tensor_n = lax.axis_size("tensor")
    units = -(-w_gate.shape[2] // 256) * 256
    blocks = place.blocks
    assert tensor_n == 4 and kv_heads == 2 and layer_n == 2 and place.seq_n == 4
    kv_group = place.tensor_i >> 1
    q_cols = heads * hd
    qkv_cols = q_cols + 2 * hd
    pack_cols = qkv_cols + q_cols
    share = rows_dev // tensor_n

    order = ORDER[0] = Order()
    w_down_t = jnp.swapaxes(w_down, 1, 2)
    w_out_t = jnp.swapaxes(w_out, 1, 2)
    smalls = (attn_gain, mlp_gain, b_query, b_key, b_value)
    whole = lambda own: [lax.all_gather(own, both, axis=0, tiled=True)]
    links = fabric(True)
    own = pack_attn(place, 0, w_query, w_key, w_value, w_out_t, smalls)
    pieces = [own]
    for n, (axis, bit) in enumerate(links):
        pieces = pieces + [swap(piece, axis, bit) for piece in pieces]
        if n == len(links) - 2:
            touch([pieces[1]] + pieces[2:3])
    attn0 = Weight(pieces, shard, True)
    wide = lambda array, layer=0: pack_wide(layer, (array,), units)
    (a_axis, a_bit), (b_axis, b_bit), *others = fabric(False)
    own_in = pack_wide(0, (w_gate, w_up), units)
    side_in = swap(own_in, b_axis, b_bit)
    *gain_rows, bias0, bias1 = unpack(place, attn0, shard, heads, bias_cols, layer_n, width)

    def far_in():
        again = pack_wide(0, (w_gate, w_up), units)
        return [again, swap(again, a_axis, a_bit)]

    def corners_in(again, far):
        part_gate, part_up = corners(far, side_in)
        corner_gate = swap(part_gate, b_axis, b_bit)
        corner_up = swap(part_up, a_axis, a_bit)
        arrays = [again, far, side_in, corner_gate, corner_up]
        gate = [(0, 0), (1, 0), (2, 0), (3, 0)]
        up = [(0, shard), (1, shard), (2, shard), (4, 0)]
        for axis, bit in others:
            count = len(arrays)
            arrays = arrays + [swap(array, axis, bit) for array in arrays]
            gate = gate + [(n + count, at) for n, at in gate]
            up = up + [(n + count, at) for n, at in up]
        return arrays, gate, up

    def second_layer():
        attn = whole(pack_attn(place, 1, w_query, w_key, w_value, w_out_t, ()))
        return attn, whole(pack_wide(1, (w_gate, w_up, w_down_t), units))

    weights = [
        (attn0, None, None, bias0, gain_rows[0], gain_rows[2]),
        (None, None, None, bias1, gain_rows[1], gain_rows[3]),
    ]

    tables = []
    for micro in range(micro_n):
        position, visible = geometry(parents[micro], place.seq_i, rows_dev)
        tables.append(wide_angles(position, hd) + (visible,))

    spot = (place.at["half"], place.at["quarter"])
    quarter = place.table[spot[0]] * 2 + place.table[spot[1]]
    arrive = {(0, "attn"): 40.0, (1, "attn"): 170.0, (1, "mlp"): 260.0}
    offloaded = [("down", "gate", "up"), ()]
    finished = {}
    busy = {"core": 0, "row": 0}
    kept, slots, grads, settled, marks = {}, {}, {}, {}, set()
    finals, tails = [None] * micro_n, [None] * micro_n

    def scatter(keep, send, at):
        got = swap(send, "tensor", 1)
        at = yield "fold", order.link("z1", "z", at), 0
        keep, send = fold(place, "quarter", keep, got)
        got = swap(send, "tensor", 2)
        return keep, got, order.link("z2", "z", at)

    def gather(own, at):
        got = swap(own, "tensor", 2)
        at = yield "join", order.link("z2", "z", at), 0
        own = join(place, "quarter", own, got)
        got = swap(own, "tensor", 1)
        return own, got, order.link("z1", "z", at)

    def last_rows(micro, middle, keep, send):
        passed = lambda key: (lambda: 0.0 if key in marks else None)
        yield "hold", passed(("attend_back", 1, micro)), 2
        got = swap(hold(send), "tensor", 1)
        at = order.link("z1", "z", order.now)
        at = yield "fold", at, 1
        keep, send = fold(place, "quarter", keep, got)
        got = swap(send, "tensor", 2)
        at = order.link("z2", "z", at)
        at = yield "finish_plain", at, 1
        low = finish_plain(middle, keep, got)
        own, got, at = yield from gather(low, at)
        yield "join", at, 3
        finals[micro] = join(place, "half", own, got)

    def tree(micro):
        cos_wide, sin_wide, visible = tables[micro]
        at = yield "entry", 20.0, 1
        state, normed = entry(place, hidden_in[micro], weights[0][4], share)
        parts = (normed,)
        for layer in range(layer_n):
            bias, gain1, gain2 = weights[layer][3:]
            ready = lambda at=at, layer=layer: (
                max(at, arrive[layer, "attn"]) if layer == 0 or layer in settled else None
            )
            at = yield "project", ready, 2
            w_attn = settled[layer][0] if layer in settled else attn0
            outs = project(place, parts, w_attn, bias, cos_wide, sin_wide, heads, hd)
            marks.add(("project", layer, micro))
            query, kv_own = outs[:2]
            normed = outs[2] if len(outs) == 3 else parts[0]
            kv_parts = [kv_own]
            for bit in axis_bits("seq")[::-1]:
                kv_parts = kv_parts + [swap(part, "seq", bit) for part in kv_parts]
            at = yield "attend", order.link("kv", "kv", at) + 2.0, 2
            attended, lse, keep, send = attend(
                place, query, kv_parts, visible, w_attn, heads, hd, width
            )
            keep, got, at = yield from scatter(keep, send, at)
            at = yield "finish_norm", at, 0
            middle, low = finish_norm(state, keep, got, gain2)
            own, got, at = yield from gather(low, at)
            ready = lambda at=at, layer=layer: (
                max(at, arrive[layer, "mlp"]) if layer or 0 in settled else None
            )
            at = yield "mlp", ready, 2 + 0.1 * micro
            w_in, w_dn = settled[layer][1:]
            normed_mlp, gate, up, mixed, keep, send = mlp(place, own, got, w_in, w_dn)
            kept[layer, micro] = (
                state, normed, query, kv_parts, lse, attended,
                middle, normed_mlp, gate, up, mixed,
            )
            if layer < layer_n - 1:
                keep, got, at = yield from scatter(keep, send, at)
                at = yield "finish_norm", at, 0
                state, low = finish_norm(middle, keep, got, weights[layer + 1][4])
                own, got, at = yield from gather(low, at)
                parts = (own, got)
            else:
                more.append(last_rows(micro, middle, keep, send))
        carry = lax.dynamic_slice_in_dim(cotangent[micro], quarter * share, share, 0).astype(f32)
        downs = (cotangent[micro],)
        for layer in reversed(range(layer_n)):
            if layer == 0:
                order.scale = 2
            bias, gain1, gain2 = weights[layer][3:]
            w_attn, w_in, w_dn = settled[layer]
            (
                state, normed, query, kv_parts, lse, attended,
                middle, normed_mlp, gate, up, mixed,
            ) = kept[layer, micro]
            at = yield "mlp_back", at, 1.5 + 0.1 * micro
            outs = mlp_back(place, downs, gate, up, w_in, w_dn)
            dgate, dup, keep, send = outs[:4]
            full_down = outs[4] if len(outs) == 5 else downs[0]
            slots[layer, micro, "mlp"] = (full_down, dgate, dup)
            marks.add(("mlp_back", layer, micro))
            keep, got, at = yield from scatter(keep, send, at)
            at = yield "finish_back", at, 0
            mid, low, term2 = finish_back(carry, keep, got, middle, gain2)
            own, got, at = yield from gather(low, at)
            at = yield "attend_back", at, 2
            full_out, dquery, keep, send = attend_back(
                place, own, got, query, kv_parts, visible, lse, cos_wide, sin_wide,
                w_attn, heads, hd,
            )
            marks.add(("attend_back", layer, micro))
            slots[layer, micro, "out"] = (full_out,)
            got = swap(send, "seq", 1)
            at = yield "fold", order.link("core", "core", at), 0
            keep, send = fold(place, place.at["chip"] + 1, keep, got)
            got = swap(send, "seq", 2)
            marks.add(("kv", layer, micro))
            at = yield "lin_back", order.link("kv", "kv", at), 1
            dlin, sums, keep, send = lin_back(
                place, dquery, keep, got, cos_wide, sin_wide, w_attn, heads, hd, width
            )
            slots[layer, micro, "lin"] = (dlin,)
            marks.add(("lin_back", layer, micro))
            keep, got, at = yield from scatter(keep, send, at)
            at = yield "finish_back", at, 0
            marks.add(("finish_back", layer, micro))
            carry, low, term1 = finish_back(mid, keep, got, state, gain1)
            slots[layer, micro, "small"] = (term1, term2, sums)
            own, got, at = yield from gather(low, at)
            downs = (own, got)
        if micro == micro_n - 1:
            marks.add("end")
        yield "join", at, 1
        late = grads[0, "gate"] if micro == micro_n - 1 else ()
        tails[micro] = join(place, "half", *downs, deps=late)

    def reduce_links(layer, name, keep, send, flip, at):
        links = fabric(not flip)[:-1] + fabric(flip)[-1:]
        axis, bit = links[-1]
        got = swap(send, axis, bit)
        busy["core"] += 1
        at = order.link("core_w", "core", at)
        for n, (axis, bit) in enumerate(links[:-1][::-1]):
            after = ("kv", layer, micro_n - 1)
            ready = lambda at=at, axis=axis, n=n: (
                max(at, order.free.get(axis, 0.0) - 4.0)
                if (axis != "seq" or after in marks) and (n or busy["row"] < 2)
                else None
            )
            at = yield "fold_rows", ready, 1
            if n == 0:
                busy["core"] -= 1
                busy["row"] += 1
            keep, send = fold_rows(keep, got)
            got = swap(send, axis, bit)
            kind = ("row2" if n == 0 else "row1") + ("" if keep.shape[1] > width else "_small")
            at = order.link(kind, axis, at)
        yield "combine", at, 1
        busy["row"] -= 1
        grads[layer, name] = (combine(keep, got),)

    def finishes():
        jobs = [
            ("down", ("down", 0), ("down", 0), w_gate.shape[2], units),
            ("gate", ("gate", 0), ("gate", 0), w_gate.shape[2], units),
            ("up", ("up", 0), ("up", 0), w_gate.shape[2], units),
            ("out", ("attn", 0), ("attn", 0), q_cols, q_cols),
            ("lin", ("attn", 1), ("attn", 1), q_cols, q_cols),
        ]
        for name, (first, first_at), (second, second_at), cols, window in jobs:
            keys = ((0, first), (1, second))
            yield "finish_grads", (
                lambda keys=keys: 0.0 if all(key in grads for key in keys) and "end" in marks else None
            ), 7
            layers = [(grads[keys[0]], first_at), (grads[keys[1]], second_at)]
            finished[name] = finish_grads(layers, cols, window)

    def fillers(layer):
        trees = range(micro_n)
        saved = lambda n: [kept[layer, micro][n] for micro in trees]
        side = lambda kind, n: [slots[layer, micro, kind][n] for micro in trees]
        done = lambda kind: (
            lambda: 0.0 if all((layer, micro, kind) in slots for micro in trees) else None
        )
        near = lambda key: (lambda: 0.0 if (key, layer, micro_n - 1) in marks else None)

        def reduce_grad(name, pairs, flip, at):
            if name in offloaded[layer]:
                (total,) = weight_grad(place, pairs, None)
                grads[layer, name] = (
                    lax.psum_scatter(total, both, scatter_dimension=0, tiled=True),
                )
                return
            keep, send = weight_grad(place, pairs, place.at["grads", flip])
            more.append(reduce_links(layer, name, keep, send, flip, at))

        down = lambda: [(side("mlp", 0), saved(10))]
        gate = lambda: [(saved(7), side("mlp", 1))]
        up = lambda: [(saved(7), side("mlp", 2))]
        out = lambda: [(side("out", 0), saved(5))]
        lin = lambda: [(saved(1), side("lin", 0))]
        free = lambda test: (
            lambda: 0.0 if test() is not None and busy["core"] == 0 else None
        )
        at = yield "weight_grad", done("mlp"), 5
        reduce_grad("down", down(), True, at)
        if layer > 0:
            at = yield "weight_grad", free(lambda: 0.0), 5
            reduce_grad("up", up(), True, at)
            at = yield "weight_grad", free(near("kv")), 3
            reduce_grad("gate", gate(), False, at)
            at = yield "weight_grad_small", free(done("lin")), 4
        else:
            at = yield "weight_grad", 0.0, 5
            reduce_grad("gate", gate(), False, at)
            at = yield "weight_grad", 0.0, 5
            reduce_grad("up", up(), True, at)
            at = yield "weight_grad_small", done("lin"), 0
        reduce_grad("attn", out() + lin(), True, at)

    def cross_sums():
        keys = [(layer, "attn") for layer in range(layer_n)]
        at = yield "kv_pick", (lambda: 0.0 if all(key in grads for key in keys) else None), 0.5
        parts = [grads[key][0] for key in keys]
        dims = (layer_n * shard, 2 * hd)
        total, low = call(
            functools.partial(kv_pick_kernel, 2 * q_cols),
            "kv_pick",
            (shape(dims, f32), shape(dims, bf16)),
            [LOAD] * len(parts),
            tuple(parts),
        )
        got = swap(low, "tensor", 1)
        at = yield "kv_add", order.link("core", "kv", at) + 2.0, 0.5
        total, low = call(
            kv_add_kernel, "kv_add", (shape(dims, f32), shape(dims, bf16)), [VMEM, VMEM],
            (total, got),
        )
        got = swap(low, "tensor", 2)
        yield "kv_place", order.link("core", "kv", at) + 3.0, 0.5
        out = shape((layer_n, shard, kv_heads * hd), f32)
        finished["kv"] = call(
            functools.partial(kv_place_kernel, place.at["quarter"]),
            "kv_place", (out, out), [SMEM, VMEM, VMEM], (place.table, total, got),
        )

    def small_sums():
        keys = [(layer, micro, "small") for layer in range(layer_n) for micro in range(micro_n)]
        at = yield "small", (lambda: 0.0 if all(key in slots for key in keys) else None), 0.5
        parts = [slots[key][n] for n in range(3) for key in keys]
        total = call(
            functools.partial(small_kernel, place, layer_n, micro_n, hd),
            "small",
            shape((4 * layer_n, width), f32),
            [SMEM] + [LOAD] * len(parts),
            (place.table, *parts),
        )
        for axis, bit in fabric(False)[::-1] + [("tensor", 1), ("tensor", 2)]:
            got = swap(total, axis, bit)
            at = yield "add", order.link("hop", "small", at), 0.5
            total = call(add_kernel, "add", shape(total.shape, f32), [VMEM, VMEM], (total, got))
        grads["small"] = total

    def arrivals():
        names = [("project", 0, micro) for micro in range(micro_n)]
        yield "pack", (lambda: 0.0 if all(name in marks for name in names) else None), 0
        again, far = far_in()
        down = whole(wide(w_down_t))
        at = order.now
        yield "touch", at + 46.0, 0
        arrays, gate, up = corners_in(again, far)
        settled[0] = (attn0, Mixed(arrays, gate, up, shard), Weight(down, shard, False))
        half = len(arrays) // 2
        arrive[0, "mlp"] = at + 75.0
        yield "touch", at + 58.0, 1
        touch(arrays[half : half + 3])
        yield "touch", at + 73.0, 1
        touch(arrays[half + 3 :])
        yield "pack", at + 71.0, 1
        attn, wide_all = second_layer()
        settled[1] = (
            Weight(attn, shard, False),
            Weight(wide_all, 3 * shard, False),
            Weight(wide_all, 3 * shard, False, 2 * shard),
        )

    more = []
    order.run([tree(micro) for micro in range(micro_n)] + [fillers(1), fillers(0), small_sums(), arrivals(), finishes(), cross_sums()], more)
    hidden_out = jnp.stack(finals)
    input_grad = jnp.stack(tails).astype(f32)

    names = ("gate", "up", "down", "lin", "out")
    gate_g, up_g, down_g, query_g, out_g = (finished[name] for name in names)
    key_g, value_g = finished["kv"]
    total = grads["small"]
    block = place.leaf_i * place.seq_n + place.seq_i
    gains = lax.dynamic_slice(total, (0, block * shard), (2 * layer_n, shard))
    cut = lambda a: lax.dynamic_slice_in_dim(a, block * bias_cols, bias_cols, a.ndim - 1)
    bq = total[2 * layer_n : 3 * layer_n].reshape(layer_n, tensor_n, heads, hd)
    bq = cut(lax.dynamic_index_in_dim(bq, place.tensor_i, 1, keepdims=False))
    kv_row = total[3 * layer_n :]
    bk = cut(kv_row[:, : 2 * hd].reshape(layer_n, 2, hd))
    bv = cut(kv_row[:, 2 * hd : 4 * hd].reshape(layer_n, 2, hd))
    return (
        hidden_out,
        input_grad,
        gains[:layer_n],
        query_g,
        bq,
        key_g,
        bk,
        value_g,
        bv,
        jnp.swapaxes(out_g, 1, 2),
        gains[layer_n:],
        gate_g,
        up_g,
        jnp.swapaxes(down_g, 1, 2),
    )


def solution(mesh):
    both = ("leaf", "seq")
    return jax.shard_map(
        body,
        mesh=mesh,
        in_specs=(
            P("leaf", "seq", None),
            P("leaf", None),
            P("leaf", "seq", None),
            P(None, both),
            P(None, both, "tensor"),
            P(None, "tensor", both),
            P(None, both, None),
            P(None, None, both),
            P(None, both, None),
            P(None, None, both),
            P(None, "tensor", both),
            P(None, both),
            P(None, both, "tensor"),
            P(None, both, "tensor"),
            P(None, "tensor", both),
        ),
        out_specs=(
            P("leaf", "seq", None),
            P("leaf", "seq", None),
            P(None, both),
            P(None, both, "tensor"),
            P(None, "tensor", both),
            P(None, both, None),
            P(None, None, both),
            P(None, both, None),
            P(None, None, both),
            P(None, "tensor", both),
            P(None, both),
            P(None, both, "tensor"),
            P(None, both, "tensor"),
            P(None, "tensor", both),
        ),
        check_vma=False,
    )
```

```python
import functools
import math

import jax
import jax.numpy as jnp
from jax import lax
from jax.experimental import pallas as pl
from jax.experimental.pallas import tpu as pltpu
from jax.sharding import PartitionSpec as P

BLK = 128
NBLK = 8
PAD = 16
COST = 16
TIMES = {
    "entry": 2.5,
    "mlp": 14,
    "mlp_back": 15,
    "attend": 5,
    "attend_back": 7.5,
    "lin_back": 4.5,
    "project": 4.2,
    "weight_grad": 9,
    "fold_rows": 3,
    "weight_grad_small": 4,
    "weight_grad_two": 17,
    "fold": 1.3,
    "join": 1.2,
    "add": 1.0,
    "finish_grads": 3,
}
START = 1.5
LINKS = {"z1": 11.0, "z2": 12.0, "kv": 6.5, "core": 3.0, "core_w": 9.0, "row2": 46, "row1": 25, "hop": 3.0,
         "row2_small": 21.0, "row1_small": 12.0}


def cost(name):
    return pl.CostEstimate(
        flops=int(TIMES.get(name, 2) * ORDER[0].scale * 1.15e9), bytes_accessed=1000, transcendentals=0
    )


class Order:
    def __init__(self):
        self.last = None
        self.now = 0.0
        self.free = {}
        self.scale = COST

    def link(self, kind, wire, at):
        begin = max(at, self.free.get(wire, 0.0))
        end = begin + LINKS[kind]
        self.free[wire] = end - 2.0
        self.now += START
        return end

    def took(self, outs):
        self.last = min(outs, key=lambda a: math.prod(a.shape))

    def run(self, tasks, more):
        waiting = [[task, next(task)] for task in tasks]
        while waiting or more:
            while more:
                task = more.pop()
                waiting.append([task, next(task)])
            ready = []
            for entry_ in waiting:
                name, when, rank = entry_[1]
                when = when() if callable(when) else when
                if when is not None:
                    ready.append((entry_, name, when, rank))
            soonest = min(when for _, _, when, _ in ready)
            self.now = max(self.now, soonest)
            chosen = min(
                (item for item in ready if item[2] <= self.now), key=lambda item: (item[3], item[2])
            )
            self.now += TIMES.get(chosen[1], 2.0)
            try:
                chosen[0][1] = chosen[0][0].send(self.now)
            except StopIteration:
                waiting.remove(chosen[0])


ORDER = [Order()]


eps_norm = 1e-06
rope_base = 1000000.0
neg_fill = -1e30

f32 = jnp.float32
bf16 = jnp.bfloat16

ANY = pl.BlockSpec(memory_space=pl.ANY)
HBM = pl.BlockSpec(memory_space=pltpu.HBM)
LOAD = pl.BlockSpec(memory_space=pltpu.HBM)
STORE = pl.BlockSpec(memory_space=pltpu.HBM)
VMEM = pl.BlockSpec(memory_space=pltpu.VMEM)
SMEM = pl.BlockSpec(memory_space=pltpu.SMEM)


def dot(left_op, right_op):
    return jnp.dot(left_op, right_op, preferred_element_type=f32)


def dot_left(left_op, right_op):
    return lax.dot_general(
        left_op, right_op, (((0,), (0,)), ((), ())), preferred_element_type=f32
    )


def dot_right(left_op, right_op):
    return lax.dot_general(
        left_op, right_op, (((1,), (1,)), ((), ())), preferred_element_type=f32
    )


def spans(total, step):
    return [(at, min(step, total - at)) for at in range(0, total, step)]


def shape(dims, dtype):
    return jax.ShapeDtypeStruct(tuple(dims), dtype)


EARLY = []


def flush(ref):
    for item in EARLY[-1]:
        if item[0] is ref and not item[2]:
            item[1].start()
            item[2] = True


def call(kernel, name, out_shape, in_specs, operands, scratch=(), out_specs=None, deps=(), **more):
    several = isinstance(out_shape, tuple)
    outs = out_shape if several else (out_shape,)
    if out_specs is None:
        out_specs = tuple(VMEM for _ in outs)
    order = ORDER[0]
    if order.last is not None:
        deps = tuple(deps) + (order.last,)
    count = len(operands)
    size = lambda a: math.prod(a.shape) * jnp.dtype(a.dtype).itemsize
    token = not any(spec is VMEM for spec in out_specs)
    if token:
        out_shape = outs = tuple(outs) + (shape((8, 128), f32),)
        spec = pl.BlockSpec((8, 128), lambda i: (0, 0)) if "grid" in more else VMEM
        out_specs = tuple(out_specs) + (spec,)
        plain = kernel

        def kernel(*refs):
            mark = refs[count + len(outs) - 1]
            mark[...] = jnp.zeros(mark.shape, f32)
            plain(*refs[: count + len(outs) - 1], *refs[count + len(outs) :])

    if "grid" in more:
        room = 24 << 20
        loads, stores = [], []
    else:
        loads = [n for n, spec in enumerate(in_specs) if spec is LOAD]
        stores = [n for n, spec in enumerate(out_specs) if spec is STORE]
        fast = (VMEM, LOAD, STORE)
        room = sum(size(a) for a, spec in zip(operands, in_specs) if spec in fast)
        room += sum(size(a) for a, spec in zip(outs, out_specs) if spec in fast)
        room += sum(size(a) for a in scratch if a.memory_space == pltpu.VMEM)
        room = min(58 << 20, room + room // 2 + (6 << 20))
    moved = [operands[n] for n in loads] + [outs[n] for n in stores]
    extra = [pltpu.VMEM(a.shape, a.dtype) for a in moved]
    if moved:
        extra.append(pltpu.SemaphoreType.DMA((len(moved),)))

    def wrapped(*refs):
        ins, rest = list(refs[:count]), refs[count + len(deps) :]
        results, rest = list(rest[: len(outs)]), rest[len(outs) :]
        inner, rest = rest[: len(scratch)], rest[len(scratch) :]
        copies, items = [], []
        for k, n in enumerate(loads):
            copies.append(pltpu.make_async_copy(ins[n], rest[k], rest[-1].at[k]))
            ins[n] = rest[k]
        for copy in copies:
            copy.start()
        for k, n in enumerate(stores, len(loads)):
            items.append([rest[k], pltpu.make_async_copy(rest[k], results[n], rest[-1].at[k]), False])
            results[n] = rest[k]
        for copy in copies:
            copy.wait()
        EARLY.append(items)
        kernel(*ins, *results, *inner)
        EARLY.pop()
        for item in items:
            if not item[2]:
                item[1].start()
        for item in items:
            item[1].wait()

    made = pl.pallas_call(
        wrapped,
        out_shape=outs,
        in_specs=list(in_specs) + [ANY] * len(deps),
        out_specs=tuple(out_specs),
        scratch_shapes=list(scratch) + extra,
        compiler_params=pltpu.CompilerParams(vmem_limit_bytes=room),
        cost_estimate=cost(name),
        name=name,
        **more,
    )(*operands, *deps)
    order.took(made)
    if token:
        made = made[:-1]
    return made if several else made[0]


def swap(array, axis, bit):
    size = lax.axis_size(axis)
    return lax.ppermute(array, axis, [(i, i ^ bit) for i in range(size)])


def axis_bits(axis):
    size = lax.axis_size(axis)
    return [1 << k for k in range(size.bit_length() - 1)]


def fabric(flip):
    seq_bits = axis_bits("seq")
    outer = [("seq", bit) for bit in seq_bits[1:]] + [("leaf", bit) for bit in axis_bits("leaf")]
    return (outer[::-1] if flip else outer) + [("seq", seq_bits[0])]


def gather_pieces(own, flip):
    pieces = [own]
    for axis, bit in fabric(flip):
        pieces = pieces + [swap(piece, axis, bit) for piece in pieces]
    return pieces


class Place:
    def __init__(self):
        self.tensor_i = lax.axis_index("tensor")
        self.seq_i = lax.axis_index("seq")
        self.leaf_i = lax.axis_index("leaf")
        self.seq_n = lax.axis_size("seq")
        self.leaf_n = lax.axis_size("leaf")
        self.blocks = self.seq_n * self.leaf_n
        values = [self.tensor_i & 1, self.tensor_i >> 1]
        self.at = {"half": 0, "quarter": 1}
        for flip in (False, True):
            self.at["blocks", flip] = len(values)
            values += self.homes(fabric(flip))
            self.at["grads", flip] = len(values)
            values += self.homes(fabric(not flip)[:-1] + fabric(flip)[-1:])
        self.at["seq"] = len(values)
        values += self.seq_homes()
        self.at["chip"] = len(values)
        values += [self.seq_i & 1, self.seq_i >> 1]
        self.table = jnp.stack([jnp.asarray(v, jnp.int32) for v in values])

    def homes(self, links):
        out = []
        for p in range(1 << len(links)):
            seq_rel = sum(b for k, (a, b) in enumerate(links) if a == "seq" and p >> k & 1)
            leaf_rel = sum(b for k, (a, b) in enumerate(links) if a == "leaf" and p >> k & 1)
            out.append((self.leaf_i ^ leaf_rel) * self.seq_n + (self.seq_i ^ seq_rel))
        return out

    def seq_homes(self):
        out = [self.seq_i]
        for bit in axis_bits("seq")[::-1]:
            out = out + [h ^ bit for h in out]
        return out


class Weight:
    def __init__(self, arrays, rows, flip, first=0):
        self.arrays = list(arrays)
        self.rows = rows
        self.flip = flip
        self.first = first

    def source(self, place, scal, refs, block, skip, rows, cols):
        skip = skip + self.first
        if len(self.arrays) == 1:
            return refs[0].at[pl.ds(block * self.rows + skip, rows), cols], block
        home = scal[place.at["blocks", self.flip] + block]
        return refs[block].at[pl.ds(skip, rows), cols], home

    def halves(self, place, scal, refs, buf, sems, skip=0):
        mid = buf.shape[1] // 256 * 128
        parts = (slice(0, mid), slice(mid, buf.shape[1]))
        return [
            self.copies(
                place, scal, refs, buf.at[:, part], sems.at[n], skip=skip, cols=part
            )
            for n, part in enumerate(parts)
        ]

    def copies(self, place, scal, refs, buf, sems, skip=0, cols=slice(None)):
        rows = buf.shape[0] // place.blocks
        out = []
        for block in range(place.blocks):
            src, home = self.source(place, scal, refs, block, skip, rows, cols)
            if not isinstance(home, int):
                home = pl.multiple_of(home * rows, PAD)
            else:
                home = home * rows
            out.append(pltpu.make_async_copy(src, buf.at[pl.ds(home, rows)], sems.at[block]))
        return out


def row_spot(index, rows):
    return pl.ds(pl.multiple_of(index * rows, PAD), rows)


def put_halves(place, scal, buf, own_ref, got_ref):
    half = own_ref.shape[0]
    which = scal[place.at["half"]]
    buf[row_spot(which, half), :] = own_ref[...]
    buf[row_spot(1 - which, half), :] = got_ref[...]


def fold_kernel(spot, scal, keep_ref, got_ref, next_keep, next_send):
    rows = next_keep.shape[0]
    which = scal[spot]
    mine = row_spot(which, rows)
    away = row_spot(1 - which, rows)
    next_keep[...] = keep_ref[mine, :] + got_ref[mine, :].astype(f32)
    next_send[...] = (keep_ref[away, :] + got_ref[away, :].astype(f32)).astype(bf16)


def fold(place, spot, keep, got):
    rows, cols = keep.shape
    return call(
        functools.partial(fold_kernel, place.at[spot] if isinstance(spot, str) else spot),
        "fold",
        (shape((rows // 2, cols), f32), shape((rows // 2, cols), bf16)),
        [SMEM, VMEM, VMEM],
        (place.table, keep, got),
    )


def join_kernel(spot, scal, own_ref, got_ref, out_ref):
    rows = own_ref.shape[0]
    which = scal[spot]
    out_ref[row_spot(which, rows), :] = own_ref[...]
    out_ref[row_spot(1 - which, rows), :] = got_ref[...]


def join(place, spot, own, got, deps=()):
    rows, cols = own.shape
    return call(
        functools.partial(join_kernel, place.at[spot]),
        "join",
        shape((2 * rows, cols), own.dtype),
        [SMEM, VMEM, VMEM],
        (place.table, own, got),
        deps=deps,
    )


def normed_rows(values, gain):
    inv = lax.rsqrt(jnp.mean(values * values, axis=1, keepdims=True) + eps_norm)
    return (values * inv * gain).astype(bf16)


def entry_kernel(place, scal, x_ref, gain_ref, share_ref, normed_ref):
    rows = share_ref.shape[0]
    values = x_ref[...].astype(f32)
    normed_ref[...] = normed_rows(values, gain_ref[...])
    spot = scal[place.at["half"]] * 2 + scal[place.at["quarter"]]
    share_ref[...] = x_ref[row_spot(spot, rows), :].astype(f32)


def entry(place, hidden, gain, share):
    rows, width = hidden.shape
    return call(
        functools.partial(entry_kernel, place),
        "entry",
        (shape((share, width), f32), shape((rows, width), bf16)),
        [SMEM, LOAD, VMEM],
        (place.table, hidden, gain),
        out_specs=(VMEM, STORE),
    )


def finish_norm_kernel(base_ref, keep_ref, got_ref, gain_ref, sum_ref, normed_ref):
    total = base_ref[...] + (keep_ref[...] + got_ref[...].astype(f32))
    sum_ref[...] = total
    normed_ref[...] = normed_rows(total, gain_ref[...])


def finish_norm(base, keep, got, gain):
    return call(
        finish_norm_kernel,
        "finish_norm",
        (shape(base.shape, f32), shape(base.shape, bf16)),
        [LOAD, VMEM, VMEM, VMEM],
        (base, keep, got, gain),
        out_specs=(STORE, VMEM),
    )


def finish_plain_kernel(base_ref, keep_ref, got_ref, out_ref):
    out_ref[...] = (base_ref[...] + (keep_ref[...] + got_ref[...].astype(f32))).astype(bf16)


def finish_plain(base, keep, got):
    return call(
        finish_plain_kernel, "finish_plain", shape(base.shape, bf16), [LOAD, VMEM, VMEM], (base, keep, got)
    )


def finish_back_kernel(carry_ref, keep_ref, got_ref, src_ref, gain_ref, grad_ref, low_ref, term_ref):
    dnorm = keep_ref[...] + got_ref[...].astype(f32)
    source = src_ref[...]
    inv = lax.rsqrt(jnp.mean(source * source, axis=1, keepdims=True) + eps_norm)
    term_ref[...] = jnp.sum(dnorm * source * inv, axis=0, keepdims=True)
    scaled = dnorm * gain_ref[...]
    back = jnp.mean(scaled * source, axis=1, keepdims=True)
    grad = carry_ref[...] + inv * scaled - source * (inv * inv * inv) * back
    grad_ref[...] = grad
    low_ref[...] = grad.astype(bf16)


def finish_back(carry, keep, got, source, gain):
    width = carry.shape[1]
    return call(
        finish_back_kernel,
        "finish_back",
        (shape(carry.shape, f32), shape(carry.shape, bf16), shape((1, width), f32)),
        [LOAD, VMEM, VMEM, LOAD, VMEM],
        (carry, keep, got, source, gain),
        out_specs=(STORE, VMEM, STORE),
    )


def split_rows(place, scal, total_ref, keep_ref, send_ref):
    half = keep_ref.shape[0]
    which = scal[place.at["half"]]
    keep_ref[...] = total_ref[row_spot(which, half), :]
    send_ref[...] = total_ref[row_spot(1 - which, half), :].astype(bf16)


def project_kernel(place, weight, heads, hd, parts, *refs):
    scal, refs = refs[0], refs[1:]
    x_refs, refs = refs[:parts], refs[parts:]
    bias_ref, cos_ref, sin_ref = refs[:3]
    refs = refs[3:]
    w_refs, refs = refs[: len(weight.arrays)], refs[len(weight.arrays) :]
    q_ref, kv_ref, refs = refs[0], refs[1], refs[2:]
    if parts == 2:
        x_out, refs = refs[0], refs[1:]
    buf, sems = refs
    cols = (heads + 2) * hd
    copies = weight.copies(place, scal, w_refs, buf, sems, cols=slice(0, cols))
    for copy in copies:
        copy.start()
    if parts == 2:
        put_halves(place, scal, x_out, *x_refs)
        values = x_out[...]
    else:
        values = x_refs[0][...]
    for copy in copies:
        copy.wait()
    cos_wide = cos_ref[...]
    sin_wide = sin_ref[...]
    lin = dot(values, buf[...]) + bias_ref[...]
    for h in range(heads + 1):
        part = lin[:, h * hd : (h + 1) * hd]
        turned = part * cos_wide + pltpu.roll(part, hd // 2, 1) * sin_wide
        if h < heads:
            q_ref[:, h * hd : (h + 1) * hd] = turned.astype(bf16)
        else:
            kv_ref[:, :hd] = turned.astype(bf16)
    kv_ref[:, hd:] = lin[:, (heads + 1) * hd :].astype(bf16)


def project(place, x_parts, weight, bias, cos_wide, sin_wide, heads, hd):
    rows = sum(part.shape[0] for part in x_parts)
    width = x_parts[0].shape[1]
    cols = (heads + 2) * hd
    outs = [shape((rows, heads * hd), bf16), shape((rows, 2 * hd), bf16)]
    if len(x_parts) == 2:
        outs.append(shape((rows, width), bf16))
    return call(
        functools.partial(project_kernel, place, weight, heads, hd, len(x_parts)),
        "project",
        tuple(outs),
        [SMEM] + [LOAD if len(x_parts) == 1 else VMEM] * len(x_parts) + [VMEM, LOAD, LOAD]
        + [ANY] * len(weight.arrays),
        (place.table, *x_parts, bias, cos_wide, sin_wide, *weight.arrays),
        [pltpu.VMEM((width, cols), bf16), pltpu.SemaphoreType.DMA((place.blocks,))],
        out_specs=(STORE, VMEM) + (STORE,) * (len(outs) - 2),
    )


def put_keys(place, scal, buf, kv_refs):
    rows = kv_refs[0].shape[0]
    for n, ref in enumerate(kv_refs):
        buf[row_spot(scal[place.at["seq"] + n], rows), :] = ref[...]


def attend_kernel(place, weight, heads, hd, *refs):
    scal, q_ref, vis_ref, refs = refs[0], refs[1], refs[2], refs[3:]
    kv_refs, refs = refs[: place.seq_n], refs[place.seq_n :]
    w_refs, refs = refs[: len(weight.arrays)], refs[len(weight.arrays) :]
    o_ref, lse_ref, keep_ref, send_ref, kv_buf, w_buf, total_buf, sems = refs
    cols = slice((heads + 2) * hd, (2 * heads + 2) * hd)
    copies = weight.copies(place, scal, w_refs, w_buf, sems, cols=cols)
    for copy in copies:
        copy.start()
    put_keys(place, scal, kv_buf, kv_refs)
    keys = kv_buf[:, :hd]
    values = kv_buf[:, hd:]
    seen = vis_ref[...] > 0.5
    scale = 1.0 / math.sqrt(hd)
    lane = lax.broadcasted_iota(jnp.int32, lse_ref.shape, 1)
    lse_all = jnp.zeros(lse_ref.shape, f32)
    for h in range(heads):
        spot = slice(h * hd, (h + 1) * hd)
        scores = dot_right(q_ref[:, spot], keys) * scale
        scores = jnp.where(seen, scores, neg_fill)
        top = jnp.max(scores, axis=1, keepdims=True)
        expo = jnp.exp(scores - top)
        total = jnp.sum(expo, axis=1, keepdims=True)
        prob = (expo * (1.0 / total)).astype(bf16)
        o_ref[:, spot] = dot(prob, values).astype(bf16)
        lse_all = jnp.where(lane == h, top + jnp.log(total), lse_all)
    lse_ref[...] = lse_all
    flush(o_ref)
    flush(lse_ref)
    for copy in copies:
        copy.wait()
    for at, size in spans(w_buf.shape[0], 512):
        total_buf[:, at : at + size] = dot_right(o_ref[...], w_buf[at : at + size, :])
    split_rows(place, scal, total_buf, keep_ref, send_ref)


def attend(place, query, kv_parts, visible, weight, heads, hd, width):
    rows = query.shape[0]
    keys = visible.shape[1]
    half = rows // 2
    return call(
        functools.partial(attend_kernel, place, weight, heads, hd),
        "attend",
        (
            shape((rows, heads * hd), bf16),
            shape((rows, 128), f32),
            shape((half, width), f32),
            shape((half, width), bf16),
        ),
        [SMEM, LOAD, LOAD] + [VMEM] * len(kv_parts) + [ANY] * len(weight.arrays),
        (place.table, query, visible, *kv_parts, *weight.arrays),
        [
            pltpu.VMEM((keys, 2 * hd), bf16),
            pltpu.VMEM((width, heads * hd), bf16),
            pltpu.VMEM((rows, width), f32),
            pltpu.SemaphoreType.DMA((place.blocks,)),
        ],
        out_specs=(STORE, STORE, VMEM, VMEM),
    )


def attend_back_kernel(place, weight, heads, hd, *refs):
    (scal, own_ref, got_ref, q_ref, vis_ref, lse_ref, cos_ref, sin_ref), refs = refs[:8], refs[8:]
    kv_refs, refs = refs[: place.seq_n], refs[place.seq_n :]
    w_refs, refs = refs[: len(weight.arrays)], refs[len(weight.arrays) :]
    full_ref, dq_ref, keep_ref, send_ref, kv_buf, w_buf, do_buf, dkv_buf, sems = refs
    cols = slice((heads + 2) * hd, (2 * heads + 2) * hd)
    copies = weight.copies(place, scal, w_refs, w_buf, sems, cols=cols)
    for copy in copies:
        copy.start()
    put_halves(place, scal, full_ref, own_ref, got_ref)
    flush(full_ref)
    put_keys(place, scal, kv_buf, kv_refs)
    keys = kv_buf[:, :hd]
    values = kv_buf[:, hd:]
    seen = vis_ref[...] > 0.5
    cos_wide = cos_ref[...]
    sin_wide = sin_ref[...]
    scale = 1.0 / math.sqrt(hd)
    for copy in copies:
        copy.wait()
    do_buf[...] = dot(full_ref[...], w_buf[...]).astype(bf16)
    for h in range(heads):
        spot = slice(h * hd, (h + 1) * hd)
        query = q_ref[:, spot]
        dout = do_buf[:, spot]
        scores = dot_right(query, keys) * scale
        scores = jnp.where(seen, scores, neg_fill)
        prob = jnp.exp(scores - lse_ref[:, h : h + 1])
        dprob = dot_right(dout, values)
        delta = jnp.sum(prob * dprob, axis=1, keepdims=True)
        dscore = (prob * (dprob - delta)).astype(bf16)
        dquery = dot(dscore, keys) * scale
        dquery = dquery * cos_wide - pltpu.roll(dquery, hd // 2, 1) * sin_wide
        dq_ref[:, spot] = dquery.astype(bf16)
        dk_part = dot_left(dscore, query) * scale
        dv_part = dot_left(prob.astype(bf16), dout)
        if h == 0:
            dkv_buf[:, :hd] = dk_part
            dkv_buf[:, hd:] = dv_part
        else:
            dkv_buf[:, :hd] += dk_part
            dkv_buf[:, hd:] += dv_part
    rows = kv_refs[0].shape[0]
    core = scal[place.at["chip"]]
    for n in range(place.seq_n // 2):
        spot = slice(n * rows, (n + 1) * rows)
        keep_ref[spot, :] = dkv_buf[row_spot(2 * n + core, rows), :]
        send_ref[spot, :] = dkv_buf[row_spot(2 * n + 1 - core, rows), :].astype(bf16)


def attend_back(place, own, got, query, kv_parts, visible, lse, cos_wide, sin_wide, weight, heads, hd, deps=()):
    rows = query.shape[0]
    keys = visible.shape[1]
    width = own.shape[1]
    return call(
        functools.partial(attend_back_kernel, place, weight, heads, hd),
        "attend_back",
        (
            shape((rows, width), bf16),
            shape((rows, heads * hd), bf16),
            shape((keys // 2, 2 * hd), f32),
            shape((keys // 2, 2 * hd), bf16),
        ),
        [SMEM, VMEM, VMEM] + [LOAD] * (5 + len(kv_parts)) + [ANY] * len(weight.arrays),
        (place.table, own, got, query, visible, lse, cos_wide, sin_wide, *kv_parts, *weight.arrays),
        [
            pltpu.VMEM((keys, 2 * hd), bf16),
            pltpu.VMEM((width, heads * hd), bf16),
            pltpu.VMEM((rows, heads * hd), bf16),
            pltpu.VMEM((keys, 2 * hd), f32),
            pltpu.SemaphoreType.DMA((place.blocks,)),
        ],
        out_specs=(STORE, STORE, VMEM, VMEM),
        deps=deps,
    )


def lin_back_kernel(place, weight, heads, hd, *refs):
    (scal, dq_ref, dkv_ref, got_ref, cos_ref, sin_ref), refs = refs[:6], refs[6:]
    w_refs, refs = refs[: len(weight.arrays)], refs[len(weight.arrays) :]
    dlin_ref, sums_ref, keep_ref, send_ref, w_buf, total_buf, sems = refs
    cols = (heads + 2) * hd
    copies = weight.copies(place, scal, w_refs, w_buf, sems, cols=slice(0, cols))
    for copy in copies:
        copy.start()
    dkv = dkv_ref[...] + got_ref[...].astype(f32)
    dkey = dkv[:, :hd]
    dkey = dkey * cos_ref[...] - pltpu.roll(dkey, hd // 2, 1) * sin_ref[...]
    dlin_ref[:, : heads * hd] = dq_ref[...]
    dlin_ref[:, heads * hd : (heads + 1) * hd] = dkey.astype(bf16)
    dlin_ref[:, (heads + 1) * hd :] = dkv[:, hd:].astype(bf16)
    dlin = dlin_ref[...]
    sums_ref[...] = jnp.sum(dlin.astype(f32), axis=0, keepdims=True)
    flush(dlin_ref)
    for copy in copies:
        copy.wait()
    for at, size in spans(w_buf.shape[0], 512):
        total_buf[:, at : at + size] = dot_right(dlin, w_buf[at : at + size, :])
    split_rows(place, scal, total_buf, keep_ref, send_ref)


def lin_back(place, dquery, dkv, got, cos_wide, sin_wide, weight, heads, hd, width, deps=()):
    rows = dquery.shape[0]
    cols = (heads + 2) * hd
    return call(
        functools.partial(lin_back_kernel, place, weight, heads, hd),
        "lin_back",
        (
            shape((rows, cols), bf16),
            shape((1, cols), f32),
            shape((rows // 2, width), f32),
            shape((rows // 2, width), bf16),
        ),
        [SMEM, LOAD, VMEM, VMEM, LOAD, LOAD] + [ANY] * len(weight.arrays),
        (place.table, dquery, dkv, got, cos_wide, sin_wide, *weight.arrays),
        [
            pltpu.VMEM((width, cols), bf16),
            pltpu.VMEM((rows, width), f32),
            pltpu.SemaphoreType.DMA((place.blocks,)),
        ],
        out_specs=(STORE, STORE, VMEM, VMEM),
        deps=deps,
    )


class Mixed:
    def __init__(self, arrays, gate, up, rows):
        self.arrays = list(arrays)
        self.spots = (gate, up)
        self.rows = rows

    def halves(self, place, scal, refs, buf, sems, skip=0):
        spots = self.spots[1 if skip else 0]
        parts = [refs[n].at[pl.ds(at, self.rows)] for n, at in spots]
        return Weight(parts, self.rows, False).halves(place, scal, parts, buf, sems)


def start_all(copies):
    for copy in copies:
        copy.start()


def wait_all(copies):
    for copy in copies:
        copy.wait()


def mlp_kernel(place, w_in, w_down, *refs):
    (scal, own_ref, got_ref), refs = refs[:3], refs[3:]
    in_refs, refs = refs[: len(w_in.arrays)], refs[len(w_in.arrays) :]
    down_refs, refs = refs[: len(w_down.arrays)], refs[len(w_down.arrays) :]
    (
        full_ref, gate_ref, up_ref, mix_ref, keep_ref, send_ref,
        gate_buf, up_buf, down_buf, total_buf, gate_sems, up_sems, down_sems,
    ) = refs
    shard = gate_buf.shape[0] // place.blocks
    gate_copies = w_in.halves(place, scal, in_refs, gate_buf, gate_sems)
    up_copies = w_in.halves(place, scal, in_refs, up_buf, up_sems, skip=shard)
    down_copies = w_down.halves(place, scal, down_refs, down_buf, down_sems)
    start_all(gate_copies[0])
    put_halves(place, scal, full_ref, own_ref, got_ref)
    flush(full_ref)
    values = full_ref[...]
    units = gate_buf.shape[1]
    mid = units // 256 * 128
    parts = (spans(mid, 384), [(mid + at, size) for at, size in spans(units - mid, 384)])
    start_all(gate_copies[1])
    wait_all(gate_copies[0])
    for n in range(2):
        start_all(up_copies[n])
        for at, size in parts[n]:
            gate_ref[:, at : at + size] = dot(values, gate_buf[:, at : at + size]).astype(bf16)
        wait_all(gate_copies[1] if n == 0 else up_copies[0])
    flush(gate_ref)
    for n in range(2):
        start_all(down_copies[n])
        for at, size in parts[n]:
            spot = slice(at, at + size)
            up = dot(values, up_buf[:, spot])
            gate = gate_ref[:, spot].astype(f32)
            up_ref[:, spot] = up.astype(bf16)
            mix_ref[:, spot] = (gate * jax.nn.sigmoid(gate) * up).astype(bf16)
        wait_all(up_copies[1] if n == 0 else down_copies[0] + down_copies[1])
    flush(up_ref)
    flush(mix_ref)
    mixed = mix_ref[...]
    for at, size in spans(down_buf.shape[0], 512):
        total_buf[:, at : at + size] = dot_right(mixed, down_buf[at : at + size, :])
    split_rows(place, scal, total_buf, keep_ref, send_ref)


def mlp(place, own, got, w_in, w_down):
    half, width = own.shape
    rows = 2 * half
    units = w_in.arrays[0].shape[1]
    dma = pltpu.SemaphoreType.DMA((2, place.blocks))
    return call(
        functools.partial(mlp_kernel, place, w_in, w_down),
        "mlp",
        (
            shape((rows, width), bf16),
            shape((rows, units), bf16),
            shape((rows, units), bf16),
            shape((rows, units), bf16),
            shape((half, width), f32),
            shape((half, width), bf16),
        ),
        [SMEM, VMEM, VMEM] + [ANY] * (len(w_in.arrays) + len(w_down.arrays)),
        (place.table, own, got, *w_in.arrays, *w_down.arrays),
        [
            pltpu.VMEM((width, units), bf16),
            pltpu.VMEM((width, units), bf16),
            pltpu.VMEM((width, units), bf16),
            pltpu.VMEM((rows, width), f32),
            dma,
            dma,
            dma,
        ],
        out_specs=(STORE, STORE, STORE, STORE, VMEM, VMEM),
    )


def mlp_back_kernel(place, w_in, w_down, parts, *refs):
    scal, refs = refs[0], refs[1:]
    d_refs, refs = refs[:parts], refs[parts:]
    gate_ref, up_ref, refs = refs[0], refs[1], refs[2:]
    in_refs, refs = refs[: len(w_in.arrays)], refs[len(w_in.arrays) :]
    down_refs, refs = refs[: len(w_down.arrays)], refs[len(w_down.arrays) :]
    dgate_ref, dup_ref, keep_ref, send_ref, refs = refs[0], refs[1], refs[2], refs[3], refs[4:]
    if parts == 2:
        full_ref, refs = refs[0], refs[1:]
    gate_buf, up_buf, down_buf, total_buf, gate_sems, up_sems, down_sems = refs
    shard = gate_buf.shape[0] // place.blocks
    gate_copies = w_in.halves(place, scal, in_refs, gate_buf, gate_sems)
    up_copies = w_in.halves(place, scal, in_refs, up_buf, up_sems, skip=shard)
    down_copies = w_down.halves(place, scal, down_refs, down_buf, down_sems)
    start_all(down_copies[0])
    if parts == 2:
        put_halves(place, scal, full_ref, *d_refs)
        flush(full_ref)
        values = full_ref[...]
    else:
        values = d_refs[0][...]
    units = gate_buf.shape[1]
    mid = units // 256 * 128
    cuts = (spans(mid, 384), [(mid + at, size) for at, size in spans(units - mid, 384)])
    start_all(down_copies[1])
    wait_all(down_copies[0])
    for n in range(2):
        start_all(gate_copies[n])
        for at, size in cuts[n]:
            spot = slice(at, at + size)
            dmixed = dot(values, down_buf[:, spot])
            gate = gate_ref[:, spot].astype(f32)
            up = up_ref[:, spot].astype(f32)
            sig = jax.nn.sigmoid(gate)
            dgate_ref[:, spot] = (dmixed * up * sig * (1.0 + gate * (1.0 - sig))).astype(bf16)
            dup_ref[:, spot] = (dmixed * (gate * sig)).astype(bf16)
        if n == 0:
            wait_all(down_copies[1])
    start_all(up_copies[0] + up_copies[1])
    flush(dgate_ref)
    flush(dup_ref)
    wait_all(gate_copies[0] + gate_copies[1])
    dgate = dgate_ref[...]
    dup = dup_ref[...]
    for at, size in spans(gate_buf.shape[0], 512):
        spot = slice(at, at + size)
        total_buf[:, spot] = dot_right(dgate, gate_buf[spot, :])
    wait_all(up_copies[0] + up_copies[1])
    for at, size in spans(gate_buf.shape[0], 512):
        spot = slice(at, at + size)
        total_buf[:, spot] += dot_right(dup, up_buf[spot, :])
    split_rows(place, scal, total_buf, keep_ref, send_ref)


def mlp_back(place, d_parts, gate, up, w_in, w_down, deps=()):
    rows = sum(part.shape[0] for part in d_parts)
    width = d_parts[0].shape[1]
    half = rows // 2
    units = gate.shape[1]
    outs = [
        shape((rows, units), bf16),
        shape((rows, units), bf16),
        shape((half, width), f32),
        shape((half, width), bf16),
    ]
    if len(d_parts) == 2:
        outs.append(shape((rows, width), bf16))
    dma = pltpu.SemaphoreType.DMA((2, place.blocks))
    return call(
        functools.partial(mlp_back_kernel, place, w_in, w_down, len(d_parts)),
        "mlp_back",
        tuple(outs),
        [SMEM] + [LOAD if len(d_parts) == 1 else VMEM] * len(d_parts) + [LOAD, LOAD]
        + [ANY] * (len(w_in.arrays) + len(w_down.arrays)),
        (place.table, *d_parts, gate, up, *w_in.arrays, *w_down.arrays),
        [
            pltpu.VMEM((width, units), bf16),
            pltpu.VMEM((width, units), bf16),
            pltpu.VMEM((width, units), bf16),
            pltpu.VMEM((rows, width), f32),
            dma,
            dma,
            dma,
        ],
        out_specs=(STORE, STORE, VMEM, VMEM) + (STORE,) * (len(outs) - 4),
        deps=deps,
    )


def weight_grad_kernel(place, micro_n, pairs, homes, *refs):
    scal, refs = refs[0], refs[1:]
    left_refs = [refs[p * micro_n : (p + 1) * micro_n] for p in range(pairs)]
    refs = refs[pairs * micro_n :]
    right_refs = [refs[p * micro_n : (p + 1) * micro_n] for p in range(pairs)]
    refs = refs[pairs * micro_n :]
    outs = 1 if homes is None else 2
    out_refs, refs = refs[:outs], refs[outs:]
    bufs, sems = refs[:pairs], refs[pairs]
    shard = bufs[0].shape[0] // place.blocks
    half = place.blocks // 2
    copies = []
    at_col = 0
    for p in range(pairs):
        buf = bufs[p]
        cols = buf.shape[1]
        ready = 0
        for at, size in spans(buf.shape[0], 256):
            spot = slice(at, at + size)
            total = None
            for left, right in zip(left_refs[p], right_refs[p]):
                part = dot_left(left[:, spot], right[...])
                total = part if total is None else total + part
            buf[spot, :] = total.astype(bf16)
            while homes is None and (ready + 1) * shard <= at + size:
                src = buf.at[pl.ds(ready * shard, shard)]
                dst = out_refs[0].at[pl.ds(ready * shard, shard), pl.ds(at_col, cols)]
                copies.append(pltpu.make_async_copy(src, dst, sems.at[len(copies)]))
                copies[-1].start()
                ready += 1
        if homes is not None:
            for block in list(range(half, place.blocks)) + list(range(half)):
                home = scal[homes + block]
                src = buf.at[pl.ds(pl.multiple_of(home * shard, PAD), shard)]
                out = out_refs[block // half]
                dst = out.at[pl.ds(block % half * shard, shard), pl.ds(at_col, cols)]
                copies.append(pltpu.make_async_copy(src, dst, sems.at[len(copies)]))
                copies[-1].start()
        at_col += cols
    for copy in copies:
        copy.wait()


def weight_grad(place, pairs, homes, deps=()):
    micro_n = len(pairs[0][0])
    rows, width = pairs[0][0][0].shape
    cols = [rights[0].shape[1] for _, rights in pairs]
    if homes is None:
        outs = (shape((width, sum(cols)), bf16),)
    else:
        outs = (shape((width // 2, sum(cols)), bf16),) * 2
    lefts = [a for left, _ in pairs for a in left]
    rights = [a for _, right in pairs for a in right]
    copies = place.blocks * len(pairs)
    return call(
        functools.partial(weight_grad_kernel, place, micro_n, len(pairs), homes),
        "weight_grad" if sum(cols) > width else "weight_grad_small",
        outs,
        [SMEM] + [LOAD] * (len(lefts) + len(rights)),
        (place.table, *lefts, *rights),
        [pltpu.VMEM((width, c), bf16) for c in cols] + [pltpu.SemaphoreType.DMA((copies,))],
        out_specs=tuple(HBM for _ in outs),
        deps=deps,
    )


def fold_rows_kernel(keep_lo, keep_hi, got_lo, got_hi, keep_ref, send_ref):
    keep_ref[...] = (keep_lo[...].astype(f32) + got_lo[...].astype(f32)).astype(bf16)
    send_ref[...] = (keep_hi[...].astype(f32) + got_hi[...].astype(f32)).astype(bf16)


def fold_rows(keep, got):
    rows, cols = keep.shape
    half = rows // 2
    tile = half
    for count in (8, 4, 3, 2):
        if half % (count * PAD) == 0:
            tile = half // count
            break
    steps = half // tile
    low = pl.BlockSpec((tile, cols), lambda i: (i, 0))
    high = pl.BlockSpec((tile, cols), lambda i: (i + steps, 0))
    return call(
        fold_rows_kernel,
        "fold_rows",
        (shape((half, cols), bf16), shape((half, cols), bf16)),
        [low, high, low, high],
        (keep, keep, got, got),
        out_specs=(low, low),
        grid=(steps,),
    )


def combine_kernel(keep_ref, got_ref, out_ref):
    out_ref[...] = (keep_ref[...].astype(f32) + got_ref[...].astype(f32)).astype(bf16)


def combine(keep, got):
    return call(
        combine_kernel,
        "combine",
        shape(keep.shape, bf16),
        [LOAD, LOAD],
        (keep, got),
        out_specs=(STORE,),
    )


def finish_grads_kernel(counts, *refs):
    out_ref = refs[-1]
    cols = out_ref.shape[1]
    layer = pl.program_id(0)
    at = 0
    for n, count in enumerate(counts):

        @pl.when(layer == n)
        def write(parts=refs[at : at + count]):
            out_ref[...] = sum(part[...].astype(f32) for part in parts)[:, :cols]

        at += count


def finish_grads(layers, cols, window):
    rows = layers[0][0][0].shape[0]
    specs, operands = [], []
    for arrays, spot in layers:
        for array in arrays:
            specs.append(pl.BlockSpec((rows, window), lambda i, spot=spot: (0, spot)))
            operands.append(array)
    return call(
        functools.partial(finish_grads_kernel, [len(arrays) for arrays, _ in layers]),
        "finish_grads",
        shape((len(layers), rows, cols), f32),
        specs,
        tuple(operands),
        out_specs=(pl.BlockSpec((pl.Squeezed(), rows, cols), lambda i: (i, 0, 0)),),
        grid=(len(layers),),
    )


def pack_attn_kernel(place, group_at, smalls, *refs):
    scal, q_ref, k_ref, v_ref, o_ref = refs[:5]
    small_refs, out_ref = refs[5:-1], refs[-1]
    rows, cols = q_ref.shape
    hd = k_ref.shape[1] // 2
    high = scal[group_at] == 1
    pick = lambda ref: jnp.where(high, ref[:, hd:], ref[:, :hd])
    out_ref[:rows, :cols] = q_ref[...]
    out_ref[:rows, cols : cols + hd] = pick(k_ref)
    out_ref[:rows, cols + hd : cols + 2 * hd] = pick(v_ref)
    out_ref[:rows, cols + 2 * hd :] = o_ref[...]
    if smalls:
        gain1, gain2, bias_q, bias_k, bias_v = small_refs
        layers, n = gain1.shape
        heads, bias_n = bias_q.shape[1:]
        out_ref[rows:, :] = jnp.zeros((2 * PAD, out_ref.shape[1]), bf16)
        at = rows
        for block in (gain1[...], gain2[...]):
            out_ref[at : at + layers, :n] = block
            at += layers
        for layer in range(layers):
            out_ref[at : at + heads, :bias_n] = bias_q[layer]
            at += heads
            for ref in (bias_k, bias_v):
                both = ref[layer].astype(f32)
                out_ref[at : at + 1, :bias_n] = jnp.where(high, both[1:], both[:1]).astype(bf16)
                at += 1


def pack_attn(place, layer, w_query, w_key, w_value, w_out_t, smalls):
    _, rows, cols = w_query.shape
    kv_cols = w_key.shape[2]
    block = lambda c: pl.BlockSpec((pl.Squeezed(), rows, c), lambda i: (layer, 0, 0))
    whole = lambda a: pl.BlockSpec(a.shape, lambda i: (0,) * a.ndim)
    out = (rows + (2 * PAD if smalls else 0), 2 * cols + kv_cols)
    return call(
        functools.partial(pack_attn_kernel, place, place.at["quarter"], bool(smalls)),
        "pack",
        shape(out, bf16),
        [SMEM, block(cols), block(kv_cols), block(kv_cols), block(cols)]
        + [whole(a) for a in smalls],
        (place.table, w_query, w_key, w_value, w_out_t, *smalls),
        out_specs=(pl.BlockSpec(out, lambda i: (0, 0)),),
        grid=(1,),
    )


def pack_wide_kernel(*refs):
    out_ref = refs[-1]
    at = 0
    for ref in refs[:-1]:
        rows, cols = ref.shape
        spot = slice(at, at + rows)
        if out_ref.shape[1] > cols:
            tail = cols // 128 * 128
            out_ref[spot, tail:] = jnp.zeros((rows, out_ref.shape[1] - tail), bf16)
        out_ref[spot, :cols] = ref[...]
        at += rows


def pack_wide(layer, arrays, units):
    _, rows, cols = arrays[0].shape
    block = pl.BlockSpec((pl.Squeezed(), rows, cols), lambda i: (layer, 0, 0))
    out = (rows * len(arrays), units)
    return call(
        pack_wide_kernel,
        "pack",
        shape(out, bf16),
        [block] * len(arrays),
        tuple(arrays),
        out_specs=(pl.BlockSpec(out, lambda i: (0, 0)),),
        grid=(1,),
    )


def unpack_kernel(place, weight, shard, heads, bias_n, layers, *refs):
    scal, refs = refs[0], refs[1:]
    w_refs, refs = refs[: len(weight.arrays)], refs[len(weight.arrays) :]
    outs, buf, sems = refs[:-2], refs[-2], refs[-1]
    copies = weight.copies(place, scal, w_refs, buf, sems, skip=shard, cols=slice(0, buf.shape[1]))
    for copy in copies:
        copy.start()
    for copy in copies:
        copy.wait()
    for block in range(place.blocks):
        part = buf[block * 2 * PAD : (block + 1) * 2 * PAD, :].astype(f32)
        at = 0
        for n in range(2 * layers):
            outs[n][:, block * shard : (block + 1) * shard] = part[at : at + 1, :shard]
            at += 1
        for layer in range(layers):
            for h in range(heads + 2):
                spot = h * bias_n * place.blocks + block * bias_n
                outs[2 * layers + layer][:, spot : spot + bias_n] = part[at : at + 1, :bias_n]
                at += 1


def unpack(place, weight, shard, heads, bias_n, layers, width):
    cols = (heads + 2) * bias_n * place.blocks
    return call(
        functools.partial(unpack_kernel, place, weight, shard, heads, bias_n, layers),
        "unpack",
        (shape((1, width), f32),) * (2 * layers) + (shape((1, cols), f32),) * layers,
        [SMEM] + [ANY] * len(weight.arrays),
        (place.table, *weight.arrays),
        [
            pltpu.VMEM((place.blocks * 2 * PAD, 256), bf16),
            pltpu.SemaphoreType.DMA((place.blocks,)),
        ],
    )


def hold_kernel(src_ref, out_ref):
    out_ref[...] = src_ref[...]


def hold(array):
    return call(hold_kernel, "hold", shape(array.shape, array.dtype), [VMEM], (array,))


def corners_kernel(far_ref, side_ref, gate_ref, up_ref, sems):
    rows = gate_ref.shape[0]
    copies = [
        pltpu.make_async_copy(far_ref.at[pl.ds(0, rows)], gate_ref, sems.at[0]),
        pltpu.make_async_copy(side_ref.at[pl.ds(rows, rows)], up_ref, sems.at[1]),
    ]
    start_all(copies)
    wait_all(copies)


def corners(far, side):
    out = shape((far.shape[0] // 2, far.shape[1]), bf16)
    return call(
        corners_kernel, "pack", (out, out), [HBM, HBM], (far, side),
        [pltpu.SemaphoreType.DMA((2,))], (HBM, HBM),
    )


def touch_kernel(*refs):
    refs[-1][...] = jnp.zeros(refs[-1].shape, f32)


def touch(arrays):
    call(touch_kernel, "touch", shape((8, 128), f32), [HBM] * len(arrays), tuple(arrays))


def small_kernel(place, layers, trees, hd, *refs):
    scal, out_ref = refs[0], refs[-1]
    refs = refs[1:-1]
    count = layers * trees
    gains1, gains2, sums = refs[:count], refs[count : 2 * count], refs[2 * count :]
    half, quarter = scal[place.at["half"]], scal[place.at["quarter"]]
    out_ref[...] = jnp.zeros(out_ref.shape, f32)
    width = out_ref.shape[1]
    for layer in range(layers):
        part = slice(layer * trees, (layer + 1) * trees)
        total = lambda group: sum(ref[...] for ref in group[part])
        out_ref[layer : layer + 1, :] = total(gains1)
        out_ref[layers + layer : layers + layer + 1, :] = total(gains2)
        row = total(sums)
        q_cols = row.shape[1] - 2 * hd
        at = 2 * layers + layer
        for n in range(width // q_cols):
            mine = quarter * 2 + half == n
            out_ref[at : at + 1, n * q_cols : (n + 1) * q_cols] = jnp.where(
                mine, row[:, :q_cols], 0.0
            )
        at += layers
        for n in range(2):
            for kind in range(2):
                spot = (2 * kind + n) * hd
                start = q_cols + kind * hd
                out_ref[at : at + 1, spot : spot + hd] = jnp.where(
                    quarter == n, row[:, start : start + hd], 0.0
                )


def kv_pick_kernel(skip, *refs):
    low_ref, total_ref = refs[-1], refs[-2]
    at = 0
    for ref in refs[:-2]:
        rows = ref.shape[0]
        low_ref[at : at + rows, :] = ref[:, skip:]
        total_ref[at : at + rows, :] = ref[:, skip:].astype(f32)
        at += rows


def kv_add_kernel(left_ref, right_ref, total_ref, low_ref):
    total = left_ref[...] + right_ref[...].astype(f32)
    total_ref[...] = total
    low_ref[...] = total.astype(bf16)


def kv_place_kernel(group_at, scal, own_ref, got_ref, key_ref, value_ref):
    layers, rows, cols = key_ref.shape
    hd = cols // 2
    high = scal[group_at] == 1
    for layer in range(layers):
        spot = slice(layer * rows, (layer + 1) * rows)
        own = own_ref[spot, :]
        got = got_ref[spot, :].astype(f32)
        first = jnp.where(high, got, own)
        second = jnp.where(high, own, got)
        key_ref[layer, :, :hd] = first[:, :hd]
        key_ref[layer, :, hd:] = second[:, :hd]
        value_ref[layer, :, :hd] = first[:, hd:]
        value_ref[layer, :, hd:] = second[:, hd:]


def add_kernel(left_ref, right_ref, out_ref):
    out_ref[...] = left_ref[...] + right_ref[...]


def tree_tables(parent_row):
    block_ids = jnp.arange(NBLK, dtype=jnp.int32)
    step_up = (block_ids[None, :] == parent_row[:, None]).astype(jnp.int32)
    reach_tab = jnp.eye(NBLK, dtype=jnp.int32) + step_up
    for repeat_idx in range(max(1, (NBLK - 1).bit_length())):
        reach_tab = (jnp.dot(reach_tab, reach_tab) > 0).astype(jnp.int32)
    depth_tab = jnp.sum(reach_tab, axis=1) - 1
    return (reach_tab, depth_tab)


def geometry(parent_row, seq_index, rows_dev):
    reach_tab, depth_tab = tree_tables(parent_row)
    token_idx = seq_index * rows_dev + jnp.arange(rows_dev, dtype=jnp.int32)
    key_idx = jnp.arange(NBLK * BLK, dtype=jnp.int32)
    block_ids = jnp.arange(NBLK, dtype=jnp.int32)
    query_hot = (token_idx[:, None] // BLK == block_ids[None, :]).astype(f32)
    key_hot = (key_idx[:, None] // BLK == block_ids[None, :]).astype(f32)
    link_rows = jnp.dot(query_hot, reach_tab.astype(f32), precision=lax.Precision.HIGHEST)
    link_tab = jnp.dot(link_rows, key_hot.T, precision=lax.Precision.HIGHEST)
    visible = (link_tab > 0.5) & (key_idx[None, :] <= token_idx[:, None])
    depth_rows = jnp.dot(query_hot, depth_tab.astype(f32), precision=lax.Precision.HIGHEST)
    position = BLK * depth_rows + (token_idx % BLK).astype(f32)
    return (position, visible.astype(f32))


def wide_angles(position, head_dim):
    freq_idx = jnp.arange(head_dim // 2, dtype=f32)
    inv_freq = rope_base ** (-2.0 * freq_idx / head_dim)
    turn_val = position[:, None] * inv_freq[None, :]
    cosine, sine_val = (jnp.cos(turn_val), jnp.sin(turn_val))
    return (
        jnp.concatenate([cosine, cosine], axis=1),
        jnp.concatenate([-sine_val, sine_val], axis=1),
    )


def body(
    hidden_in,
    parents,
    cotangent,
    attn_gain,
    w_query,
    b_query,
    w_key,
    b_key,
    w_value,
    b_value,
    w_out,
    mlp_gain,
    w_gate,
    w_up,
    w_down,
):
    place = Place()
    both = ("leaf", "seq")
    micro_n, rows_dev, width = hidden_in.shape
    layer_n, shard = w_query.shape[:2]
    heads, bias_cols = b_query.shape[1:]
    kv_heads = b_key.shape[1]
    hd = w_key.shape[2] // kv_heads
    tensor_n = lax.axis_size("tensor")
    units = -(-w_gate.shape[2] // 256) * 256
    blocks = place.blocks
    assert tensor_n == 4 and kv_heads == 2 and layer_n == 2 and place.seq_n == 4
    kv_group = place.tensor_i >> 1
    q_cols = heads * hd
    qkv_cols = q_cols + 2 * hd
    pack_cols = qkv_cols + q_cols
    share = rows_dev // tensor_n

    order = ORDER[0] = Order()
    w_down_t = jnp.swapaxes(w_down, 1, 2)
    w_out_t = jnp.swapaxes(w_out, 1, 2)
    smalls = (attn_gain, mlp_gain, b_query, b_key, b_value)
    whole = lambda own: [lax.all_gather(own, both, axis=0, tiled=True)]
    links = fabric(True)
    own = pack_attn(place, 0, w_query, w_key, w_value, w_out_t, smalls)
    pieces = [own]
    for n, (axis, bit) in enumerate(links):
        pieces = pieces + [swap(piece, axis, bit) for piece in pieces]
        if n == len(links) - 2:
            touch([pieces[1]] + pieces[2:3])
    attn0 = Weight(pieces, shard, True)
    wide = lambda array, layer=0: pack_wide(layer, (array,), units)
    (a_axis, a_bit), (b_axis, b_bit), *others = fabric(False)
    own_in = pack_wide(0, (w_gate, w_up), units)
    side_in = swap(own_in, b_axis, b_bit)
    *gain_rows, bias0, bias1 = unpack(place, attn0, shard, heads, bias_cols, layer_n, width)

    def far_in():
        again = pack_wide(0, (w_gate, w_up), units)
        return [again, swap(again, a_axis, a_bit)]

    def corners_in(again, far):
        part_gate, part_up = corners(far, side_in)
        corner_gate = swap(part_gate, b_axis, b_bit)
        corner_up = swap(part_up, a_axis, a_bit)
        arrays = [again, far, side_in, corner_gate, corner_up]
        gate = [(0, 0), (1, 0), (2, 0), (3, 0)]
        up = [(0, shard), (1, shard), (2, shard), (4, 0)]
        for axis, bit in others:
            count = len(arrays)
            arrays = arrays + [swap(array, axis, bit) for array in arrays]
            gate = gate + [(n + count, at) for n, at in gate]
            up = up + [(n + count, at) for n, at in up]
        return arrays, gate, up

    def second_layer():
        attn = whole(pack_attn(place, 1, w_query, w_key, w_value, w_out_t, ()))
        return attn, whole(pack_wide(1, (w_gate, w_up, w_down_t), units))

    weights = [
        (attn0, None, None, bias0, gain_rows[0], gain_rows[2]),
        (None, None, None, bias1, gain_rows[1], gain_rows[3]),
    ]

    tables = []
    for micro in range(micro_n):
        position, visible = geometry(parents[micro], place.seq_i, rows_dev)
        tables.append(wide_angles(position, hd) + (visible,))

    spot = (place.at["half"], place.at["quarter"])
    quarter = place.table[spot[0]] * 2 + place.table[spot[1]]
    arrive = {(0, "attn"): 40.0, (1, "attn"): 170.0, (1, "mlp"): 260.0}
    offloaded = [("down", "in"), ()]
    finished = {}
    busy = {"core": 0, "row": 0}
    kept, slots, grads, settled, marks = {}, {}, {}, {}, set()
    finals, tails = [None] * micro_n, [None] * micro_n

    def scatter(keep, send, at):
        got = swap(send, "tensor", 1)
        at = yield "fold", order.link("z1", "z", at), 0
        keep, send = fold(place, "quarter", keep, got)
        got = swap(send, "tensor", 2)
        return keep, got, order.link("z2", "z", at)

    def gather(own, at):
        got = swap(own, "tensor", 2)
        at = yield "join", order.link("z2", "z", at), 0
        own = join(place, "quarter", own, got)
        got = swap(own, "tensor", 1)
        return own, got, order.link("z1", "z", at)

    def last_rows(micro, middle, keep, send):
        passed = lambda key: (lambda: 0.0 if key in marks else None)
        yield "hold", passed(("attend_back", 1, micro)), 2
        got = swap(hold(send), "tensor", 1)
        at = order.link("z1", "z", order.now)
        at = yield "fold", at, 1
        keep, send = fold(place, "quarter", keep, got)
        got = swap(send, "tensor", 2)
        at = order.link("z2", "z", at)
        at = yield "finish_plain", at, 1
        low = finish_plain(middle, keep, got)
        own, got, at = yield from gather(low, at)
        yield "join", at, 3
        finals[micro] = join(place, "half", own, got)

    def tree(micro):
        cos_wide, sin_wide, visible = tables[micro]
        at = yield "entry", 20.0, 1
        state, normed = entry(place, hidden_in[micro], weights[0][4], share)
        parts = (normed,)
        for layer in range(layer_n):
            bias, gain1, gain2 = weights[layer][3:]
            ready = lambda at=at, layer=layer: (
                max(at, arrive[layer, "attn"]) if layer == 0 or layer in settled else None
            )
            at = yield "project", ready, 2
            w_attn = settled[layer][0] if layer in settled else attn0
            outs = project(place, parts, w_attn, bias, cos_wide, sin_wide, heads, hd)
            marks.add(("project", layer, micro))
            query, kv_own = outs[:2]
            normed = outs[2] if len(outs) == 3 else parts[0]
            kv_parts = [kv_own]
            for bit in axis_bits("seq")[::-1]:
                kv_parts = kv_parts + [swap(part, "seq", bit) for part in kv_parts]
            at = yield "attend", order.link("kv", "kv", at) + 2.0, 2
            attended, lse, keep, send = attend(
                place, query, kv_parts, visible, w_attn, heads, hd, width
            )
            keep, got, at = yield from scatter(keep, send, at)
            at = yield "finish_norm", at, 0
            middle, low = finish_norm(state, keep, got, gain2)
            own, got, at = yield from gather(low, at)
            ready = lambda at=at, layer=layer: (
                max(at, arrive[layer, "mlp"]) if layer or 0 in settled else None
            )
            at = yield "mlp", ready, 2 + 0.1 * micro
            w_in, w_dn = settled[layer][1:]
            normed_mlp, gate, up, mixed, keep, send = mlp(place, own, got, w_in, w_dn)
            kept[layer, micro] = (
                state, normed, query, kv_parts, lse, attended,
                middle, normed_mlp, gate, up, mixed,
            )
            if layer < layer_n - 1:
                keep, got, at = yield from scatter(keep, send, at)
                at = yield "finish_norm", at, 0
                state, low = finish_norm(middle, keep, got, weights[layer + 1][4])
                own, got, at = yield from gather(low, at)
                parts = (own, got)
            else:
                more.append(last_rows(micro, middle, keep, send))
        carry = lax.dynamic_slice_in_dim(cotangent[micro], quarter * share, share, 0).astype(f32)
        downs = (cotangent[micro],)
        for layer in reversed(range(layer_n)):
            if layer == 0:
                order.scale = 1
            bias, gain1, gain2 = weights[layer][3:]
            w_attn, w_in, w_dn = settled[layer]
            (
                state, normed, query, kv_parts, lse, attended,
                middle, normed_mlp, gate, up, mixed,
            ) = kept[layer, micro]
            at = yield "mlp_back", at, 1.5 + 0.1 * micro
            outs = mlp_back(place, downs, gate, up, w_in, w_dn)
            dgate, dup, keep, send = outs[:4]
            full_down = outs[4] if len(outs) == 5 else downs[0]
            slots[layer, micro, "mlp"] = (full_down, dgate, dup)
            marks.add(("mlp_back", layer, micro))
            keep, got, at = yield from scatter(keep, send, at)
            at = yield "finish_back", at, 0
            mid, low, term2 = finish_back(carry, keep, got, middle, gain2)
            own, got, at = yield from gather(low, at)
            at = yield "attend_back", at, 2
            full_out, dquery, keep, send = attend_back(
                place, own, got, query, kv_parts, visible, lse, cos_wide, sin_wide,
                w_attn, heads, hd,
            )
            marks.add(("attend_back", layer, micro))
            slots[layer, micro, "out"] = (full_out,)
            got = swap(send, "seq", 1)
            at = yield "fold", order.link("core", "core", at), 0
            keep, send = fold(place, place.at["chip"] + 1, keep, got)
            got = swap(send, "seq", 2)
            marks.add(("kv", layer, micro))
            at = yield "lin_back", order.link("kv", "kv", at), 1
            dlin, sums, keep, send = lin_back(
                place, dquery, keep, got, cos_wide, sin_wide, w_attn, heads, hd, width
            )
            slots[layer, micro, "lin"] = (dlin,)
            marks.add(("lin_back", layer, micro))
            keep, got, at = yield from scatter(keep, send, at)
            at = yield "finish_back", at, 0
            marks.add(("finish_back", layer, micro))
            carry, low, term1 = finish_back(mid, keep, got, state, gain1)
            slots[layer, micro, "small"] = (term1, term2, sums)
            own, got, at = yield from gather(low, at)
            downs = (own, got)
        if micro == micro_n - 1:
            marks.add("end")
        yield "join", at, 1
        late = grads[0, "down"] if micro == micro_n - 1 else ()
        tails[micro] = join(place, "half", *downs, deps=late)

    def reduce_links(layer, name, keep, send, flip, at):
        links = fabric(not flip)[:-1] + fabric(flip)[-1:]
        axis, bit = links[-1]
        got = swap(send, axis, bit)
        busy["core"] += 1
        at = order.link("core_w", "core", at)
        for n, (axis, bit) in enumerate(links[:-1][::-1]):
            after = ("kv", layer, micro_n - 1)
            ready = lambda at=at, axis=axis, n=n: (
                max(at, order.free.get(axis, 0.0) - 4.0)
                if (axis != "seq" or after in marks) and (n or busy["row"] < 2)
                else None
            )
            at = yield "fold_rows", ready, 1
            if n == 0:
                busy["core"] -= 1
                busy["row"] += 1
            keep, send = fold_rows(keep, got)
            got = swap(send, axis, bit)
            kind = ("row2" if n == 0 else "row1") + ("" if keep.shape[1] > width else "_small")
            at = order.link(kind, axis, at)
        yield "combine", at, 1
        busy["row"] -= 1
        grads[layer, name] = (combine(keep, got),)

    def finishes():
        jobs = [
            ("down", ("down", 0), ("down", 0), w_gate.shape[2], units),
            ("gate", ("in", 0), ("gate", 0), w_gate.shape[2], units),
            ("up", ("in", 1), ("up", 0), w_gate.shape[2], units),
            ("out", ("attn", 0), ("attn", 0), q_cols, q_cols),
            ("lin", ("attn", 1), ("attn", 1), q_cols, q_cols),
        ]
        for name, (first, first_at), (second, second_at), cols, window in jobs:
            keys = ((0, first), (1, second))
            yield "finish_grads", (
                lambda keys=keys: 0.0 if all(key in grads for key in keys) and "end" in marks else None
            ), 7
            layers = [(grads[keys[0]], first_at), (grads[keys[1]], second_at)]
            finished[name] = finish_grads(layers, cols, window)

    def fillers(layer):
        trees = range(micro_n)
        saved = lambda n: [kept[layer, micro][n] for micro in trees]
        side = lambda kind, n: [slots[layer, micro, kind][n] for micro in trees]
        done = lambda kind: (
            lambda: 0.0 if all((layer, micro, kind) in slots for micro in trees) else None
        )
        near = lambda key: (lambda: 0.0 if (key, layer, micro_n - 1) in marks else None)

        def reduce_grad(name, pairs, flip, at):
            if name in offloaded[layer]:
                (total,) = weight_grad(place, pairs, None)
                grads[layer, name] = (
                    lax.psum_scatter(total, both, scatter_dimension=0, tiled=True),
                )
                return
            keep, send = weight_grad(place, pairs, place.at["grads", flip])
            more.append(reduce_links(layer, name, keep, send, flip, at))

        down = lambda: [(side("mlp", 0), saved(10))]
        gate = lambda: [(saved(7), side("mlp", 1))]
        up = lambda: [(saved(7), side("mlp", 2))]
        out = lambda: [(side("out", 0), saved(5))]
        lin = lambda: [(saved(1), side("lin", 0))]
        free = lambda test: (
            lambda: 0.0 if test() is not None and busy["core"] == 0 else None
        )
        at = yield "weight_grad", done("mlp"), 5
        reduce_grad("down", down(), True, at)
        if layer > 0:
            at = yield "weight_grad", free(lambda: 0.0), 5
            reduce_grad("up", up(), True, at)
            at = yield "weight_grad", free(near("kv")), 3
            reduce_grad("gate", gate(), False, at)
            at = yield "weight_grad_small", free(done("lin")), 4
        else:
            at = yield "weight_grad_two", 0.0, 5
            reduce_grad("in", gate() + up(), False, at)
            at = yield "weight_grad_small", done("lin"), 0
        reduce_grad("attn", out() + lin(), True, at)

    def cross_sums():
        keys = [(layer, "attn") for layer in range(layer_n)]
        at = yield "kv_pick", (lambda: 0.0 if all(key in grads for key in keys) else None), 0.5
        parts = [grads[key][0] for key in keys]
        dims = (layer_n * shard, 2 * hd)
        total, low = call(
            functools.partial(kv_pick_kernel, 2 * q_cols),
            "kv_pick",
            (shape(dims, f32), shape(dims, bf16)),
            [LOAD] * len(parts),
            tuple(parts),
        )
        got = swap(low, "tensor", 1)
        at = yield "kv_add", order.link("core", "kv", at) + 2.0, 0.5
        total, low = call(
            kv_add_kernel, "kv_add", (shape(dims, f32), shape(dims, bf16)), [VMEM, VMEM],
            (total, got),
        )
        got = swap(low, "tensor", 2)
        yield "kv_place", order.link("core", "kv", at) + 3.0, 0.5
        out = shape((layer_n, shard, kv_heads * hd), f32)
        finished["kv"] = call(
            functools.partial(kv_place_kernel, place.at["quarter"]),
            "kv_place", (out, out), [SMEM, VMEM, VMEM], (place.table, total, got),
        )

    def small_sums():
        keys = [(layer, micro, "small") for layer in range(layer_n) for micro in range(micro_n)]
        at = yield "small", (lambda: 0.0 if all(key in slots for key in keys) else None), 0.5
        parts = [slots[key][n] for n in range(3) for key in keys]
        total = call(
            functools.partial(small_kernel, place, layer_n, micro_n, hd),
            "small",
            shape((4 * layer_n, width), f32),
            [SMEM] + [LOAD] * len(parts),
            (place.table, *parts),
        )
        for axis, bit in fabric(False)[::-1] + [("tensor", 1), ("tensor", 2)]:
            got = swap(total, axis, bit)
            at = yield "add", order.link("hop", "small", at), 0.5
            total = call(add_kernel, "add", shape(total.shape, f32), [VMEM, VMEM], (total, got))
        grads["small"] = total

    def arrivals():
        names = [("project", 0, micro) for micro in range(micro_n)]
        yield "pack", (lambda: 0.0 if all(name in marks for name in names) else None), 0
        again, far = far_in()
        down = whole(wide(w_down_t))
        at = order.now
        yield "touch", at + 46.0, 0
        arrays, gate, up = corners_in(again, far)
        settled[0] = (attn0, Mixed(arrays, gate, up, shard), Weight(down, shard, False))
        half = len(arrays) // 2
        arrive[0, "mlp"] = at + 75.0
        yield "touch", at + 58.0, 1
        touch(arrays[half : half + 3])
        yield "touch", at + 73.0, 1
        touch(arrays[half + 3 :])
        yield "pack", at + 71.0, 1
        attn, wide_all = second_layer()
        settled[1] = (
            Weight(attn, shard, False),
            Weight(wide_all, 3 * shard, False),
            Weight(wide_all, 3 * shard, False, 2 * shard),
        )

    more = []
    order.run([tree(micro) for micro in range(micro_n)] + [fillers(1), fillers(0), small_sums(), arrivals(), finishes(), cross_sums()], more)
    hidden_out = jnp.stack(finals)
    input_grad = jnp.stack(tails).astype(f32)

    names = ("gate", "up", "down", "lin", "out")
    gate_g, up_g, down_g, query_g, out_g = (finished[name] for name in names)
    key_g, value_g = finished["kv"]
    total = grads["small"]
    block = place.leaf_i * place.seq_n + place.seq_i
    gains = lax.dynamic_slice(total, (0, block * shard), (2 * layer_n, shard))
    cut = lambda a: lax.dynamic_slice_in_dim(a, block * bias_cols, bias_cols, a.ndim - 1)
    bq = total[2 * layer_n : 3 * layer_n].reshape(layer_n, tensor_n, heads, hd)
    bq = cut(lax.dynamic_index_in_dim(bq, place.tensor_i, 1, keepdims=False))
    kv_row = total[3 * layer_n :]
    bk = cut(kv_row[:, : 2 * hd].reshape(layer_n, 2, hd))
    bv = cut(kv_row[:, 2 * hd : 4 * hd].reshape(layer_n, 2, hd))
    return (
        hidden_out,
        input_grad,
        gains[:layer_n],
        query_g,
        bq,
        key_g,
        bk,
        value_g,
        bv,
        jnp.swapaxes(out_g, 1, 2),
        gains[layer_n:],
        gate_g,
        up_g,
        jnp.swapaxes(down_g, 1, 2),
    )


def solution(mesh):
    both = ("leaf", "seq")
    return jax.shard_map(
        body,
        mesh=mesh,
        in_specs=(
            P("leaf", "seq", None),
            P("leaf", None),
            P("leaf", "seq", None),
            P(None, both),
            P(None, both, "tensor"),
            P(None, "tensor", both),
            P(None, both, None),
            P(None, None, both),
            P(None, both, None),
            P(None, None, both),
            P(None, "tensor", both),
            P(None, both),
            P(None, both, "tensor"),
            P(None, both, "tensor"),
            P(None, "tensor", both),
        ),
        out_specs=(
            P("leaf", "seq", None),
            P("leaf", "seq", None),
            P(None, both),
            P(None, both, "tensor"),
            P(None, "tensor", both),
            P(None, both, None),
            P(None, None, both),
            P(None, both, None),
            P(None, None, both),
            P(None, "tensor", both),
            P(None, both),
            P(None, both, "tensor"),
            P(None, both, "tensor"),
            P(None, "tensor", both),
        ),
        check_vma=False,
    )
```

```python
import functools
import math

import jax
import jax.numpy as jnp
from jax import lax
from jax.experimental import pallas as pl
from jax.experimental.pallas import tpu as pltpu
from jax.sharding import PartitionSpec as P

BLK = 128
NBLK = 8
PAD = 16
COST = 16
TIMES = {
    "entry": 2.5,
    "mlp": 14,
    "mlp_back": 15,
    "attend": 5,
    "attend_back": 7.5,
    "lin_back": 4.5,
    "project": 4.2,
    "weight_grad": 9,
    "fold_rows": 3,
    "weight_grad_small": 4,
    "weight_grad_two": 17,
    "fold": 1.3,
    "join": 1.2,
    "add": 1.0,
    "finish_grads": 3,
}
START = 1.5
LINKS = {"z1": 11.0, "z2": 12.0, "kv": 6.5, "core": 3.0, "core_w": 9.0, "row2": 46, "row1": 25, "hop": 3.0,
         "row2_small": 21.0, "row1_small": 12.0}


def cost(name):
    return pl.CostEstimate(
        flops=int(TIMES.get(name, 2) * ORDER[0].scale * 1.15e9), bytes_accessed=1000, transcendentals=0
    )


class Order:
    def __init__(self):
        self.last = None
        self.now = 0.0
        self.free = {}
        self.scale = COST

    def link(self, kind, wire, at):
        begin = max(at, self.free.get(wire, 0.0))
        end = begin + LINKS[kind]
        self.free[wire] = end - 2.0
        self.now += START
        return end

    def took(self, outs):
        self.last = min(outs, key=lambda a: math.prod(a.shape))

    def run(self, tasks, more):
        waiting = [[task, next(task)] for task in tasks]
        while waiting or more:
            while more:
                task = more.pop()
                waiting.append([task, next(task)])
            ready = []
            for entry_ in waiting:
                name, when, rank = entry_[1]
                when = when() if callable(when) else when
                if when is not None:
                    ready.append((entry_, name, when, rank))
            soonest = min(when for _, _, when, _ in ready)
            self.now = max(self.now, soonest)
            chosen = min(
                (item for item in ready if item[2] <= self.now), key=lambda item: (item[3], item[2])
            )
            self.now += TIMES.get(chosen[1], 2.0)
            try:
                chosen[0][1] = chosen[0][0].send(self.now)
            except StopIteration:
                waiting.remove(chosen[0])


ORDER = [Order()]


eps_norm = 1e-06
rope_base = 1000000.0
neg_fill = -1e30

f32 = jnp.float32
bf16 = jnp.bfloat16

ANY = pl.BlockSpec(memory_space=pl.ANY)
HBM = pl.BlockSpec(memory_space=pltpu.HBM)
LOAD = pl.BlockSpec(memory_space=pltpu.HBM)
STORE = pl.BlockSpec(memory_space=pltpu.HBM)
VMEM = pl.BlockSpec(memory_space=pltpu.VMEM)
SMEM = pl.BlockSpec(memory_space=pltpu.SMEM)


def dot(left_op, right_op):
    return jnp.dot(left_op, right_op, preferred_element_type=f32)


def dot_left(left_op, right_op):
    return lax.dot_general(
        left_op, right_op, (((0,), (0,)), ((), ())), preferred_element_type=f32
    )


def dot_right(left_op, right_op):
    return lax.dot_general(
        left_op, right_op, (((1,), (1,)), ((), ())), preferred_element_type=f32
    )


def spans(total, step):
    return [(at, min(step, total - at)) for at in range(0, total, step)]


def shape(dims, dtype):
    return jax.ShapeDtypeStruct(tuple(dims), dtype)


EARLY = []


def flush(ref):
    for item in EARLY[-1]:
        if item[0] is ref and not item[2]:
            item[1].start()
            item[2] = True


def call(kernel, name, out_shape, in_specs, operands, scratch=(), out_specs=None, deps=(), **more):
    several = isinstance(out_shape, tuple)
    outs = out_shape if several else (out_shape,)
    if out_specs is None:
        out_specs = tuple(VMEM for _ in outs)
    order = ORDER[0]
    if order.last is not None:
        deps = tuple(deps) + (order.last,)
    count = len(operands)
    size = lambda a: math.prod(a.shape) * jnp.dtype(a.dtype).itemsize
    token = not any(spec is VMEM for spec in out_specs)
    if token:
        out_shape = outs = tuple(outs) + (shape((8, 128), f32),)
        spec = pl.BlockSpec((8, 128), lambda i: (0, 0)) if "grid" in more else VMEM
        out_specs = tuple(out_specs) + (spec,)
        plain = kernel

        def kernel(*refs):
            mark = refs[count + len(outs) - 1]
            mark[...] = jnp.zeros(mark.shape, f32)
            plain(*refs[: count + len(outs) - 1], *refs[count + len(outs) :])

    if "grid" in more:
        room = 24 << 20
        loads, stores = [], []
    else:
        loads = [n for n, spec in enumerate(in_specs) if spec is LOAD]
        stores = [n for n, spec in enumerate(out_specs) if spec is STORE]
        fast = (VMEM, LOAD, STORE)
        room = sum(size(a) for a, spec in zip(operands, in_specs) if spec in fast)
        room += sum(size(a) for a, spec in zip(outs, out_specs) if spec in fast)
        room += sum(size(a) for a in scratch if a.memory_space == pltpu.VMEM)
        room = min(58 << 20, room + room // 2 + (6 << 20))
    moved = [operands[n] for n in loads] + [outs[n] for n in stores]
    extra = [pltpu.VMEM(a.shape, a.dtype) for a in moved]
    if moved:
        extra.append(pltpu.SemaphoreType.DMA((len(moved),)))

    def wrapped(*refs):
        ins, rest = list(refs[:count]), refs[count + len(deps) :]
        results, rest = list(rest[: len(outs)]), rest[len(outs) :]
        inner, rest = rest[: len(scratch)], rest[len(scratch) :]
        copies, items = [], []
        for k, n in enumerate(loads):
            copies.append(pltpu.make_async_copy(ins[n], rest[k], rest[-1].at[k]))
            ins[n] = rest[k]
        for copy in copies:
            copy.start()
        for k, n in enumerate(stores, len(loads)):
            items.append([rest[k], pltpu.make_async_copy(rest[k], results[n], rest[-1].at[k]), False])
            results[n] = rest[k]
        for copy in copies:
            copy.wait()
        EARLY.append(items)
        kernel(*ins, *results, *inner)
        EARLY.pop()
        for item in items:
            if not item[2]:
                item[1].start()
        for item in items:
            item[1].wait()

    made = pl.pallas_call(
        wrapped,
        out_shape=outs,
        in_specs=list(in_specs) + [ANY] * len(deps),
        out_specs=tuple(out_specs),
        scratch_shapes=list(scratch) + extra,
        compiler_params=pltpu.CompilerParams(vmem_limit_bytes=room),
        cost_estimate=cost(name),
        name=name,
        **more,
    )(*operands, *deps)
    order.took(made)
    if token:
        made = made[:-1]
    return made if several else made[0]


def swap(array, axis, bit):
    size = lax.axis_size(axis)
    return lax.ppermute(array, axis, [(i, i ^ bit) for i in range(size)])


def axis_bits(axis):
    size = lax.axis_size(axis)
    return [1 << k for k in range(size.bit_length() - 1)]


def fabric(flip):
    seq_bits = axis_bits("seq")
    outer = [("seq", bit) for bit in seq_bits[1:]] + [("leaf", bit) for bit in axis_bits("leaf")]
    return (outer[::-1] if flip else outer) + [("seq", seq_bits[0])]


def gather_pieces(own, flip):
    pieces = [own]
    for axis, bit in fabric(flip):
        pieces = pieces + [swap(piece, axis, bit) for piece in pieces]
    return pieces


class Place:
    def __init__(self):
        self.tensor_i = lax.axis_index("tensor")
        self.seq_i = lax.axis_index("seq")
        self.leaf_i = lax.axis_index("leaf")
        self.seq_n = lax.axis_size("seq")
        self.leaf_n = lax.axis_size("leaf")
        self.blocks = self.seq_n * self.leaf_n
        values = [self.tensor_i & 1, self.tensor_i >> 1]
        self.at = {"half": 0, "quarter": 1}
        for flip in (False, True):
            self.at["blocks", flip] = len(values)
            values += self.homes(fabric(flip))
            self.at["grads", flip] = len(values)
            values += self.homes(fabric(not flip)[:-1] + fabric(flip)[-1:])
        self.at["seq"] = len(values)
        values += self.seq_homes()
        self.at["chip"] = len(values)
        values += [self.seq_i & 1, self.seq_i >> 1]
        self.table = jnp.stack([jnp.asarray(v, jnp.int32) for v in values])

    def homes(self, links):
        out = []
        for p in range(1 << len(links)):
            seq_rel = sum(b for k, (a, b) in enumerate(links) if a == "seq" and p >> k & 1)
            leaf_rel = sum(b for k, (a, b) in enumerate(links) if a == "leaf" and p >> k & 1)
            out.append((self.leaf_i ^ leaf_rel) * self.seq_n + (self.seq_i ^ seq_rel))
        return out

    def seq_homes(self):
        out = [self.seq_i]
        for bit in axis_bits("seq")[::-1]:
            out = out + [h ^ bit for h in out]
        return out


class Weight:
    def __init__(self, arrays, rows, flip, first=0):
        self.arrays = list(arrays)
        self.rows = rows
        self.flip = flip
        self.first = first

    def source(self, place, scal, refs, block, skip, rows, cols):
        skip = skip + self.first
        if len(self.arrays) == 1:
            return refs[0].at[pl.ds(block * self.rows + skip, rows), cols], block
        home = scal[place.at["blocks", self.flip] + block]
        return refs[block].at[pl.ds(skip, rows), cols], home

    def halves(self, place, scal, refs, buf, sems, skip=0):
        mid = buf.shape[1] // 256 * 128
        parts = (slice(0, mid), slice(mid, buf.shape[1]))
        return [
            self.copies(
                place, scal, refs, buf.at[:, part], sems.at[n], skip=skip, cols=part
            )
            for n, part in enumerate(parts)
        ]

    def copies(self, place, scal, refs, buf, sems, skip=0, cols=slice(None)):
        rows = buf.shape[0] // place.blocks
        out = []
        for block in range(place.blocks):
            src, home = self.source(place, scal, refs, block, skip, rows, cols)
            if not isinstance(home, int):
                home = pl.multiple_of(home * rows, PAD)
            else:
                home = home * rows
            out.append(pltpu.make_async_copy(src, buf.at[pl.ds(home, rows)], sems.at[block]))
        return out


def row_spot(index, rows):
    return pl.ds(pl.multiple_of(index * rows, PAD), rows)


def put_halves(place, scal, buf, own_ref, got_ref):
    half = own_ref.shape[0]
    which = scal[place.at["half"]]
    buf[row_spot(which, half), :] = own_ref[...]
    buf[row_spot(1 - which, half), :] = got_ref[...]


def fold_kernel(spot, scal, keep_ref, got_ref, next_keep, next_send):
    rows = next_keep.shape[0]
    which = scal[spot]
    mine = row_spot(which, rows)
    away = row_spot(1 - which, rows)
    next_keep[...] = keep_ref[mine, :] + got_ref[mine, :].astype(f32)
    next_send[...] = (keep_ref[away, :] + got_ref[away, :].astype(f32)).astype(bf16)


def fold(place, spot, keep, got):
    rows, cols = keep.shape
    return call(
        functools.partial(fold_kernel, place.at[spot] if isinstance(spot, str) else spot),
        "fold",
        (shape((rows // 2, cols), f32), shape((rows // 2, cols), bf16)),
        [SMEM, VMEM, VMEM],
        (place.table, keep, got),
    )


def join_kernel(spot, scal, own_ref, got_ref, out_ref):
    rows = own_ref.shape[0]
    which = scal[spot]
    out_ref[row_spot(which, rows), :] = own_ref[...]
    out_ref[row_spot(1 - which, rows), :] = got_ref[...]


def join(place, spot, own, got, deps=()):
    rows, cols = own.shape
    return call(
        functools.partial(join_kernel, place.at[spot]),
        "join",
        shape((2 * rows, cols), own.dtype),
        [SMEM, VMEM, VMEM],
        (place.table, own, got),
        deps=deps,
    )


def normed_rows(values, gain):
    inv = lax.rsqrt(jnp.mean(values * values, axis=1, keepdims=True) + eps_norm)
    return (values * inv * gain).astype(bf16)


def entry_kernel(place, scal, x_ref, gain_ref, share_ref, normed_ref):
    rows = share_ref.shape[0]
    values = x_ref[...].astype(f32)
    normed_ref[...] = normed_rows(values, gain_ref[...])
    spot = scal[place.at["half"]] * 2 + scal[place.at["quarter"]]
    share_ref[...] = x_ref[row_spot(spot, rows), :].astype(f32)


def entry(place, hidden, gain, share):
    rows, width = hidden.shape
    return call(
        functools.partial(entry_kernel, place),
        "entry",
        (shape((share, width), f32), shape((rows, width), bf16)),
        [SMEM, LOAD, VMEM],
        (place.table, hidden, gain),
        out_specs=(VMEM, STORE),
    )


def finish_norm_kernel(base_ref, keep_ref, got_ref, gain_ref, sum_ref, normed_ref):
    total = base_ref[...] + (keep_ref[...] + got_ref[...].astype(f32))
    sum_ref[...] = total
    normed_ref[...] = normed_rows(total, gain_ref[...])


def finish_norm(base, keep, got, gain):
    return call(
        finish_norm_kernel,
        "finish_norm",
        (shape(base.shape, f32), shape(base.shape, bf16)),
        [LOAD, VMEM, VMEM, VMEM],
        (base, keep, got, gain),
        out_specs=(STORE, VMEM),
    )


def finish_plain_kernel(base_ref, keep_ref, got_ref, out_ref):
    out_ref[...] = (base_ref[...] + (keep_ref[...] + got_ref[...].astype(f32))).astype(bf16)


def finish_plain(base, keep, got):
    return call(
        finish_plain_kernel, "finish_plain", shape(base.shape, bf16), [LOAD, VMEM, VMEM], (base, keep, got)
    )


def finish_back_kernel(carry_ref, keep_ref, got_ref, src_ref, gain_ref, grad_ref, low_ref, term_ref):
    dnorm = keep_ref[...] + got_ref[...].astype(f32)
    source = src_ref[...]
    inv = lax.rsqrt(jnp.mean(source * source, axis=1, keepdims=True) + eps_norm)
    term_ref[...] = jnp.sum(dnorm * source * inv, axis=0, keepdims=True)
    scaled = dnorm * gain_ref[...]
    back = jnp.mean(scaled * source, axis=1, keepdims=True)
    grad = carry_ref[...] + inv * scaled - source * (inv * inv * inv) * back
    grad_ref[...] = grad
    low_ref[...] = grad.astype(bf16)


def finish_back(carry, keep, got, source, gain):
    width = carry.shape[1]
    return call(
        finish_back_kernel,
        "finish_back",
        (shape(carry.shape, f32), shape(carry.shape, bf16), shape((1, width), f32)),
        [LOAD, VMEM, VMEM, LOAD, VMEM],
        (carry, keep, got, source, gain),
        out_specs=(STORE, VMEM, STORE),
    )


def split_rows(place, scal, total_ref, keep_ref, send_ref):
    half = keep_ref.shape[0]
    which = scal[place.at["half"]]
    keep_ref[...] = total_ref[row_spot(which, half), :]
    send_ref[...] = total_ref[row_spot(1 - which, half), :].astype(bf16)


def project_kernel(place, weight, heads, hd, parts, *refs):
    scal, refs = refs[0], refs[1:]
    x_refs, refs = refs[:parts], refs[parts:]
    bias_ref, cos_ref, sin_ref = refs[:3]
    refs = refs[3:]
    w_refs, refs = refs[: len(weight.arrays)], refs[len(weight.arrays) :]
    q_ref, kv_ref, refs = refs[0], refs[1], refs[2:]
    if parts == 2:
        x_out, refs = refs[0], refs[1:]
    buf, sems = refs
    cols = (heads + 2) * hd
    copies = weight.copies(place, scal, w_refs, buf, sems, cols=slice(0, cols))
    for copy in copies:
        copy.start()
    if parts == 2:
        put_halves(place, scal, x_out, *x_refs)
        values = x_out[...]
    else:
        values = x_refs[0][...]
    for copy in copies:
        copy.wait()
    cos_wide = cos_ref[...]
    sin_wide = sin_ref[...]
    lin = dot(values, buf[...]) + bias_ref[...]
    for h in range(heads + 1):
        part = lin[:, h * hd : (h + 1) * hd]
        turned = part * cos_wide + pltpu.roll(part, hd // 2, 1) * sin_wide
        if h < heads:
            q_ref[:, h * hd : (h + 1) * hd] = turned.astype(bf16)
        else:
            kv_ref[:, :hd] = turned.astype(bf16)
    kv_ref[:, hd:] = lin[:, (heads + 1) * hd :].astype(bf16)


def project(place, x_parts, weight, bias, cos_wide, sin_wide, heads, hd):
    rows = sum(part.shape[0] for part in x_parts)
    width = x_parts[0].shape[1]
    cols = (heads + 2) * hd
    outs = [shape((rows, heads * hd), bf16), shape((rows, 2 * hd), bf16)]
    if len(x_parts) == 2:
        outs.append(shape((rows, width), bf16))
    return call(
        functools.partial(project_kernel, place, weight, heads, hd, len(x_parts)),
        "project",
        tuple(outs),
        [SMEM] + [LOAD if len(x_parts) == 1 else VMEM] * len(x_parts) + [VMEM, LOAD, LOAD]
        + [ANY] * len(weight.arrays),
        (place.table, *x_parts, bias, cos_wide, sin_wide, *weight.arrays),
        [pltpu.VMEM((width, cols), bf16), pltpu.SemaphoreType.DMA((place.blocks,))],
        out_specs=(STORE, VMEM) + (STORE,) * (len(outs) - 2),
    )


def put_keys(place, scal, buf, kv_refs):
    rows = kv_refs[0].shape[0]
    for n, ref in enumerate(kv_refs):
        buf[row_spot(scal[place.at["seq"] + n], rows), :] = ref[...]


def attend_kernel(place, weight, heads, hd, *refs):
    scal, q_ref, vis_ref, refs = refs[0], refs[1], refs[2], refs[3:]
    kv_refs, refs = refs[: place.seq_n], refs[place.seq_n :]
    w_refs, refs = refs[: len(weight.arrays)], refs[len(weight.arrays) :]
    o_ref, lse_ref, keep_ref, send_ref, kv_buf, w_buf, total_buf, sems = refs
    cols = slice((heads + 2) * hd, (2 * heads + 2) * hd)
    copies = weight.copies(place, scal, w_refs, w_buf, sems, cols=cols)
    for copy in copies:
        copy.start()
    put_keys(place, scal, kv_buf, kv_refs)
    keys = kv_buf[:, :hd]
    values = kv_buf[:, hd:]
    seen = vis_ref[...] > 0.5
    scale = 1.0 / math.sqrt(hd)
    lane = lax.broadcasted_iota(jnp.int32, lse_ref.shape, 1)
    lse_all = jnp.zeros(lse_ref.shape, f32)
    for h in range(heads):
        spot = slice(h * hd, (h + 1) * hd)
        scores = dot_right(q_ref[:, spot], keys) * scale
        scores = jnp.where(seen, scores, neg_fill)
        top = jnp.max(scores, axis=1, keepdims=True)
        expo = jnp.exp(scores - top)
        total = jnp.sum(expo, axis=1, keepdims=True)
        prob = (expo * (1.0 / total)).astype(bf16)
        o_ref[:, spot] = dot(prob, values).astype(bf16)
        lse_all = jnp.where(lane == h, top + jnp.log(total), lse_all)
    lse_ref[...] = lse_all
    flush(o_ref)
    flush(lse_ref)
    for copy in copies:
        copy.wait()
    for at, size in spans(w_buf.shape[0], 512):
        total_buf[:, at : at + size] = dot_right(o_ref[...], w_buf[at : at + size, :])
    split_rows(place, scal, total_buf, keep_ref, send_ref)


def attend(place, query, kv_parts, visible, weight, heads, hd, width):
    rows = query.shape[0]
    keys = visible.shape[1]
    half = rows // 2
    return call(
        functools.partial(attend_kernel, place, weight, heads, hd),
        "attend",
        (
            shape((rows, heads * hd), bf16),
            shape((rows, 128), f32),
            shape((half, width), f32),
            shape((half, width), bf16),
        ),
        [SMEM, LOAD, LOAD] + [VMEM] * len(kv_parts) + [ANY] * len(weight.arrays),
        (place.table, query, visible, *kv_parts, *weight.arrays),
        [
            pltpu.VMEM((keys, 2 * hd), bf16),
            pltpu.VMEM((width, heads * hd), bf16),
            pltpu.VMEM((rows, width), f32),
            pltpu.SemaphoreType.DMA((place.blocks,)),
        ],
        out_specs=(STORE, STORE, VMEM, VMEM),
    )


def attend_back_kernel(place, weight, heads, hd, *refs):
    (scal, own_ref, got_ref, q_ref, vis_ref, lse_ref, cos_ref, sin_ref), refs = refs[:8], refs[8:]
    kv_refs, refs = refs[: place.seq_n], refs[place.seq_n :]
    w_refs, refs = refs[: len(weight.arrays)], refs[len(weight.arrays) :]
    full_ref, dq_ref, keep_ref, send_ref, kv_buf, w_buf, do_buf, dkv_buf, sems = refs
    cols = slice((heads + 2) * hd, (2 * heads + 2) * hd)
    copies = weight.copies(place, scal, w_refs, w_buf, sems, cols=cols)
    for copy in copies:
        copy.start()
    put_halves(place, scal, full_ref, own_ref, got_ref)
    flush(full_ref)
    put_keys(place, scal, kv_buf, kv_refs)
    keys = kv_buf[:, :hd]
    values = kv_buf[:, hd:]
    seen = vis_ref[...] > 0.5
    cos_wide = cos_ref[...]
    sin_wide = sin_ref[...]
    scale = 1.0 / math.sqrt(hd)
    for copy in copies:
        copy.wait()
    do_buf[...] = dot(full_ref[...], w_buf[...]).astype(bf16)
    for h in range(heads):
        spot = slice(h * hd, (h + 1) * hd)
        query = q_ref[:, spot]
        dout = do_buf[:, spot]
        scores = dot_right(query, keys) * scale
        scores = jnp.where(seen, scores, neg_fill)
        prob = jnp.exp(scores - lse_ref[:, h : h + 1])
        dprob = dot_right(dout, values)
        delta = jnp.sum(prob * dprob, axis=1, keepdims=True)
        dscore = (prob * (dprob - delta)).astype(bf16)
        dquery = dot(dscore, keys) * scale
        dquery = dquery * cos_wide - pltpu.roll(dquery, hd // 2, 1) * sin_wide
        dq_ref[:, spot] = dquery.astype(bf16)
        dk_part = dot_left(dscore, query) * scale
        dv_part = dot_left(prob.astype(bf16), dout)
        if h == 0:
            dkv_buf[:, :hd] = dk_part
            dkv_buf[:, hd:] = dv_part
        else:
            dkv_buf[:, :hd] += dk_part
            dkv_buf[:, hd:] += dv_part
    rows = kv_refs[0].shape[0]
    core = scal[place.at["chip"]]
    for n in range(place.seq_n // 2):
        spot = slice(n * rows, (n + 1) * rows)
        keep_ref[spot, :] = dkv_buf[row_spot(2 * n + core, rows), :]
        send_ref[spot, :] = dkv_buf[row_spot(2 * n + 1 - core, rows), :].astype(bf16)


def attend_back(place, own, got, query, kv_parts, visible, lse, cos_wide, sin_wide, weight, heads, hd, deps=()):
    rows = query.shape[0]
    keys = visible.shape[1]
    width = own.shape[1]
    return call(
        functools.partial(attend_back_kernel, place, weight, heads, hd),
        "attend_back",
        (
            shape((rows, width), bf16),
            shape((rows, heads * hd), bf16),
            shape((keys // 2, 2 * hd), f32),
            shape((keys // 2, 2 * hd), bf16),
        ),
        [SMEM, VMEM, VMEM] + [LOAD] * (5 + len(kv_parts)) + [ANY] * len(weight.arrays),
        (place.table, own, got, query, visible, lse, cos_wide, sin_wide, *kv_parts, *weight.arrays),
        [
            pltpu.VMEM((keys, 2 * hd), bf16),
            pltpu.VMEM((width, heads * hd), bf16),
            pltpu.VMEM((rows, heads * hd), bf16),
            pltpu.VMEM((keys, 2 * hd), f32),
            pltpu.SemaphoreType.DMA((place.blocks,)),
        ],
        out_specs=(STORE, STORE, VMEM, VMEM),
        deps=deps,
    )


def lin_back_kernel(place, weight, heads, hd, *refs):
    (scal, dq_ref, dkv_ref, got_ref, cos_ref, sin_ref), refs = refs[:6], refs[6:]
    w_refs, refs = refs[: len(weight.arrays)], refs[len(weight.arrays) :]
    dlin_ref, sums_ref, keep_ref, send_ref, w_buf, total_buf, sems = refs
    cols = (heads + 2) * hd
    copies = weight.copies(place, scal, w_refs, w_buf, sems, cols=slice(0, cols))
    for copy in copies:
        copy.start()
    dkv = dkv_ref[...] + got_ref[...].astype(f32)
    dkey = dkv[:, :hd]
    dkey = dkey * cos_ref[...] - pltpu.roll(dkey, hd // 2, 1) * sin_ref[...]
    dlin_ref[:, : heads * hd] = dq_ref[...]
    dlin_ref[:, heads * hd : (heads + 1) * hd] = dkey.astype(bf16)
    dlin_ref[:, (heads + 1) * hd :] = dkv[:, hd:].astype(bf16)
    dlin = dlin_ref[...]
    sums_ref[...] = jnp.sum(dlin.astype(f32), axis=0, keepdims=True)
    flush(dlin_ref)
    for copy in copies:
        copy.wait()
    for at, size in spans(w_buf.shape[0], 512):
        total_buf[:, at : at + size] = dot_right(dlin, w_buf[at : at + size, :])
    split_rows(place, scal, total_buf, keep_ref, send_ref)


def lin_back(place, dquery, dkv, got, cos_wide, sin_wide, weight, heads, hd, width, deps=()):
    rows = dquery.shape[0]
    cols = (heads + 2) * hd
    return call(
        functools.partial(lin_back_kernel, place, weight, heads, hd),
        "lin_back",
        (
            shape((rows, cols), bf16),
            shape((1, cols), f32),
            shape((rows // 2, width), f32),
            shape((rows // 2, width), bf16),
        ),
        [SMEM, LOAD, VMEM, VMEM, LOAD, LOAD] + [ANY] * len(weight.arrays),
        (place.table, dquery, dkv, got, cos_wide, sin_wide, *weight.arrays),
        [
            pltpu.VMEM((width, cols), bf16),
            pltpu.VMEM((rows, width), f32),
            pltpu.SemaphoreType.DMA((place.blocks,)),
        ],
        out_specs=(STORE, STORE, VMEM, VMEM),
        deps=deps,
    )


class Mixed:
    def __init__(self, arrays, gate, up, rows):
        self.arrays = list(arrays)
        self.spots = (gate, up)
        self.rows = rows

    def halves(self, place, scal, refs, buf, sems, skip=0):
        spots = self.spots[1 if skip else 0]
        parts = [refs[n].at[pl.ds(at, self.rows)] for n, at in spots]
        return Weight(parts, self.rows, False).halves(place, scal, parts, buf, sems)


def start_all(copies):
    for copy in copies:
        copy.start()


def wait_all(copies):
    for copy in copies:
        copy.wait()


def mlp_kernel(place, w_in, w_down, *refs):
    (scal, own_ref, got_ref), refs = refs[:3], refs[3:]
    in_refs, refs = refs[: len(w_in.arrays)], refs[len(w_in.arrays) :]
    down_refs, refs = refs[: len(w_down.arrays)], refs[len(w_down.arrays) :]
    (
        full_ref, gate_ref, up_ref, mix_ref, keep_ref, send_ref,
        gate_buf, up_buf, down_buf, total_buf, gate_sems, up_sems, down_sems,
    ) = refs
    shard = gate_buf.shape[0] // place.blocks
    gate_copies = w_in.halves(place, scal, in_refs, gate_buf, gate_sems)
    up_copies = w_in.halves(place, scal, in_refs, up_buf, up_sems, skip=shard)
    down_copies = w_down.halves(place, scal, down_refs, down_buf, down_sems)
    start_all(gate_copies[0])
    put_halves(place, scal, full_ref, own_ref, got_ref)
    flush(full_ref)
    values = full_ref[...]
    units = gate_buf.shape[1]
    mid = units // 256 * 128
    parts = (spans(mid, 384), [(mid + at, size) for at, size in spans(units - mid, 384)])
    start_all(gate_copies[1])
    wait_all(gate_copies[0])
    for n in range(2):
        start_all(up_copies[n])
        for at, size in parts[n]:
            gate_ref[:, at : at + size] = dot(values, gate_buf[:, at : at + size]).astype(bf16)
        wait_all(gate_copies[1] if n == 0 else up_copies[0])
    flush(gate_ref)
    for n in range(2):
        start_all(down_copies[n])
        for at, size in parts[n]:
            spot = slice(at, at + size)
            up = dot(values, up_buf[:, spot])
            gate = gate_ref[:, spot].astype(f32)
            up_ref[:, spot] = up.astype(bf16)
            mix_ref[:, spot] = (gate * jax.nn.sigmoid(gate) * up).astype(bf16)
        wait_all(up_copies[1] if n == 0 else down_copies[0] + down_copies[1])
    flush(up_ref)
    flush(mix_ref)
    mixed = mix_ref[...]
    for at, size in spans(down_buf.shape[0], 512):
        total_buf[:, at : at + size] = dot_right(mixed, down_buf[at : at + size, :])
    split_rows(place, scal, total_buf, keep_ref, send_ref)


def mlp(place, own, got, w_in, w_down):
    half, width = own.shape
    rows = 2 * half
    units = w_in.arrays[0].shape[1]
    dma = pltpu.SemaphoreType.DMA((2, place.blocks))
    return call(
        functools.partial(mlp_kernel, place, w_in, w_down),
        "mlp",
        (
            shape((rows, width), bf16),
            shape((rows, units), bf16),
            shape((rows, units), bf16),
            shape((rows, units), bf16),
            shape((half, width), f32),
            shape((half, width), bf16),
        ),
        [SMEM, VMEM, VMEM] + [ANY] * (len(w_in.arrays) + len(w_down.arrays)),
        (place.table, own, got, *w_in.arrays, *w_down.arrays),
        [
            pltpu.VMEM((width, units), bf16),
            pltpu.VMEM((width, units), bf16),
            pltpu.VMEM((width, units), bf16),
            pltpu.VMEM((rows, width), f32),
            dma,
            dma,
            dma,
        ],
        out_specs=(STORE, STORE, STORE, STORE, VMEM, VMEM),
    )


def mlp_back_kernel(place, w_in, w_down, parts, *refs):
    scal, refs = refs[0], refs[1:]
    d_refs, refs = refs[:parts], refs[parts:]
    gate_ref, up_ref, refs = refs[0], refs[1], refs[2:]
    in_refs, refs = refs[: len(w_in.arrays)], refs[len(w_in.arrays) :]
    down_refs, refs = refs[: len(w_down.arrays)], refs[len(w_down.arrays) :]
    dgate_ref, dup_ref, keep_ref, send_ref, refs = refs[0], refs[1], refs[2], refs[3], refs[4:]
    if parts == 2:
        full_ref, refs = refs[0], refs[1:]
    gate_buf, up_buf, down_buf, total_buf, gate_sems, up_sems, down_sems = refs
    shard = gate_buf.shape[0] // place.blocks
    gate_copies = w_in.halves(place, scal, in_refs, gate_buf, gate_sems)
    up_copies = w_in.halves(place, scal, in_refs, up_buf, up_sems, skip=shard)
    down_copies = w_down.halves(place, scal, down_refs, down_buf, down_sems)
    start_all(down_copies[0])
    if parts == 2:
        put_halves(place, scal, full_ref, *d_refs)
        flush(full_ref)
        values = full_ref[...]
    else:
        values = d_refs[0][...]
    units = gate_buf.shape[1]
    mid = units // 256 * 128
    cuts = (spans(mid, 384), [(mid + at, size) for at, size in spans(units - mid, 384)])
    start_all(down_copies[1])
    wait_all(down_copies[0])
    for n in range(2):
        start_all(gate_copies[n])
        for at, size in cuts[n]:
            spot = slice(at, at + size)
            dmixed = dot(values, down_buf[:, spot])
            gate = gate_ref[:, spot].astype(f32)
            up = up_ref[:, spot].astype(f32)
            sig = jax.nn.sigmoid(gate)
            dgate_ref[:, spot] = (dmixed * up * sig * (1.0 + gate * (1.0 - sig))).astype(bf16)
            dup_ref[:, spot] = (dmixed * (gate * sig)).astype(bf16)
        if n == 0:
            wait_all(down_copies[1])
    start_all(up_copies[0] + up_copies[1])
    flush(dgate_ref)
    flush(dup_ref)
    wait_all(gate_copies[0] + gate_copies[1])
    dgate = dgate_ref[...]
    dup = dup_ref[...]
    for at, size in spans(gate_buf.shape[0], 512):
        spot = slice(at, at + size)
        total_buf[:, spot] = dot_right(dgate, gate_buf[spot, :])
    wait_all(up_copies[0] + up_copies[1])
    for at, size in spans(gate_buf.shape[0], 512):
        spot = slice(at, at + size)
        total_buf[:, spot] += dot_right(dup, up_buf[spot, :])
    split_rows(place, scal, total_buf, keep_ref, send_ref)


def mlp_back(place, d_parts, gate, up, w_in, w_down, deps=()):
    rows = sum(part.shape[0] for part in d_parts)
    width = d_parts[0].shape[1]
    half = rows // 2
    units = gate.shape[1]
    outs = [
        shape((rows, units), bf16),
        shape((rows, units), bf16),
        shape((half, width), f32),
        shape((half, width), bf16),
    ]
    if len(d_parts) == 2:
        outs.append(shape((rows, width), bf16))
    dma = pltpu.SemaphoreType.DMA((2, place.blocks))
    return call(
        functools.partial(mlp_back_kernel, place, w_in, w_down, len(d_parts)),
        "mlp_back",
        tuple(outs),
        [SMEM] + [LOAD if len(d_parts) == 1 else VMEM] * len(d_parts) + [LOAD, LOAD]
        + [ANY] * (len(w_in.arrays) + len(w_down.arrays)),
        (place.table, *d_parts, gate, up, *w_in.arrays, *w_down.arrays),
        [
            pltpu.VMEM((width, units), bf16),
            pltpu.VMEM((width, units), bf16),
            pltpu.VMEM((width, units), bf16),
            pltpu.VMEM((rows, width), f32),
            dma,
            dma,
            dma,
        ],
        out_specs=(STORE, STORE, VMEM, VMEM) + (STORE,) * (len(outs) - 4),
        deps=deps,
    )


def weight_grad_kernel(place, micro_n, pairs, homes, *refs):
    scal, refs = refs[0], refs[1:]
    left_refs = [refs[p * micro_n : (p + 1) * micro_n] for p in range(pairs)]
    refs = refs[pairs * micro_n :]
    right_refs = [refs[p * micro_n : (p + 1) * micro_n] for p in range(pairs)]
    refs = refs[pairs * micro_n :]
    outs = 1 if homes is None else 2
    out_refs, refs = refs[:outs], refs[outs:]
    bufs, sems = refs[:pairs], refs[pairs]
    shard = bufs[0].shape[0] // place.blocks
    half = place.blocks // 2
    copies = []
    at_col = 0
    for p in range(pairs):
        buf = bufs[p]
        cols = buf.shape[1]
        ready = 0
        for at, size in spans(buf.shape[0], 256):
            spot = slice(at, at + size)
            total = None
            for left, right in zip(left_refs[p], right_refs[p]):
                part = dot_left(left[:, spot], right[...])
                total = part if total is None else total + part
            buf[spot, :] = total.astype(bf16)
            while homes is None and (ready + 1) * shard <= at + size:
                src = buf.at[pl.ds(ready * shard, shard)]
                dst = out_refs[0].at[pl.ds(ready * shard, shard), pl.ds(at_col, cols)]
                copies.append(pltpu.make_async_copy(src, dst, sems.at[len(copies)]))
                copies[-1].start()
                ready += 1
        if homes is not None:
            for block in list(range(half, place.blocks)) + list(range(half)):
                home = scal[homes + block]
                src = buf.at[pl.ds(pl.multiple_of(home * shard, PAD), shard)]
                out = out_refs[block // half]
                dst = out.at[pl.ds(block % half * shard, shard), pl.ds(at_col, cols)]
                copies.append(pltpu.make_async_copy(src, dst, sems.at[len(copies)]))
                copies[-1].start()
        at_col += cols
    for copy in copies:
        copy.wait()


def weight_grad(place, pairs, homes, deps=()):
    micro_n = len(pairs[0][0])
    rows, width = pairs[0][0][0].shape
    cols = [rights[0].shape[1] for _, rights in pairs]
    if homes is None:
        outs = (shape((width, sum(cols)), bf16),)
    else:
        outs = (shape((width // 2, sum(cols)), bf16),) * 2
    lefts = [a for left, _ in pairs for a in left]
    rights = [a for _, right in pairs for a in right]
    copies = place.blocks * len(pairs)
    return call(
        functools.partial(weight_grad_kernel, place, micro_n, len(pairs), homes),
        "weight_grad" if sum(cols) > width else "weight_grad_small",
        outs,
        [SMEM] + [LOAD] * (len(lefts) + len(rights)),
        (place.table, *lefts, *rights),
        [pltpu.VMEM((width, c), bf16) for c in cols] + [pltpu.SemaphoreType.DMA((copies,))],
        out_specs=tuple(HBM for _ in outs),
        deps=deps,
    )


def fold_rows_kernel(keep_lo, keep_hi, got_lo, got_hi, keep_ref, send_ref):
    keep_ref[...] = (keep_lo[...].astype(f32) + got_lo[...].astype(f32)).astype(bf16)
    send_ref[...] = (keep_hi[...].astype(f32) + got_hi[...].astype(f32)).astype(bf16)


def fold_rows(keep, got):
    rows, cols = keep.shape
    half = rows // 2
    tile = half
    for count in (8, 4, 3, 2):
        if half % (count * PAD) == 0:
            tile = half // count
            break
    steps = half // tile
    low = pl.BlockSpec((tile, cols), lambda i: (i, 0))
    high = pl.BlockSpec((tile, cols), lambda i: (i + steps, 0))
    return call(
        fold_rows_kernel,
        "fold_rows",
        (shape((half, cols), bf16), shape((half, cols), bf16)),
        [low, high, low, high],
        (keep, keep, got, got),
        out_specs=(low, low),
        grid=(steps,),
    )


def combine_kernel(keep_ref, got_ref, out_ref):
    out_ref[...] = (keep_ref[...].astype(f32) + got_ref[...].astype(f32)).astype(bf16)


def combine(keep, got):
    return call(
        combine_kernel,
        "combine",
        shape(keep.shape, bf16),
        [LOAD, LOAD],
        (keep, got),
        out_specs=(STORE,),
    )


def finish_grads_kernel(counts, *refs):
    out_ref = refs[-1]
    cols = out_ref.shape[1]
    layer = pl.program_id(0)
    at = 0
    for n, count in enumerate(counts):

        @pl.when(layer == n)
        def write(parts=refs[at : at + count]):
            out_ref[...] = sum(part[...].astype(f32) for part in parts)[:, :cols]

        at += count


def finish_grads(layers, cols, window):
    rows = layers[0][0][0].shape[0]
    specs, operands = [], []
    for arrays, spot in layers:
        for array in arrays:
            specs.append(pl.BlockSpec((rows, window), lambda i, spot=spot: (0, spot)))
            operands.append(array)
    return call(
        functools.partial(finish_grads_kernel, [len(arrays) for arrays, _ in layers]),
        "finish_grads",
        shape((len(layers), rows, cols), f32),
        specs,
        tuple(operands),
        out_specs=(pl.BlockSpec((pl.Squeezed(), rows, cols), lambda i: (i, 0, 0)),),
        grid=(len(layers),),
    )


def pack_attn_kernel(place, group_at, smalls, *refs):
    scal, q_ref, k_ref, v_ref, o_ref = refs[:5]
    small_refs, out_ref = refs[5:-1], refs[-1]
    rows, cols = q_ref.shape
    hd = k_ref.shape[1] // 2
    high = scal[group_at] == 1
    pick = lambda ref: jnp.where(high, ref[:, hd:], ref[:, :hd])
    out_ref[:rows, :cols] = q_ref[...]
    out_ref[:rows, cols : cols + hd] = pick(k_ref)
    out_ref[:rows, cols + hd : cols + 2 * hd] = pick(v_ref)
    out_ref[:rows, cols + 2 * hd :] = o_ref[...]
    if smalls:
        gain1, gain2, bias_q, bias_k, bias_v = small_refs
        layers, n = gain1.shape
        heads, bias_n = bias_q.shape[1:]
        out_ref[rows:, :] = jnp.zeros((2 * PAD, out_ref.shape[1]), bf16)
        at = rows
        for block in (gain1[...], gain2[...]):
            out_ref[at : at + layers, :n] = block
            at += layers
        for layer in range(layers):
            out_ref[at : at + heads, :bias_n] = bias_q[layer]
            at += heads
            for ref in (bias_k, bias_v):
                both = ref[layer].astype(f32)
                out_ref[at : at + 1, :bias_n] = jnp.where(high, both[1:], both[:1]).astype(bf16)
                at += 1


def pack_attn(place, layer, w_query, w_key, w_value, w_out_t, smalls):
    _, rows, cols = w_query.shape
    kv_cols = w_key.shape[2]
    block = lambda c: pl.BlockSpec((pl.Squeezed(), rows, c), lambda i: (layer, 0, 0))
    whole = lambda a: pl.BlockSpec(a.shape, lambda i: (0,) * a.ndim)
    out = (rows + (2 * PAD if smalls else 0), 2 * cols + kv_cols)
    return call(
        functools.partial(pack_attn_kernel, place, place.at["quarter"], bool(smalls)),
        "pack",
        shape(out, bf16),
        [SMEM, block(cols), block(kv_cols), block(kv_cols), block(cols)]
        + [whole(a) for a in smalls],
        (place.table, w_query, w_key, w_value, w_out_t, *smalls),
        out_specs=(pl.BlockSpec(out, lambda i: (0, 0)),),
        grid=(1,),
    )


def pack_wide_kernel(*refs):
    out_ref = refs[-1]
    at = 0
    for ref in refs[:-1]:
        rows, cols = ref.shape
        spot = slice(at, at + rows)
        if out_ref.shape[1] > cols:
            tail = cols // 128 * 128
            out_ref[spot, tail:] = jnp.zeros((rows, out_ref.shape[1] - tail), bf16)
        out_ref[spot, :cols] = ref[...]
        at += rows


def pack_wide(layer, arrays, units):
    _, rows, cols = arrays[0].shape
    block = pl.BlockSpec((pl.Squeezed(), rows, cols), lambda i: (layer, 0, 0))
    out = (rows * len(arrays), units)
    return call(
        pack_wide_kernel,
        "pack",
        shape(out, bf16),
        [block] * len(arrays),
        tuple(arrays),
        out_specs=(pl.BlockSpec(out, lambda i: (0, 0)),),
        grid=(1,),
    )


def unpack_kernel(place, weight, shard, heads, bias_n, layers, *refs):
    scal, refs = refs[0], refs[1:]
    w_refs, refs = refs[: len(weight.arrays)], refs[len(weight.arrays) :]
    outs, buf, sems = refs[:-2], refs[-2], refs[-1]
    copies = weight.copies(place, scal, w_refs, buf, sems, skip=shard, cols=slice(0, buf.shape[1]))
    for copy in copies:
        copy.start()
    for copy in copies:
        copy.wait()
    for block in range(place.blocks):
        part = buf[block * 2 * PAD : (block + 1) * 2 * PAD, :].astype(f32)
        at = 0
        for n in range(2 * layers):
            outs[n][:, block * shard : (block + 1) * shard] = part[at : at + 1, :shard]
            at += 1
        for layer in range(layers):
            for h in range(heads + 2):
                spot = h * bias_n * place.blocks + block * bias_n
                outs[2 * layers + layer][:, spot : spot + bias_n] = part[at : at + 1, :bias_n]
                at += 1


def unpack(place, weight, shard, heads, bias_n, layers, width):
    cols = (heads + 2) * bias_n * place.blocks
    return call(
        functools.partial(unpack_kernel, place, weight, shard, heads, bias_n, layers),
        "unpack",
        (shape((1, width), f32),) * (2 * layers) + (shape((1, cols), f32),) * layers,
        [SMEM] + [ANY] * len(weight.arrays),
        (place.table, *weight.arrays),
        [
            pltpu.VMEM((place.blocks * 2 * PAD, 256), bf16),
            pltpu.SemaphoreType.DMA((place.blocks,)),
        ],
    )


def hold_kernel(src_ref, out_ref):
    out_ref[...] = src_ref[...]


def hold(array):
    return call(hold_kernel, "hold", shape(array.shape, array.dtype), [VMEM], (array,))


def corners_kernel(far_ref, side_ref, gate_ref, up_ref, sems):
    rows = gate_ref.shape[0]
    copies = [
        pltpu.make_async_copy(far_ref.at[pl.ds(0, rows)], gate_ref, sems.at[0]),
        pltpu.make_async_copy(side_ref.at[pl.ds(rows, rows)], up_ref, sems.at[1]),
    ]
    start_all(copies)
    wait_all(copies)


def corners(far, side):
    out = shape((far.shape[0] // 2, far.shape[1]), bf16)
    return call(
        corners_kernel, "pack", (out, out), [HBM, HBM], (far, side),
        [pltpu.SemaphoreType.DMA((2,))], (HBM, HBM),
    )


def touch_kernel(*refs):
    refs[-1][...] = jnp.zeros(refs[-1].shape, f32)


def touch(arrays):
    call(touch_kernel, "touch", shape((8, 128), f32), [HBM] * len(arrays), tuple(arrays))


def small_kernel(place, layers, trees, hd, *refs):
    scal, out_ref = refs[0], refs[-1]
    refs = refs[1:-1]
    count = layers * trees
    gains1, gains2, sums = refs[:count], refs[count : 2 * count], refs[2 * count :]
    half, quarter = scal[place.at["half"]], scal[place.at["quarter"]]
    out_ref[...] = jnp.zeros(out_ref.shape, f32)
    width = out_ref.shape[1]
    for layer in range(layers):
        part = slice(layer * trees, (layer + 1) * trees)
        total = lambda group: sum(ref[...] for ref in group[part])
        out_ref[layer : layer + 1, :] = total(gains1)
        out_ref[layers + layer : layers + layer + 1, :] = total(gains2)
        row = total(sums)
        q_cols = row.shape[1] - 2 * hd
        at = 2 * layers + layer
        for n in range(width // q_cols):
            mine = quarter * 2 + half == n
            out_ref[at : at + 1, n * q_cols : (n + 1) * q_cols] = jnp.where(
                mine, row[:, :q_cols], 0.0
            )
        at += layers
        for n in range(2):
            for kind in range(2):
                spot = (2 * kind + n) * hd
                start = q_cols + kind * hd
                out_ref[at : at + 1, spot : spot + hd] = jnp.where(
                    quarter == n, row[:, start : start + hd], 0.0
                )


def kv_pick_kernel(skip, *refs):
    low_ref, total_ref = refs[-1], refs[-2]
    at = 0
    for ref in refs[:-2]:
        rows = ref.shape[0]
        low_ref[at : at + rows, :] = ref[:, skip:]
        total_ref[at : at + rows, :] = ref[:, skip:].astype(f32)
        at += rows


def kv_add_kernel(left_ref, right_ref, total_ref, low_ref):
    total = left_ref[...] + right_ref[...].astype(f32)
    total_ref[...] = total
    low_ref[...] = total.astype(bf16)


def kv_place_kernel(group_at, scal, own_ref, got_ref, key_ref, value_ref):
    layers, rows, cols = key_ref.shape
    hd = cols // 2
    high = scal[group_at] == 1
    for layer in range(layers):
        spot = slice(layer * rows, (layer + 1) * rows)
        own = own_ref[spot, :]
        got = got_ref[spot, :].astype(f32)
        first = jnp.where(high, got, own)
        second = jnp.where(high, own, got)
        key_ref[layer, :, :hd] = first[:, :hd]
        key_ref[layer, :, hd:] = second[:, :hd]
        value_ref[layer, :, :hd] = first[:, hd:]
        value_ref[layer, :, hd:] = second[:, hd:]


def add_kernel(left_ref, right_ref, out_ref):
    out_ref[...] = left_ref[...] + right_ref[...]


def tree_tables(parent_row):
    block_ids = jnp.arange(NBLK, dtype=jnp.int32)
    step_up = (block_ids[None, :] == parent_row[:, None]).astype(jnp.int32)
    reach_tab = jnp.eye(NBLK, dtype=jnp.int32) + step_up
    for repeat_idx in range(max(1, (NBLK - 1).bit_length())):
        reach_tab = (jnp.dot(reach_tab, reach_tab) > 0).astype(jnp.int32)
    depth_tab = jnp.sum(reach_tab, axis=1) - 1
    return (reach_tab, depth_tab)


def geometry(parent_row, seq_index, rows_dev):
    reach_tab, depth_tab = tree_tables(parent_row)
    token_idx = seq_index * rows_dev + jnp.arange(rows_dev, dtype=jnp.int32)
    key_idx = jnp.arange(NBLK * BLK, dtype=jnp.int32)
    block_ids = jnp.arange(NBLK, dtype=jnp.int32)
    query_hot = (token_idx[:, None] // BLK == block_ids[None, :]).astype(f32)
    key_hot = (key_idx[:, None] // BLK == block_ids[None, :]).astype(f32)
    link_rows = jnp.dot(query_hot, reach_tab.astype(f32), precision=lax.Precision.HIGHEST)
    link_tab = jnp.dot(link_rows, key_hot.T, precision=lax.Precision.HIGHEST)
    visible = (link_tab > 0.5) & (key_idx[None, :] <= token_idx[:, None])
    depth_rows = jnp.dot(query_hot, depth_tab.astype(f32), precision=lax.Precision.HIGHEST)
    position = BLK * depth_rows + (token_idx % BLK).astype(f32)
    return (position, visible.astype(f32))


def wide_angles(position, head_dim):
    freq_idx = jnp.arange(head_dim // 2, dtype=f32)
    inv_freq = rope_base ** (-2.0 * freq_idx / head_dim)
    turn_val = position[:, None] * inv_freq[None, :]
    cosine, sine_val = (jnp.cos(turn_val), jnp.sin(turn_val))
    return (
        jnp.concatenate([cosine, cosine], axis=1),
        jnp.concatenate([-sine_val, sine_val], axis=1),
    )


def body(
    hidden_in,
    parents,
    cotangent,
    attn_gain,
    w_query,
    b_query,
    w_key,
    b_key,
    w_value,
    b_value,
    w_out,
    mlp_gain,
    w_gate,
    w_up,
    w_down,
):
    place = Place()
    both = ("leaf", "seq")
    micro_n, rows_dev, width = hidden_in.shape
    layer_n, shard = w_query.shape[:2]
    heads, bias_cols = b_query.shape[1:]
    kv_heads = b_key.shape[1]
    hd = w_key.shape[2] // kv_heads
    tensor_n = lax.axis_size("tensor")
    units = -(-w_gate.shape[2] // 256) * 256
    blocks = place.blocks
    assert tensor_n == 4 and kv_heads == 2 and layer_n == 2 and place.seq_n == 4
    kv_group = place.tensor_i >> 1
    q_cols = heads * hd
    qkv_cols = q_cols + 2 * hd
    pack_cols = qkv_cols + q_cols
    share = rows_dev // tensor_n

    order = ORDER[0] = Order()
    w_down_t = jnp.swapaxes(w_down, 1, 2)
    w_out_t = jnp.swapaxes(w_out, 1, 2)
    smalls = (attn_gain, mlp_gain, b_query, b_key, b_value)
    whole = lambda own: [lax.all_gather(own, both, axis=0, tiled=True)]
    links = fabric(True)
    own = pack_attn(place, 0, w_query, w_key, w_value, w_out_t, smalls)
    pieces = [own]
    for n, (axis, bit) in enumerate(links):
        pieces = pieces + [swap(piece, axis, bit) for piece in pieces]
        if n == len(links) - 2:
            touch([pieces[1]] + pieces[2:3])
    attn0 = Weight(pieces, shard, True)
    wide = lambda array, layer=0: pack_wide(layer, (array,), units)
    (a_axis, a_bit), (b_axis, b_bit), *others = fabric(False)
    own_in = pack_wide(0, (w_gate, w_up), units)
    side_in = swap(own_in, b_axis, b_bit)
    *gain_rows, bias0, bias1 = unpack(place, attn0, shard, heads, bias_cols, layer_n, width)

    def far_in():
        again = pack_wide(0, (w_gate, w_up), units)
        return [again, swap(again, a_axis, a_bit)]

    def corners_in(again, far):
        part_gate, part_up = corners(far, side_in)
        corner_gate = swap(part_gate, b_axis, b_bit)
        corner_up = swap(part_up, a_axis, a_bit)
        arrays = [again, far, side_in, corner_gate, corner_up]
        gate = [(0, 0), (1, 0), (2, 0), (3, 0)]
        up = [(0, shard), (1, shard), (2, shard), (4, 0)]
        for axis, bit in others:
            count = len(arrays)
            arrays = arrays + [swap(array, axis, bit) for array in arrays]
            gate = gate + [(n + count, at) for n, at in gate]
            up = up + [(n + count, at) for n, at in up]
        return arrays, gate, up

    def second_layer():
        attn = whole(pack_attn(place, 1, w_query, w_key, w_value, w_out_t, ()))
        return attn, whole(pack_wide(1, (w_gate, w_up, w_down_t), units))

    weights = [
        (attn0, None, None, bias0, gain_rows[0], gain_rows[2]),
        (None, None, None, bias1, gain_rows[1], gain_rows[3]),
    ]

    tables = []
    for micro in range(micro_n):
        position, visible = geometry(parents[micro], place.seq_i, rows_dev)
        tables.append(wide_angles(position, hd) + (visible,))

    spot = (place.at["half"], place.at["quarter"])
    quarter = place.table[spot[0]] * 2 + place.table[spot[1]]
    arrive = {(0, "attn"): 40.0, (1, "attn"): 170.0, (1, "mlp"): 260.0}
    offloaded = [("down", "in"), ()]
    finished = {}
    busy = {"core": 0, "row": 0}
    kept, slots, grads, settled, marks = {}, {}, {}, {}, set()
    finals, tails = [None] * micro_n, [None] * micro_n

    def scatter(keep, send, at):
        got = swap(send, "tensor", 1)
        at = yield "fold", order.link("z1", "z", at), 0
        keep, send = fold(place, "quarter", keep, got)
        got = swap(send, "tensor", 2)
        return keep, got, order.link("z2", "z", at)

    def gather(own, at):
        got = swap(own, "tensor", 2)
        at = yield "join", order.link("z2", "z", at), 0
        own = join(place, "quarter", own, got)
        got = swap(own, "tensor", 1)
        return own, got, order.link("z1", "z", at)

    def last_rows(micro, middle, keep, send):
        passed = lambda key: (lambda: 0.0 if key in marks else None)
        yield "hold", passed(("attend_back", 1, micro)), 2
        got = swap(hold(send), "tensor", 1)
        at = order.link("z1", "z", order.now)
        at = yield "fold", at, 1
        keep, send = fold(place, "quarter", keep, got)
        got = swap(send, "tensor", 2)
        at = order.link("z2", "z", at)
        at = yield "finish_plain", at, 1
        low = finish_plain(middle, keep, got)
        own, got, at = yield from gather(low, at)
        yield "join", at, 3
        finals[micro] = join(place, "half", own, got)

    def tree(micro):
        cos_wide, sin_wide, visible = tables[micro]
        at = yield "entry", 20.0, 1
        state, normed = entry(place, hidden_in[micro], weights[0][4], share)
        parts = (normed,)
        for layer in range(layer_n):
            bias, gain1, gain2 = weights[layer][3:]
            ready = lambda at=at, layer=layer: (
                max(at, arrive[layer, "attn"]) if layer == 0 or layer in settled else None
            )
            at = yield "project", ready, 2
            w_attn = settled[layer][0] if layer in settled else attn0
            outs = project(place, parts, w_attn, bias, cos_wide, sin_wide, heads, hd)
            marks.add(("project", layer, micro))
            query, kv_own = outs[:2]
            normed = outs[2] if len(outs) == 3 else parts[0]
            kv_parts = [kv_own]
            for bit in axis_bits("seq")[::-1]:
                kv_parts = kv_parts + [swap(part, "seq", bit) for part in kv_parts]
            at = yield "attend", order.link("kv", "kv", at) + 2.0, 2
            attended, lse, keep, send = attend(
                place, query, kv_parts, visible, w_attn, heads, hd, width
            )
            keep, got, at = yield from scatter(keep, send, at)
            at = yield "finish_norm", at, 0
            middle, low = finish_norm(state, keep, got, gain2)
            own, got, at = yield from gather(low, at)
            ready = lambda at=at, layer=layer: (
                max(at, arrive[layer, "mlp"]) if layer or 0 in settled else None
            )
            at = yield "mlp", ready, 2 + 0.1 * micro
            w_in, w_dn = settled[layer][1:]
            marks.add(("mlp", layer, micro))
            normed_mlp, gate, up, mixed, keep, send = mlp(place, own, got, w_in, w_dn)
            kept[layer, micro] = (
                state, normed, query, kv_parts, lse, attended,
                middle, normed_mlp, gate, up, mixed,
            )
            if layer < layer_n - 1:
                keep, got, at = yield from scatter(keep, send, at)
                at = yield "finish_norm", at, 0
                state, low = finish_norm(middle, keep, got, weights[layer + 1][4])
                own, got, at = yield from gather(low, at)
                parts = (own, got)
            else:
                more.append(last_rows(micro, middle, keep, send))
        carry = lax.dynamic_slice_in_dim(cotangent[micro], quarter * share, share, 0).astype(f32)
        downs = (cotangent[micro],)
        for layer in reversed(range(layer_n)):
            if layer == 0:
                order.scale = 1
            bias, gain1, gain2 = weights[layer][3:]
            w_attn, w_in, w_dn = settled[layer]
            (
                state, normed, query, kv_parts, lse, attended,
                middle, normed_mlp, gate, up, mixed,
            ) = kept[layer, micro]
            at = yield "mlp_back", at, 1.5 + 0.1 * micro
            outs = mlp_back(place, downs, gate, up, w_in, w_dn)
            dgate, dup, keep, send = outs[:4]
            full_down = outs[4] if len(outs) == 5 else downs[0]
            slots[layer, micro, "mlp"] = (full_down, dgate, dup)
            marks.add(("mlp_back", layer, micro))
            keep, got, at = yield from scatter(keep, send, at)
            at = yield "finish_back", at, 0
            mid, low, term2 = finish_back(carry, keep, got, middle, gain2)
            own, got, at = yield from gather(low, at)
            at = yield "attend_back", at, 2
            full_out, dquery, keep, send = attend_back(
                place, own, got, query, kv_parts, visible, lse, cos_wide, sin_wide,
                w_attn, heads, hd,
            )
            marks.add(("attend_back", layer, micro))
            slots[layer, micro, "out"] = (full_out,)
            got = swap(send, "seq", 1)
            at = yield "fold", order.link("core", "core", at), 0
            keep, send = fold(place, place.at["chip"] + 1, keep, got)
            got = swap(send, "seq", 2)
            marks.add(("kv", layer, micro))
            at = yield "lin_back", order.link("kv", "kv", at), 1
            dlin, sums, keep, send = lin_back(
                place, dquery, keep, got, cos_wide, sin_wide, w_attn, heads, hd, width
            )
            slots[layer, micro, "lin"] = (dlin,)
            marks.add(("lin_back", layer, micro))
            keep, got, at = yield from scatter(keep, send, at)
            at = yield "finish_back", at, 0
            marks.add(("finish_back", layer, micro))
            carry, low, term1 = finish_back(mid, keep, got, state, gain1)
            slots[layer, micro, "small"] = (term1, term2, sums)
            own, got, at = yield from gather(low, at)
            downs = (own, got)
        if micro == micro_n - 1:
            marks.add("end")
        yield "join", at, 1
        late = grads[0, "down"] if micro == micro_n - 1 else ()
        tails[micro] = join(place, "half", *downs, deps=late)

    def reduce_links(layer, name, keep, send, flip, at):
        links = fabric(not flip)[:-1] + fabric(flip)[-1:]
        axis, bit = links[-1]
        got = swap(send, axis, bit)
        busy["core"] += 1
        at = order.link("core_w", "core", at)
        for n, (axis, bit) in enumerate(links[:-1][::-1]):
            after = ("kv", layer, micro_n - 1)
            ready = lambda at=at, axis=axis, n=n: (
                max(at, order.free.get(axis, 0.0) - 4.0)
                if (axis != "seq" or after in marks) and (n or busy["row"] < 2)
                else None
            )
            at = yield "fold_rows", ready, 1
            if n == 0:
                busy["core"] -= 1
                busy["row"] += 1
            keep, send = fold_rows(keep, got)
            got = swap(send, axis, bit)
            kind = ("row2" if n == 0 else "row1") + ("" if keep.shape[1] > width else "_small")
            at = order.link(kind, axis, at)
        yield "combine", at, 1
        busy["row"] -= 1
        grads[layer, name] = (combine(keep, got),)

    def finishes():
        jobs = [
            ("down", ("down", 0), ("down", 0), w_gate.shape[2], units),
            ("gate", ("in", 0), ("gate", 0), w_gate.shape[2], units),
            ("up", ("in", 1), ("up", 0), w_gate.shape[2], units),
            ("out", ("attn", 0), ("attn", 0), q_cols, q_cols),
            ("lin", ("attn", 1), ("attn", 1), q_cols, q_cols),
        ]
        for name, (first, first_at), (second, second_at), cols, window in jobs:
            keys = ((0, first), (1, second))
            yield "finish_grads", (
                lambda keys=keys: 0.0 if all(key in grads for key in keys) and "end" in marks else None
            ), 7
            layers = [(grads[keys[0]], first_at), (grads[keys[1]], second_at)]
            finished[name] = finish_grads(layers, cols, window)

    def fillers(layer):
        trees = range(micro_n)
        saved = lambda n: [kept[layer, micro][n] for micro in trees]
        side = lambda kind, n: [slots[layer, micro, kind][n] for micro in trees]
        done = lambda kind: (
            lambda: 0.0 if all((layer, micro, kind) in slots for micro in trees) else None
        )
        near = lambda key: (lambda: 0.0 if (key, layer, micro_n - 1) in marks else None)

        def reduce_grad(name, pairs, flip, at):
            if name in offloaded[layer]:
                (total,) = weight_grad(place, pairs, None)
                grads[layer, name] = (
                    lax.psum_scatter(total, both, scatter_dimension=0, tiled=True),
                )
                return
            keep, send = weight_grad(place, pairs, place.at["grads", flip])
            more.append(reduce_links(layer, name, keep, send, flip, at))

        down = lambda: [(side("mlp", 0), saved(10))]
        gate = lambda: [(saved(7), side("mlp", 1))]
        up = lambda: [(saved(7), side("mlp", 2))]
        out = lambda: [(side("out", 0), saved(5))]
        lin = lambda: [(saved(1), side("lin", 0))]
        free = lambda test: (
            lambda: 0.0 if test() is not None and busy["core"] == 0 else None
        )
        at = yield "weight_grad", done("mlp"), 5
        reduce_grad("down", down(), True, at)
        if layer > 0:
            at = yield "weight_grad", free(lambda: 0.0), 5
            reduce_grad("up", up(), True, at)
            at = yield "weight_grad", free(near("kv")), 3
            reduce_grad("gate", gate(), False, at)
            at = yield "weight_grad_small", free(done("lin")), 4
        else:
            at = yield "weight_grad_two", 0.0, 5
            reduce_grad("in", gate() + up(), False, at)
            at = yield "weight_grad_small", done("lin"), 0
        reduce_grad("attn", out() + lin(), True, at)

    def cross_sums():
        keys = [(layer, "attn") for layer in range(layer_n)]
        at = yield "kv_pick", (lambda: 0.0 if all(key in grads for key in keys) else None), 0.5
        parts = [grads[key][0] for key in keys]
        dims = (layer_n * shard, 2 * hd)
        total, low = call(
            functools.partial(kv_pick_kernel, 2 * q_cols),
            "kv_pick",
            (shape(dims, f32), shape(dims, bf16)),
            [LOAD] * len(parts),
            tuple(parts),
        )
        got = swap(low, "tensor", 1)
        at = yield "kv_add", order.link("core", "kv", at) + 2.0, 0.5
        total, low = call(
            kv_add_kernel, "kv_add", (shape(dims, f32), shape(dims, bf16)), [VMEM, VMEM],
            (total, got),
        )
        got = swap(low, "tensor", 2)
        yield "kv_place", order.link("core", "kv", at) + 3.0, 0.5
        out = shape((layer_n, shard, kv_heads * hd), f32)
        finished["kv"] = call(
            functools.partial(kv_place_kernel, place.at["quarter"]),
            "kv_place", (out, out), [SMEM, VMEM, VMEM], (place.table, total, got),
        )

    def small_sums():
        keys = [(layer, micro, "small") for layer in range(layer_n) for micro in range(micro_n)]
        at = yield "small", (lambda: 0.0 if all(key in slots for key in keys) else None), 0.5
        parts = [slots[key][n] for n in range(3) for key in keys]
        total = call(
            functools.partial(small_kernel, place, layer_n, micro_n, hd),
            "small",
            shape((4 * layer_n, width), f32),
            [SMEM] + [LOAD] * len(parts),
            (place.table, *parts),
        )
        for axis, bit in fabric(False)[::-1] + [("tensor", 1), ("tensor", 2)]:
            got = swap(total, axis, bit)
            at = yield "add", order.link("hop", "small", at), 0.5
            total = call(add_kernel, "add", shape(total.shape, f32), [VMEM, VMEM], (total, got))
        grads["small"] = total

    def arrivals():
        names = [("project", 0, micro) for micro in range(micro_n)]
        yield "pack", (lambda: 0.0 if all(name in marks for name in names) else None), 0
        again, far = far_in()
        down = whole(wide(w_down_t))
        at = order.now
        yield "touch", at + 46.0, 0
        arrays, gate, up = corners_in(again, far)
        settled[0] = (attn0, Mixed(arrays, gate, up, shard), Weight(down, shard, False))
        half = len(arrays) // 2
        arrive[0, "mlp"] = at + 75.0
        yield "touch", at + 58.0, 1
        touch(arrays[half : half + 3])
        yield "touch", at + 73.0, 1
        touch(arrays[half + 3 :])
        yield "pack", (lambda: 0.0 if ("mlp", 0, 0) in marks else None), 1.5
        attn, wide_all = second_layer()
        settled[1] = (
            Weight(attn, shard, False),
            Weight(wide_all, 3 * shard, False),
            Weight(wide_all, 3 * shard, False, 2 * shard),
        )

    more = []
    order.run([tree(micro) for micro in range(micro_n)] + [fillers(1), fillers(0), small_sums(), arrivals(), finishes(), cross_sums()], more)
    hidden_out = jnp.stack(finals)
    input_grad = jnp.stack(tails).astype(f32)

    names = ("gate", "up", "down", "lin", "out")
    gate_g, up_g, down_g, query_g, out_g = (finished[name] for name in names)
    key_g, value_g = finished["kv"]
    total = grads["small"]
    block = place.leaf_i * place.seq_n + place.seq_i
    gains = lax.dynamic_slice(total, (0, block * shard), (2 * layer_n, shard))
    cut = lambda a: lax.dynamic_slice_in_dim(a, block * bias_cols, bias_cols, a.ndim - 1)
    bq = total[2 * layer_n : 3 * layer_n].reshape(layer_n, tensor_n, heads, hd)
    bq = cut(lax.dynamic_index_in_dim(bq, place.tensor_i, 1, keepdims=False))
    kv_row = total[3 * layer_n :]
    bk = cut(kv_row[:, : 2 * hd].reshape(layer_n, 2, hd))
    bv = cut(kv_row[:, 2 * hd : 4 * hd].reshape(layer_n, 2, hd))
    return (
        hidden_out,
        input_grad,
        gains[:layer_n],
        query_g,
        bq,
        key_g,
        bk,
        value_g,
        bv,
        jnp.swapaxes(out_g, 1, 2),
        gains[layer_n:],
        gate_g,
        up_g,
        jnp.swapaxes(down_g, 1, 2),
    )


def solution(mesh):
    both = ("leaf", "seq")
    return jax.shard_map(
        body,
        mesh=mesh,
        in_specs=(
            P("leaf", "seq", None),
            P("leaf", None),
            P("leaf", "seq", None),
            P(None, both),
            P(None, both, "tensor"),
            P(None, "tensor", both),
            P(None, both, None),
            P(None, None, both),
            P(None, both, None),
            P(None, None, both),
            P(None, "tensor", both),
            P(None, both),
            P(None, both, "tensor"),
            P(None, both, "tensor"),
            P(None, "tensor", both),
        ),
        out_specs=(
            P("leaf", "seq", None),
            P("leaf", "seq", None),
            P(None, both),
            P(None, both, "tensor"),
            P(None, "tensor", both),
            P(None, both, None),
            P(None, None, both),
            P(None, both, None),
            P(None, None, both),
            P(None, "tensor", both),
            P(None, both),
            P(None, both, "tensor"),
            P(None, both, "tensor"),
            P(None, "tensor", both),
        ),
        check_vma=False,
    )
```
